32 devices in a mesh: dp: 16 (over z, x, core), tensor: 2 (over y).
Axes of the slice: x: 2, y: 2, z: 4, core: 2. Of those that a mesh axis runs over, the one named last changes fastest.
Arguments:
- inputs: bfloat16 [12288, 768], P('dp'), may hold values from -6 to 6
- clip_ids: int32 [12288], replicated, may hold values from 0 to 11, never falling along the last dimension, each value on 1 to 1500 neighbouring positions
- attn_gain: bfloat16 [768], replicated, may hold values from 0.5 to 1.5
- attn_shift: bfloat16 [768], replicated, may hold values from -1.75 to 1.75
- w_query: bfloat16 [768, 768], P(None, 'tensor'), may hold values from -0.21875 to 0.21875
- query_bias: bfloat16 [768], P('tensor'), may hold values from -1.75 to 1.75
- w_key: bfloat16 [768, 768], P(None, 'tensor'), may hold values from -0.21875 to 0.21875
- w_value: bfloat16 [768, 768], P(None, 'tensor'), may hold values from -0.21875 to 0.21875
- value_bias: bfloat16 [768], P('tensor'), may hold values from -3 to 3
- w_out: bfloat16 [768, 768], P('tensor'), may hold values from -4 to 4
- out_bias: bfloat16 [768], replicated, may hold values from -1.75 to 1.75
- mlp_gain: bfloat16 [768], replicated, may hold values from 0.5 to 1.5
- mlp_shift: bfloat16 [768], replicated, may hold values from -1.75 to 1.75
- w_fc1: bfloat16 [768, 3072], P(None, 'tensor'), may hold values from -0.21875 to 0.21875
- fc1_bias: bfloat16 [3072], P('tensor'), may hold values from -3 to 3
- w_fc2: bfloat16 [3072, 768], P('tensor'), may hold values from -0.109375 to 0.109375
- fc2_bias: bfloat16 [768], replicated, may hold values from -1.75 to 1.75
- cotangent: bfloat16 [12288, 768], P('dp'), may hold values from -6 to 6
Outputs:
- layer_out: bfloat16 [12288, 768], P('dp')
- inputs_grad: float32 [12288, 768], P('dp')
- attn_gain_grad: float32 [768], replicated
- attn_shift_grad: float32 [768], replicated
- w_query_grad: float32 [768, 768], P(None, 'tensor')
- query_bias_grad: float32 [768], P('tensor')
- w_key_grad: float32 [768, 768], P(None, 'tensor')
- w_value_grad: float32 [768, 768], P(None, 'tensor')
- value_bias_grad: float32 [768], P('tensor')
- w_out_grad: float32 [768, 768], P('tensor')
- out_bias_grad: float32 [768], replicated
- mlp_gain_grad: float32 [768], replicated
- mlp_shift_grad: float32 [768], replicated
- w_fc1_grad: float32 [768, 3072], P(None, 'tensor')
- fc1_bias_grad: float32 [3072], P('tensor')
- w_fc2_grad: float32 [3072, 768], P('tensor')
- fc2_bias_grad: float32 [768], replicated
The draws below stay inside these ranges and needn't reach their ends.
Inputs may be any that keep to these rules, and one draw needn't show every extreme that they name: `clip_ids`: clip numbers never fall along the tokens; each of the 12 clips holds 1 to 1500 consecutive tokens, and one holds exactly 1500.
All inputs are finite; a program needn't handle non-finite values.
Results may differ from the reference program's by a relative error of at most 0.012.
Values may be sent and summed in bfloat16 or wider, within the bound.
A program may use at most 128 MiB of HBM per device.

```python
import math
import jax
import jax.numpy as jnp
import numpy as np
from jax import lax

D = 768
HEADS = 12
HEAD_DIM = 64
FF = 3072
TOK_DEV = 768
MOST = 1500
REACH = 2
TOKENS = 12288
CLIPS = 12
N_DP = 16


def shard_levels(key, shape, cuts, smallest, high):
    level = 1.0
    for position, parts in cuts:
        steps = jax.random.uniform(jax.random.fold_in(jax.random.fold_in(key, 6), position), (parts,), jnp.float32, smallest / len(cuts), high / len(cuts))
        level = level * jnp.repeat(jnp.exp(steps), shape[position] // parts).reshape((-1,) + (1,) * (len(shape) - 1 - position))
    return level


def profile(count, total, limit, lean):
    portions = [(1 << 20) // math.isqrt(standing ** lean) + 1 for standing in range(2, count + 1)]
    rest, counts = total - limit - (count - 1), [1] * (count - 1)
    while rest > 0:
        free = [i for i in range(count - 1) if counts[i] < limit]
        whole, budget = sum([portions[i] for i in free]), rest
        for i in free:
            extra = min(limit - counts[i], max(1, budget * portions[i] // whole), rest)
            counts[i] = counts[i] + extra
            rest = rest - extra
    return np.array([limit] + counts)


def uneven_parts(key, number_of, total, limit, slope):
    if number_of == 2:
        one = jax.random.randint(key, (), max(1, total - limit), min(limit, total - 1) + 1)
        return jnp.stack([one, total - one])
    lengths = jnp.asarray(profile(number_of, total, limit, slope), jnp.int32)
    twos = (number_of - 1) // 2
    donor, sink = lengths[1:1 + 2 * twos:2], lengths[2:2 + 2 * twos:2]
    room = jnp.minimum(donor - 1, limit - sink)
    moved = jax.random.randint(jax.random.fold_in(key, 1), (twos,), 0, 1 << 20) % (room + 1)
    lengths = lengths.at[1:1 + 2 * twos:2].set(donor - moved).at[2:2 + 2 * twos:2].set(sink + moved)
    return lengths[jax.random.permutation(jax.random.fold_in(key, 2), number_of)]


def gaussian(own_key, dims, deviation, limit, cuts=(), held_as=jnp.bfloat16):
    entries = jax.random.normal(own_key, dims, jnp.float32) * deviation
    if len(cuts) > 0:
        entries = shard_levels(own_key, dims, cuts, -0.22, 0.18) * entries
    return jnp.clip(entries, min=-limit, max=limit).astype(held_as)


def setup_inputs(seed: int = 0) -> dict:
    streams_of = jax.random.split(jax.random.key(seed), 19)
    return {
        "inputs": gaussian(streams_of[0], (TOKENS, D), 1.0, 6.0, ((0, 16),)),
        "clip_ids": jnp.searchsorted(jnp.cumsum(uneven_parts(streams_of[1], CLIPS, TOKENS, MOST, 1)), jnp.arange(TOKENS), side="right").astype(jnp.int32),
        "attn_gain": jnp.clip(1.0 + 0.1 * jax.random.normal(streams_of[2], (D,), jnp.float32), 0.5, 1.5).astype(jnp.bfloat16),
        "attn_shift": gaussian(streams_of[3], (D,), 0.3, 1.75),
        "w_query": gaussian(streams_of[4], (D, D), D ** -0.5, 0.21875, ((1, 2),)),
        "query_bias": gaussian(streams_of[5], (D,), 0.3, 1.75, ((0, 2),)),
        "w_key": gaussian(streams_of[6], (D, D), D ** -0.5, 0.21875, ((1, 2),)),
        "w_value": gaussian(streams_of[7], (D, D), D ** -0.5, 0.21875, ((1, 2),)),
        "value_bias": gaussian(streams_of[8], (D,), 0.5, 3.0, ((0, 2),)),
        "w_out": gaussian(streams_of[9], (D, D), (max(1, D * 4 // MOST)) ** -0.5, 4.0, ((0, 2),)),
        "out_bias": gaussian(streams_of[10], (D,), 0.3, 1.75),
        "mlp_gain": jnp.clip(1.0 + 0.1 * jax.random.normal(streams_of[11], (D,), jnp.float32), 0.5, 1.5).astype(jnp.bfloat16),
        "mlp_shift": gaussian(streams_of[12], (D,), 0.3, 1.75),
        "w_fc1": gaussian(streams_of[13], (D, FF), D ** -0.5, 0.21875, ((1, 2),)),
        "fc1_bias": gaussian(streams_of[14], (FF,), 0.5, 3.0, ((0, 2),)),
        "w_fc2": gaussian(streams_of[15], (FF, D), FF ** -0.5, 0.109375, ((0, 2),)),
        "fc2_bias": gaussian(streams_of[16], (D,), 0.3, 1.75),
        "cotangent": gaussian(streams_of[17], (TOKENS, D), 1.0, 6.0, ((0, 16),)),
    }


@jax.custom_vjp
def low(v):
    return lax.optimization_barrier(v.astype(jnp.bfloat16)).astype(jnp.float32)

@jax.custom_vjp
def low_back(v):
    return v

def low_keep(v):
    return (low(v), None)

def low_pass(kept, grad):
    return (grad,)

def back_keep(v):
    return (v, None)

def back_low(kept, grad):
    return (low(grad),)
low.defvjp(low_keep, low_pass)
low_back.defvjp(back_keep, back_low)

def layer_norm(values, gain_row, bias_row):
    middle = lax.optimization_barrier(jnp.mean(values, axis=-1, keepdims=True))
    centred = values - middle
    spread = lax.optimization_barrier(jnp.mean(centred * centred, axis=-1, keepdims=True))
    return centred * lax.rsqrt(spread + 1e-05) * gain_row + bias_row

def attention(queries, keys, values, clip_ids):
    margin = REACH * TOK_DEV
    breadth = (2 * REACH + 1) * TOK_DEV
    highest = lax.Precision.HIGHEST
    factor = HEAD_DIM ** (-0.5)
    padded_keys = jnp.pad(keys, ((margin, margin), (0, 0)))
    padded_values = jnp.pad(values, ((margin, margin), (0, 0)))
    padded_labels = jnp.pad(clip_ids, (margin, margin), constant_values=-1)
    query_blocks = queries.reshape(N_DP, TOK_DEV, HEADS, HEAD_DIM)
    starts = jnp.arange(N_DP, dtype=jnp.int32) * TOK_DEV

    def one_block(operands):
        query_block, begin_at = operands
        begin_at = begin_at.astype(jnp.int32)
        key_block = lax.dynamic_slice_in_dim(padded_keys, begin_at, breadth, 0).reshape(breadth, HEADS, HEAD_DIM)
        value_block = lax.dynamic_slice_in_dim(padded_values, begin_at, breadth, 0).reshape(breadth, HEADS, HEAD_DIM)
        key_labels = lax.dynamic_slice_in_dim(padded_labels, begin_at, breadth, 0)
        own_labels = lax.dynamic_slice_in_dim(clip_ids, begin_at, TOK_DEV, 0)
        allowed = own_labels[:, None] == key_labels[None, :]
        scores = low_back(jnp.einsum('qhd,khd->hqk', query_block, key_block, precision=highest) * factor)
        scores = jnp.where(allowed[None], scores, -1e+30)
        largest = lax.optimization_barrier(jnp.max(scores, axis=-1, keepdims=True))
        expset = jnp.exp(scores - largest)
        probs = low(expset / lax.optimization_barrier(jnp.sum(expset, axis=-1, keepdims=True)))
        mixed = jnp.einsum('hqk,khd->qhd', probs, value_block, precision=highest)
        return mixed.reshape(TOK_DEV, HEADS * HEAD_DIM)
    mixed_all = lax.map(jax.checkpoint(one_block), (query_blocks, starts))
    return mixed_all.reshape(N_DP * TOK_DEV, HEADS * HEAD_DIM)

def forward(source, clip_ids, params):
    attn_gain, attn_shift, w_query, query_bias, w_key, w_value, value_bias, w_out, out_bias, mlp_gain, mlp_shift, w_fc1, fc1_bias, w_fc2, fc2_bias = params
    highest = lax.Precision.HIGHEST
    attn_input = low(layer_norm(source, attn_gain, attn_shift))
    queries = low_back(low(jnp.dot(attn_input, w_query, precision=highest) + query_bias))
    keys = low_back(low(jnp.dot(attn_input, w_key, precision=highest)))
    values = low_back(low(jnp.dot(attn_input, w_value, precision=highest) + value_bias))
    mixed = low_back(low(attention(queries, keys, values, clip_ids)))
    attn_total = low_back(jnp.dot(mixed, w_out, precision=highest) + out_bias)
    residual = source + attn_total
    mlp_input = low(layer_norm(residual, mlp_gain, mlp_shift))
    preact = low_back(jnp.dot(mlp_input, w_fc1, precision=highest) + fc1_bias)
    activated = low(jax.nn.gelu(preact, approximate=False))
    return residual + jnp.dot(activated, w_fc2, precision=highest) + fc2_bias

def reference(inputs, clip_ids, attn_gain, attn_shift, w_query, query_bias, w_key, w_value, value_bias, w_out, out_bias, mlp_gain, mlp_shift, w_fc1, fc1_bias, w_fc2, fc2_bias, cotangent):
    params = tuple((item.astype(jnp.float32) for item in (attn_gain, attn_shift, w_query, query_bias, w_key, w_value, value_bias, w_out, out_bias, mlp_gain, mlp_shift, w_fc1, fc1_bias, w_fc2, fc2_bias)))

    def apply(source, weights):
        return forward(source, clip_ids, weights)
    result, back = jax.vjp(apply, inputs.astype(jnp.float32), params)
    source_grad, grads = back(cotangent.astype(jnp.float32))
    return (result.astype(jnp.bfloat16), source_grad, grads[0], grads[1], grads[2], grads[3], grads[4], grads[5], grads[6], grads[7], grads[8], grads[9], grads[10], grads[11], grads[12], grads[13], grads[14])
```

```python
import functools

import jax
import jax.numpy as jnp
from jax import lax
from jax.experimental import pallas as pl
from jax.experimental.pallas import tpu as pltpu
from jax.sharding import PartitionSpec as P

HEAD_DIM = 64
REACH = 2
TILE = 256
PIECES = 3
NEG = -1e30
BF = jnp.bfloat16
F32 = jnp.float32
MESH = pl.DeviceIdType.MESH
VMEM = pltpu.VMEM
VMEM_BYTES = 66_000_000
DMA = pltpu.SemaphoreType.DMA


def dot_nn(left, right):
    return jnp.dot(left, right, preferred_element_type=F32)


def dot_tn(left, right):
    return lax.dot_general(left, right, (((0,), (0,)), ((), ())), preferred_element_type=F32)


def dot_nt(left, right):
    return lax.dot_general(left, right, (((1,), (1,)), ((), ())), preferred_element_type=F32)


def whole():
    return pl.BlockSpec(memory_space=VMEM)


def remote(src, dst, send_sem, recv_sem, device):
    return pltpu.make_async_remote_copy(
        src_ref=src,
        dst_ref=dst,
        send_sem=send_sem,
        recv_sem=recv_sem,
        device_id=device,
        device_id_type=MESH,
    )


def place():
    d = lax.axis_index("dp")
    chip = d // 2
    core = d - 2 * chip
    has_left = chip > 0
    has_right = chip < lax.axis_size("dp") // 2 - 1
    return d, core, has_left, has_right


def greet(targets):
    barrier = pltpu.get_barrier_semaphore()
    count = 0
    for present, device in targets:
        if present is None:
            pl.semaphore_signal(barrier, inc=1, device_id=device, device_id_type=MESH)
            count = count + 1
        else:

            @pl.when(present)
            def _():
                pl.semaphore_signal(barrier, inc=1, device_id=device, device_id_type=MESH)

            count = count + present.astype(jnp.int32)
    pl.semaphore_wait(barrier, count)


def norm_rows(values):
    middle = jnp.mean(values, axis=-1, keepdims=True)
    centred = values - middle
    spread = jnp.mean(centred * centred, axis=-1, keepdims=True)
    return centred * lax.rsqrt(spread + 1e-05)


def halo_kernel(
    x_ref, wo_ref, gain_ref, shift_ref, wq_ref, wk_ref, wv_ref, qb_ref, vb_ref,
    q_ref, k_ref, v_ref, a_ref, wof_ref,
    win, sx, rx, sy, ry, ss, rs, sf, rf, sw, rw, sv, rv,
):
    d, core, has_left, has_right = place()
    t = lax.axis_index("tensor")
    height = x_ref.shape[0]
    half = height // 2
    piece = half // PIECES
    sibling = {"dp": d + 1 - 2 * core}
    across = {"tensor": 1 - t}
    exists = (has_left, has_right)
    slots = (0, 2 * REACH)
    greet([(None, sibling), (None, across), (has_left, {"dp": d - 2}), (has_right, {"dp": d + 2})])

    def rows(which, p):
        return pl.ds(pl.multiple_of(which * half + p * piece, piece), piece)

    def x_copy(side, p):
        return remote(
            x_ref.at[rows(t, p)], win.at[slots[side], rows(t, p)], sx.at[side, p], rx.at[side, p],
            {"dp": d + 2 if side == 0 else d - 2},
        )

    def y_copy(side, p):
        spot = win.at[slots[side], rows(t, p)]
        return remote(spot, spot, sy.at[side, p], ry.at[side, p], across)

    def f_copy(which, p):
        span = rows(t if which == 0 else 1 - t, p)
        return remote(
            win.at[4 - 4 * core, span], win.at[3 - 2 * core, span], sf.at[which, p], rf.at[which, p],
            sibling,
        )

    own_copy = remote(x_ref, win.at[1 + 2 * core], ss, rs, sibling)
    part = wo_ref.shape[0] // 2
    wo_rows = pl.ds(pl.multiple_of(core * part, part), part)

    def full_rows(which):
        return pl.ds(pl.multiple_of((2 * which + core) * part, part), part)

    w_copy = remote(wo_ref.at[wo_rows], wof_ref.at[full_rows(t)], sw, rw, across)
    wf_copy = remote(wof_ref.at[full_rows(1 - t)], wof_ref.at[full_rows(1 - t)], sv, rv, sibling)

    for p in range(PIECES):
        for side in (0, 1):

            @pl.when(exists[1 - side])
            def _():
                x_copy(side, p).start()

    own_copy.start()
    gain, shift = gain_ref[...].astype(F32), shift_ref[...].astype(F32)
    query_bias, value_bias = qb_ref[...].astype(F32), vb_ref[...].astype(F32)

    def project(values, slot, start, keep=False):
        attn = (norm_rows(values.astype(F32)) * gain + shift).astype(BF)
        out = pl.ds(pl.multiple_of(slot * height + start, 128), half)
        if keep:
            a_ref[pl.ds(pl.multiple_of(start, half), half), :] = attn
        q_ref[out, :] = ((dot_nn(attn, wq_ref[...]) + query_bias) * HEAD_DIM**-0.5).astype(BF)
        k_ref[out, :] = dot_nn(attn, wk_ref[...]).astype(BF)
        v_ref[out, :] = (dot_nn(attn, wv_ref[...]) + value_bias).astype(BF)

    def project_half(slot, which):
        start = which * half
        project(win[slot, pl.ds(pl.multiple_of(start, half), half), :], slot, start)

    def project_block(slot):
        def step(i, carry):
            project_half(slot, i)
            return carry

        lax.fori_loop(0, 2, step, 0)

    def own_step(i, carry):
        project(x_ref[pl.ds(pl.multiple_of(i * half, half), half), :], REACH, i * half, True)
        return carry

    def pass_on(p):
        for side in (0, 1):

            @pl.when(exists[side])
            def _():
                x_copy(side, p).wait_recv()
                y_copy(side, p).start()

            @pl.when(jnp.logical_and(exists[side], core == 1 - side))
            def _():
                f_copy(0, p).start()

    lax.fori_loop(0, 2, own_step, 0)
    wof_ref[pl.ds(pl.multiple_of(t * 2 * part, part), 2 * part), :] = wo_ref[...]
    pass_on(0)
    own_copy.wait_recv()
    project_block(3 - 2 * core)
    for p in range(1, PIECES):
        pass_on(p)
    w_copy.start()
    for side in (0, 1):

        @pl.when(exists[side])
        def _():
            project_half(slots[side], t)

    for p in range(PIECES):
        for side in (0, 1):

            @pl.when(exists[side])
            def _():
                y_copy(side, p).wait_recv()

            @pl.when(jnp.logical_and(exists[side], core == 1 - side))
            def _():
                f_copy(1, p).start()

    w_copy.wait_recv()
    wf_copy.start()
    for side in (0, 1):

        @pl.when(exists[side])
        def _():
            project_half(slots[side], 1 - t)

        @pl.when(jnp.logical_and(exists[side], core == side))
        def _():
            for which in (0, 1):
                for p in range(PIECES):
                    f_copy(which, p).wait_recv()
            project_block(1 + 2 * core)

    wf_copy.wait_recv()
    for copy in (own_copy, w_copy, wf_copy):
        copy.wait_send()
    for p in range(PIECES):
        for side in (0, 1):

            @pl.when(exists[1 - side])
            def _():
                x_copy(side, p).wait_send()

            @pl.when(exists[side])
            def _():
                y_copy(side, p).wait_send()

            @pl.when(jnp.logical_and(exists[side], core == 1 - side))
            def _():
                f_copy(0, p).wait_send()
                f_copy(1, p).wait_send()


def halo_qkv(x, wo, gain, shift, wq, wk, wv, qb, vb):
    height, width = x.shape
    cols = wq.shape[1]
    blocks = 2 * REACH + 1
    wide = jax.ShapeDtypeStruct((blocks * height, cols), BF)
    pair = DMA((2, PIECES))
    return pl.pallas_call(
        halo_kernel,
        out_shape=(
            wide, wide, wide,
            jax.ShapeDtypeStruct((height, width), BF),
            jax.ShapeDtypeStruct((2 * wo.shape[0], wo.shape[1]), BF),
        ),
        in_specs=[whole()] * 9,
        out_specs=[whole()] * 5,
        scratch_shapes=[pltpu.VMEM((blocks, height, width), BF)]
        + [pair, pair, pair, pair, DMA, DMA, pair, pair, DMA, DMA, DMA, DMA],
        compiler_params=pltpu.CompilerParams(
            collective_id=0, has_side_effects=True, vmem_limit_bytes=VMEM_BYTES
        ),
        name="halo_qkv",
    )(x, wo, gain, shift, wq, wk, wv, qb, vb)


def back_halo_kernel(x_ref, st_ref, xw_ref, sw_ref, sx, rx, ss, rs, sf, rf):
    d, core, has_left, has_right = place()
    height = x_ref.shape[0]
    piece = height // PIECES
    sibling = {"dp": d + 1 - 2 * core}
    exists = (has_left, has_right)
    slots = (0, 2 * REACH)
    greet([(None, sibling), (has_left, {"dp": d - 2}), (has_right, {"dp": d + 2})])

    def refs(p):
        if p == PIECES:
            return st_ref, lambda slot: sw_ref.at[slot]
        span = pl.ds(p * piece, piece)
        return x_ref.at[span], lambda slot: xw_ref.at[slot, span]

    def x_copy(side, p):
        src, dst = refs(p)
        return remote(
            src, dst(slots[side]), sx.at[side, p], rx.at[side, p],
            {"dp": d + 2 if side == 0 else d - 2},
        )

    def s_copy(p):
        src, dst = refs(p)
        return remote(src, dst(1 + 2 * core), ss.at[p], rs.at[p], sibling)

    def f_copy(p):
        _, dst = refs(p)
        return remote(dst(4 - 4 * core), dst(3 - 2 * core), sf.at[p], rf.at[p], sibling)

    order = (PIECES,) + tuple(range(PIECES))
    for p in order:
        for side in (0, 1):

            @pl.when(exists[1 - side])
            def _():
                x_copy(side, p).start()

    for p in order:
        s_copy(p).start()
    xw_ref[REACH] = x_ref[...]
    sw_ref[REACH] = st_ref[...]
    for p in order:
        for side in (0, 1):

            @pl.when(exists[side])
            def _():
                x_copy(side, p).wait_recv()

            @pl.when(jnp.logical_and(exists[side], core == 1 - side))
            def _():
                f_copy(p).start()

    for p in order:
        s_copy(p).wait()
        for side in (0, 1):

            @pl.when(exists[1 - side])
            def _():
                x_copy(side, p).wait_send()

            @pl.when(jnp.logical_and(exists[side], core == 1 - side))
            def _():
                f_copy(p).wait_send()

            @pl.when(jnp.logical_and(exists[side], core == side))
            def _():
                f_copy(p).wait_recv()


def back_halo(x, stats):
    blocks = 2 * REACH + 1
    pair, line = DMA((2, PIECES + 1)), DMA((PIECES + 1,))
    return pl.pallas_call(
        back_halo_kernel,
        out_shape=(
            jax.ShapeDtypeStruct((blocks,) + x.shape, x.dtype),
            jax.ShapeDtypeStruct((blocks,) + stats.shape, stats.dtype),
        ),
        in_specs=[whole()] * 2,
        out_specs=[whole()] * 2,
        scratch_shapes=[pair, pair, line, line, line, line],
        compiler_params=pltpu.CompilerParams(
            collective_id=1, has_side_effects=True, vmem_limit_bytes=VMEM_BYTES
        ),
        name="back_halo",
    )(x, stats)


def only(values, lower, keep_low):
    return jnp.where(lower if keep_low else jnp.logical_not(lower), values, jnp.zeros_like(values))


def low_lanes(shape):
    return lax.broadcasted_iota(jnp.int32, shape, 1) < HEAD_DIM


def key_tile(j):
    return pl.ds(pl.multiple_of(j * TILE, TILE), TILE)


def attend_kernel(b_ref, q_ref, k_ref, v_ref, own_ref, win_ref, o_ref, lse_ref, row_ref, s_ref, m_ref, l_ref, acc_ref):
    i = pl.program_id(1)
    lo, hi = b_ref[0, i], b_ref[1, i]
    lower = low_lanes((TILE, 128))
    query = q_ref[...]
    queries = (only(query, lower, True), only(query, lower, False))
    own = own_ref[...]
    m_ref[...] = jnp.full(m_ref.shape, NEG, F32)
    l_ref[...] = jnp.zeros(l_ref.shape, F32)
    acc_ref[...] = jnp.zeros(acc_ref.shape, F32)

    def score(j, carry):
        keys = k_ref[key_tile(j), :]
        same = own == win_ref[j]
        for h in (0, 1):
            s = jnp.where(same, dot_nt(queries[h], keys), NEG)
            s_ref[h, j - lo] = s
            m_ref[h] = jnp.maximum(m_ref[h], jnp.maximum(s[:, :128], s[:, 128:]))
        return carry

    lax.fori_loop(lo, hi, score, 0)
    tops = [jnp.max(m_ref[h], axis=1, keepdims=True) for h in (0, 1)]

    def weigh(j, carry):
        values = v_ref[key_tile(j), :]
        for h in (0, 1):
            e = jnp.exp(s_ref[h, j - lo] - tops[h])
            l_ref[h] += e[:, :128] + e[:, 128:]
            acc_ref[h] += dot_nn(e.astype(BF), values)
        return carry

    lax.fori_loop(lo, hi, weigh, 0)
    totals = [jnp.sum(l_ref[h], axis=1, keepdims=True) for h in (0, 1)]
    o_ref[...] = jnp.where(lower, acc_ref[0] / totals[0], acc_ref[1] / totals[1]).astype(BF)
    logs = jnp.where(lower, tops[0] + jnp.log(totals[0]), tops[1] + jnp.log(totals[1]))
    lse_ref[0] = logs
    turned = jnp.transpose(logs)
    row_ref[0, 0:8, :] = turned[0:8]
    row_ref[0, 8:16, :] = turned[HEAD_DIM : HEAD_DIM + 8]


def attend(bounds, q, k, v, own, win):
    window, cols = k.shape
    tiles = own.shape[0] // TILE
    pairs = cols // 128
    first = REACH * tiles
    most = 2 * REACH * tiles + tiles
    grid = pltpu.PrefetchScalarGridSpec(
        num_scalar_prefetch=1,
        grid=(pairs, tiles),
        in_specs=[
            pl.BlockSpec((TILE, 128), lambda p, i, b: (first + i, p)),
            pl.BlockSpec((window, 128), lambda p, i, b: (0, p)),
            pl.BlockSpec((window, 128), lambda p, i, b: (0, p)),
            pl.BlockSpec((TILE, 1), lambda p, i, b: (i, 0)),
            pl.BlockSpec(win.shape, lambda p, i, b: (0, 0, 0)),
        ],
        out_specs=[
            pl.BlockSpec((TILE, 128), lambda p, i, b: (i, p)),
            pl.BlockSpec((1, TILE, 128), lambda p, i, b: (p, i, 0)),
            pl.BlockSpec((1, 16, TILE), lambda p, i, b: (p, 0, i)),
        ],
        scratch_shapes=[
            pltpu.VMEM((2, most, TILE, TILE), F32),
            pltpu.VMEM((2, TILE, 128), F32),
            pltpu.VMEM((2, TILE, 128), F32),
            pltpu.VMEM((2, TILE, 128), F32),
        ],
    )
    return pl.pallas_call(
        attend_kernel,
        grid_spec=grid,
        out_shape=(
            jax.ShapeDtypeStruct((tiles * TILE, cols), BF),
            jax.ShapeDtypeStruct((pairs, tiles * TILE, 128), F32),
            jax.ShapeDtypeStruct((pairs, 16, tiles * TILE), F32),
        ),
        compiler_params=pltpu.CompilerParams(vmem_limit_bytes=VMEM_BYTES),
        name="attend",
    )(bounds, q, k, v, own, win)


def query_back_kernel(b_ref, q_ref, k_ref, v_ref, o_ref, g_ref, lse_ref, own_ref, win_ref, dq_ref, acc_ref):
    i = pl.program_id(1)
    lo, hi = b_ref[0, i], b_ref[1, i]
    lower = low_lanes((TILE, 128))
    query, grad = q_ref[...], g_ref[...]
    queries = (only(query, lower, True), only(query, lower, False))
    grads = (only(grad, lower, True), only(grad, lower, False))
    product = grad.astype(F32) * o_ref[...].astype(F32)
    centres = [jnp.sum(only(product, lower, h == 0), axis=1, keepdims=True) for h in (0, 1)]
    logs = [lse_ref[0, :, 0:1], lse_ref[0, :, HEAD_DIM : HEAD_DIM + 1]]
    own = own_ref[...]
    acc_ref[...] = jnp.zeros(acc_ref.shape, F32)

    def step(j, carry):
        keys, values = k_ref[key_tile(j), :], v_ref[key_tile(j), :]
        same = own == win_ref[j]
        for h in (0, 1):
            s = jnp.where(same, dot_nt(queries[h], keys), NEG)
            probs = jnp.exp(s - logs[h])
            d_score = probs * (dot_nt(grads[h], values) - centres[h])
            acc_ref[h] += dot_nn(d_score.astype(BF), keys)
        return carry

    lax.fori_loop(lo, hi, step, 0)
    dq_ref[...] = (jnp.where(lower, acc_ref[0], acc_ref[1]) * HEAD_DIM**-0.5).astype(BF)


def query_back(bounds, q, k, v, o, g, lse, own, win):
    window, cols = k.shape
    tiles = own.shape[0] // TILE
    pairs = cols // 128
    first = REACH * tiles
    tile = pl.BlockSpec((TILE, 128), lambda p, i, b: (i, p))
    grid = pltpu.PrefetchScalarGridSpec(
        num_scalar_prefetch=1,
        grid=(pairs, tiles),
        in_specs=[
            pl.BlockSpec((TILE, 128), lambda p, i, b: (first + i, p)),
            pl.BlockSpec((window, 128), lambda p, i, b: (0, p)),
            pl.BlockSpec((window, 128), lambda p, i, b: (0, p)),
            tile,
            tile,
            pl.BlockSpec((1, TILE, 128), lambda p, i, b: (p, i, 0)),
            pl.BlockSpec((TILE, 1), lambda p, i, b: (i, 0)),
            pl.BlockSpec(win.shape, lambda p, i, b: (0, 0, 0)),
        ],
        out_specs=tile,
        scratch_shapes=[pltpu.VMEM((2, TILE, 128), F32)],
    )
    return pl.pallas_call(
        query_back_kernel,
        grid_spec=grid,
        out_shape=jax.ShapeDtypeStruct((tiles * TILE, cols), BF),
        compiler_params=pltpu.CompilerParams(vmem_limit_bytes=VMEM_BYTES),
        name="query_back",
    )(bounds, q, k, v, o, g, lse, own, win)


def key_back_kernel(b_ref, q_ref, k_ref, v_ref, g_ref, st_ref, own_ref, win_ref, dk_ref, dv_ref, acck_ref, accv_ref):
    p, i = pl.program_id(0), pl.program_id(1)
    lo, hi = b_ref[0, i], b_ref[1, i]
    lower = low_lanes((TILE, 128))
    key, value = k_ref[...], v_ref[...]
    keys = (only(key, lower, True), only(key, lower, False))
    values = (only(value, lower, True), only(value, lower, False))
    own = own_ref[...]
    acck_ref[...] = jnp.zeros(acck_ref.shape, F32)
    accv_ref[...] = jnp.zeros(accv_ref.shape, F32)

    def step(j, carry):
        queries, grads = q_ref[key_tile(j), :], g_ref[key_tile(j), :]
        same = own == win_ref[j]
        for h in (0, 1):
            logs = st_ref[j, pl.ds(2 * p + h, 1), :]
            centres = st_ref[j, pl.ds(8 + 2 * p + h, 1), :]
            s = jnp.where(same, dot_nt(keys[h], queries), NEG)
            probs = jnp.exp(s - logs)
            d_score = probs * (dot_nt(values[h], grads) - centres)
            accv_ref[h] += dot_nn(probs.astype(BF), grads)
            acck_ref[h] += dot_nn(d_score.astype(BF), queries)
        return carry

    lax.fori_loop(lo, hi, step, 0)
    dk_ref[...] = jnp.where(lower, acck_ref[0], acck_ref[1]).astype(BF)
    dv_ref[...] = jnp.where(lower, accv_ref[0], accv_ref[1]).astype(BF)


def key_back(bounds, q, k, v, g, stats, own, win):
    window, cols = k.shape
    tiles = own.shape[0] // TILE
    pairs = cols // 128
    first = REACH * tiles
    tile = pl.BlockSpec((TILE, 128), lambda p, i, b: (i, p))
    centre = pl.BlockSpec((TILE, 128), lambda p, i, b: (first + i, p))
    strip = pl.BlockSpec((window, 128), lambda p, i, b: (0, p))
    grid = pltpu.PrefetchScalarGridSpec(
        num_scalar_prefetch=1,
        grid=(pairs, tiles),
        in_specs=[
            strip,
            centre,
            centre,
            strip,
            pl.BlockSpec(stats.shape, lambda p, i, b: (0, 0, 0)),
            pl.BlockSpec((TILE, 1), lambda p, i, b: (i, 0)),
            pl.BlockSpec(win.shape, lambda p, i, b: (0, 0, 0)),
        ],
        out_specs=[tile, tile],
        scratch_shapes=[pltpu.VMEM((2, TILE, 128), F32), pltpu.VMEM((2, TILE, 128), F32)],
    )
    return pl.pallas_call(
        key_back_kernel,
        grid_spec=grid,
        out_shape=(jax.ShapeDtypeStruct((tiles * TILE, cols), BF),) * 2,
        compiler_params=pltpu.CompilerParams(vmem_limit_bytes=VMEM_BYTES),
        name="key_back",
    )(bounds, q, k, v, g, stats, own, win)


def ring_kernel(arrays, *refs):
    given = refs[:arrays]
    outs = refs[arrays : 2 * arrays]
    sibs = refs[2 * arrays : 3 * arrays]
    bufs = refs[3 * arrays : 4 * arrays]
    ss, rs, sr, rr, sg, rg, sc, rc = refs[4 * arrays :]
    d = lax.axis_index("dp")
    n = lax.axis_size("dp") // 2
    chip = d // 2
    core = d - 2 * chip
    sibling = {"dp": d + 1 - 2 * core}
    odd = chip - 2 * (chip // 2)
    spot = (1 - odd) * (chip // 2) + odd * (n - 1 - chip // 2)
    here = (1 - core) * spot + core * (n - 1 - spot)

    def wrap(index):
        return lax.rem(index + 2 * n, n)

    def device_at(rank):
        walk = (1 - core) * rank + core * (n - 1 - rank)
        late = walk // (n // 2)
        return 2 * ((1 - late) * (2 * walk) + late * (2 * (n - walk) - 1)) + core

    after = {"dp": device_at(wrap(here + 1))}
    before = {"dp": device_at(wrap(here - 1))}
    greet([(None, sibling), (None, after), (None, before)])

    def spans(a, owner, j):
        rows, cols = given[a].shape[0] // 2, given[a].shape[1]
        count = cols // bufs[a].shape[2]
        high, wide = bufs[a].shape[1], bufs[a].shape[2]
        line = j // count
        row = pl.multiple_of(owner * rows + line * high, high)
        col = pl.multiple_of((j - line * count) * wide, wide)
        return pl.ds(row, high), pl.ds(col, wide)

    def s_copy(a):
        rows = given[a].shape[0] // 2
        span = pl.ds(pl.multiple_of((1 - core) * rows, rows), rows)
        return remote(given[a].at[span], sibs[a], ss.at[a], rs.at[a], sibling)

    def r_copy(a, s):
        return remote(bufs[a].at[s], bufs[a].at[s + 1], sr.at[a, s], rr.at[a, s], after)

    def g_copy(a, s):
        spot = outs[a].at[spans(a, core, wrap(here + 1 - s))]
        return remote(spot, spot, sg.at[a, s], rg.at[a, s], after)

    def c_copy(a, s):
        spot = outs[a].at[spans(a, core, wrap(here + 1 - s))]
        return remote(spot, spot, sc.at[a, s], rc.at[a, s], sibling)

    def terms(a, j):
        mine = given[a][spans(a, core, j)].astype(F32)
        return mine + sibs[a][spans(a, 0, j)].astype(F32)

    for a in range(arrays):
        s_copy(a).start()
    for a in range(arrays):
        s_copy(a).wait_recv()
        bufs[a][0] = terms(a, here).astype(bufs[a].dtype)
        r_copy(a, 0).start()

    def reduce_step(s, carry):
        for a in range(arrays):
            j = wrap(here - s)
            local = terms(a, j)
            r_copy(a, s - 1).wait_recv()
            bufs[a][s] = (bufs[a][s].astype(F32) + local).astype(bufs[a].dtype)
            r_copy(a, s).start()
        return carry

    lax.fori_loop(1, n - 1, reduce_step, 0)
    for a in range(arrays):
        j = wrap(here + 1)
        local = terms(a, j)
        r_copy(a, n - 2).wait_recv()
        done = (bufs[a][n - 1].astype(F32) + local).astype(bufs[a].dtype)
        outs[a][spans(a, core, j)] = done
        g_copy(a, 0).start()
        c_copy(a, 0).start()

    def gather_step(s, carry):
        for a in range(arrays):
            g_copy(a, s - 1).wait_recv()
            g_copy(a, s).start()
            c_copy(a, s).start()
        return carry

    lax.fori_loop(1, n - 1, gather_step, 0)
    for a in range(arrays):
        g_copy(a, n - 2).wait_recv()
        c_copy(a, n - 1).start()
    for a in range(arrays):
        s_copy(a).wait_send()
        c_copy(a, n - 1).wait()

    def settle(s, carry):
        for a in range(arrays):
            r_copy(a, s).wait_send()
            g_copy(a, s).wait_send()
            c_copy(a, s).wait()
        return carry

    lax.fori_loop(0, n - 1, settle, 0)


def ring_sum(values, ident):
    n = lax.axis_size("dp") // 2
    count = len(values)
    sibs, bufs = [], []
    for value in values:
        rows, cols = value.shape
        wide = min(cols, 384)
        sibs.append(pltpu.VMEM((rows // 2, cols), value.dtype))
        bufs.append(pltpu.VMEM((n, rows * cols // (2 * n * wide), wide), value.dtype))
    return pl.pallas_call(
        functools.partial(ring_kernel, count),
        out_shape=tuple(jax.ShapeDtypeStruct(v.shape, v.dtype) for v in values),
        in_specs=[whole()] * count,
        out_specs=[whole()] * count,
        scratch_shapes=sibs
        + bufs
        + [DMA((count,)), DMA((count,))]
        + [DMA((count, n - 1))] * 4
        + [DMA((count, n))] * 2,
        compiler_params=pltpu.CompilerParams(
            collective_id=ident, has_side_effects=True, vmem_limit_bytes=VMEM_BYTES
        ),
        name="ring_sum",
    )(*values)


def swapped(value):
    return lax.ppermute(value, "tensor", [(0, 1), (1, 0)])


def norm_back(grad, source, gain):
    middle = jnp.mean(source, axis=-1, keepdims=True)
    centred = source - middle
    inverse = lax.rsqrt(jnp.mean(centred * centred, axis=-1, keepdims=True) + 1e-05)
    n = centred * inverse
    t = grad * gain
    back = (t - jnp.mean(t, axis=-1, keepdims=True) - n * jnp.mean(t * n, axis=-1, keepdims=True)) * inverse
    return back, jnp.sum(grad * n, axis=0), jnp.sum(grad, axis=0)


def on_device(
    inputs, clip_ids, attn_gain, attn_shift, w_query, query_bias, w_key, w_value, value_bias,
    w_out, out_bias, mlp_gain, mlp_shift, w_fc1, fc1_bias, w_fc2, fc2_bias, cotangent,
):
    height, width = inputs.shape
    tiles = height // TILE
    d = lax.axis_index("dp")
    t = lax.axis_index("tensor")
    reach = REACH * height
    heads = w_query.shape[1] // HEAD_DIM

    padded = jnp.pad(clip_ids, (reach, reach), constant_values=-1)
    window = lax.dynamic_slice_in_dim(padded, d * height, height + 2 * reach)
    own = lax.dynamic_slice_in_dim(clip_ids, d * height, height)
    firsts, lasts = own[::TILE], own[TILE - 1 :: TILE]
    origin = d * height - reach
    begin = jnp.sum((clip_ids[None, :] < firsts[:, None]).astype(jnp.int32), axis=1) - origin
    end = jnp.sum((clip_ids[None, :] <= lasts[:, None]).astype(jnp.int32), axis=1) - origin
    bounds = jnp.stack([begin // TILE, (end + TILE - 1) // TILE])
    own = own[:, None]
    window = window.reshape(-1, 1, TILE)

    row = lambda v: v[None, :]
    q, k, v, attn_input, w_out_full = halo_qkv(
        inputs, w_out, row(attn_gain), row(attn_shift), w_query, w_key, w_value,
        row(query_bias), row(value_bias),
    )
    mixed, lse, lse_rows = attend(bounds, q, k, v, own, window)
    other = swapped(mixed)
    flip = t == 0
    w_mine = w_out
    w_other = lax.dynamic_slice_in_dim(w_out_full, (1 - t) * w_out.shape[0], w_out.shape[0])
    source = inputs.astype(F32)
    residual = source + dot_nn(mixed, w_mine) + dot_nn(other, w_other) + out_bias.astype(F32)
    mlp_input = (norm_rows(residual) * mlp_gain.astype(F32) + mlp_shift.astype(F32)).astype(BF)
    preact = dot_nn(mlp_input, w_fc1) + fc1_bias.astype(F32)
    cdf = 0.5 * (1.0 + lax.erf(preact * (2.0**-0.5)))
    pdf = jnp.exp(-0.5 * preact * preact) * 0.3989422804014327
    activated = (preact * cdf).astype(BF)
    slope = cdf + preact * pdf
    pre_grad = (dot_nt(cotangent, w_fc2) * slope).astype(BF)
    part = dot_nt(pre_grad, w_fc1).astype(BF)
    mlp_in_grad = part.astype(F32) + swapped(part).astype(F32)
    out_part = dot_nn(activated, w_fc2).astype(BF)
    layer_out = (
        residual + (out_part.astype(F32) + swapped(out_part).astype(F32)) + fc2_bias.astype(F32)
    ).astype(BF)
    cot = cotangent.astype(F32)
    resid_back, mlp_gain_grad, mlp_shift_grad = norm_back(mlp_in_grad, residual, mlp_gain.astype(F32))
    residual_grad = cot + resid_back
    attn_grad_low = residual_grad.astype(BF)
    mixed_grad = dot_nt(attn_grad_low, w_out).astype(BF)

    fc1_grad = dot_tn(mlp_input, pre_grad).astype(BF)
    fc2_grad = dot_tn(activated, cotangent).astype(BF)
    out_grad = dot_tn(attn_grad_low, mixed).astype(BF)
    fc2_bias_grad = jnp.sum(cot, axis=0)
    fc1_bias_grad = jnp.sum(pre_grad.astype(F32), axis=0)
    out_bias_grad = jnp.sum(attn_grad_low.astype(F32), axis=0)

    product = (mixed_grad.astype(F32) * mixed.astype(F32)).reshape(height, heads, HEAD_DIM)
    centres = jnp.sum(product, axis=2).T
    logs = jnp.stack([lse_rows[h // 2, 8 * (h % 2)] for h in range(heads)])
    gap = jnp.zeros((8 - heads, height), F32)
    stats = jnp.concatenate([logs, gap, centres, gap])
    grad_win, stat_win = back_halo(mixed_grad, stats)
    grad_win = grad_win.reshape(-1, grad_win.shape[2])
    stat_win = stat_win.reshape(-1, 16, tiles, TILE).transpose(0, 2, 1, 3).reshape(-1, 16, TILE)
    query_low = query_back(bounds, q, k, v, mixed, mixed_grad, lse, own, window)
    key_low, value_low = key_back(bounds, q, k, v, grad_win, stat_win, own, window)

    attn_part = (
        dot_nt(query_low, w_query) + dot_nt(key_low, w_key) + dot_nt(value_low, w_value)
    ).astype(BF)
    attn_in_grad = attn_part.astype(F32) + swapped(attn_part).astype(F32)
    source_back, attn_gain_grad, attn_shift_grad = norm_back(attn_in_grad, source, attn_gain.astype(F32))
    inputs_grad = residual_grad + source_back
    query_bias_grad = jnp.sum(query_low.astype(F32), axis=0)
    value_bias_grad = jnp.sum(value_low.astype(F32), axis=0)
    attn_weights = jnp.concatenate(
        [
            dot_tn(attn_input, query_low).astype(BF),
            dot_tn(attn_input, key_low).astype(BF),
            dot_tn(attn_input, value_low).astype(BF),
            out_grad,
        ],
        axis=1,
    )
    vectors = [
        query_bias_grad, value_bias_grad, out_bias_grad, attn_gain_grad, attn_shift_grad,
        fc1_bias_grad, fc2_bias_grad, mlp_gain_grad, mlp_shift_grad,
    ]
    sizes = [vector.shape[0] for vector in vectors]
    room = lax.axis_size("dp") * 1024
    packed = jnp.pad(jnp.concatenate(vectors), (0, room - sum(sizes))).reshape(-1, 128)
    attn_sum, fc1_sum, fc2_sum, packed_sum = ring_sum([attn_weights, fc1_grad, fc2_grad, packed], 2)
    flat = packed_sum.reshape(-1)
    sums, start = [], 0
    for size in sizes:
        sums.append(flat[start : start + size])
        start += size
    (
        query_bias_grad, value_bias_grad, out_bias_grad, attn_gain_grad, attn_shift_grad,
        fc1_bias_grad, fc2_bias_grad, mlp_gain_grad, mlp_shift_grad,
    ) = sums
    cols = w_query.shape[1]
    pieces = [attn_sum[:, i * cols : (i + 1) * cols].astype(F32) for i in range(4)]
    return (
        layer_out, inputs_grad, attn_gain_grad, attn_shift_grad,
        pieces[0], query_bias_grad, pieces[1], pieces[2], value_bias_grad,
        pieces[3].T, out_bias_grad, mlp_gain_grad, mlp_shift_grad,
        fc1_sum.astype(F32), fc1_bias_grad, fc2_sum.astype(F32), fc2_bias_grad,
    )


def solution(mesh):
    rows, cols, split, every = P("dp", None), P(None, "tensor"), P("tensor"), P()
    tall = P("tensor", None)
    in_specs = (
        rows, every, every, every, cols, split, cols, cols, split, tall, every, every, every,
        cols, split, tall, every, rows,
    )
    out_specs = (
        rows, rows, every, every, cols, split, cols, cols, split, tall, every, every, every,
        cols, split, tall, every,
    )
    return jax.shard_map(on_device, mesh=mesh, in_specs=in_specs, out_specs=out_specs, check_vma=False)
```

```python
import functools

import jax
import jax.numpy as jnp
from jax import lax
from jax.experimental import pallas as pl
from jax.experimental.pallas import tpu as pltpu
from jax.sharding import PartitionSpec as P

HEAD_DIM = 64
REACH = 2
TILE = 256
PIECES = 6
AHEAD = 2
NEG = -3e38
CLIPS = 64
LOGS = 64
CENTRES = 96
FAR = -(2.0**100)
SAFE = 40.0
BF = jnp.bfloat16
F32 = jnp.float32
MESH = pl.DeviceIdType.MESH
VMEM = pltpu.VMEM
VMEM_BYTES = 26_000_000
DMA = pltpu.SemaphoreType.DMA


def dot_nn(left, right):
    return jnp.dot(left, right, preferred_element_type=F32)


def dot_tn(left, right):
    return lax.dot_general(left, right, (((0,), (0,)), ((), ())), preferred_element_type=F32)


def dot_nt(left, right):
    return lax.dot_general(left, right, (((1,), (1,)), ((), ())), preferred_element_type=F32)


def whole():
    return pl.BlockSpec(memory_space=VMEM)


def remote(src, dst, send_sem, recv_sem, device):
    return pltpu.make_async_remote_copy(
        src_ref=src,
        dst_ref=dst,
        send_sem=send_sem,
        recv_sem=recv_sem,
        device_id=device,
        device_id_type=MESH,
    )


def place():
    d = lax.axis_index("dp")
    chip = d // 2
    core = d - 2 * chip
    has_left = chip > 0
    has_right = chip < lax.axis_size("dp") // 2 - 1
    return d, core, has_left, has_right


def greet(targets):
    barrier = pltpu.get_barrier_semaphore()
    count = 0
    for present, device in targets:
        if present is None:
            pl.semaphore_signal(barrier, inc=1, device_id=device, device_id_type=MESH)
            count = count + 1
        else:

            @pl.when(present)
            def _():
                pl.semaphore_signal(barrier, inc=1, device_id=device, device_id_type=MESH)

            count = count + present.astype(jnp.int32)
    pl.semaphore_wait(barrier, count)


def norm_rows(values):
    middle = jnp.mean(values, axis=-1, keepdims=True)
    centred = values - middle
    spread = jnp.mean(centred * centred, axis=-1, keepdims=True)
    return centred * lax.rsqrt(spread + 1e-05)


def halo_kernel(
    x_ref, wo_ref, gain_ref, shift_ref, wq_ref, wk_ref, wv_ref, qb_ref, vb_ref,
    q_ref, k_ref, v_ref, a_ref, wof_ref, n_ref,
    win, sx, rx, sy, ry, ss, rs, sf, rf, sw, rw, sv, rv,
):
    d, core, has_left, has_right = place()
    t = lax.axis_index("tensor")
    height = x_ref.shape[0]
    half = height // 2
    piece = half // PIECES
    sibling = {"dp": d + 1 - 2 * core}
    across = {"tensor": 1 - t}
    exists = (has_left, has_right)
    slots = (0, 2 * REACH)
    greet([(None, sibling), (None, across), (has_left, {"dp": d - 2}), (has_right, {"dp": d + 2})])

    def rows(which, p):
        return pl.ds(pl.multiple_of(which * half + p * piece, piece), piece)

    def x_copy(side, p):
        return remote(
            x_ref.at[rows(t, p)], win.at[slots[side], rows(t, p)], sx.at[side, p], rx.at[side, p],
            {"dp": d + 2 if side == 0 else d - 2},
        )

    def y_copy(side, p):
        spot = win.at[slots[side], rows(t, p)]
        return remote(spot, spot, sy.at[side, p], ry.at[side, p], across)

    def f_copy(which, p):
        span = rows(t if which == 0 else 1 - t, p)
        return remote(
            win.at[4 - 4 * core, span], win.at[3 - 2 * core, span], sf.at[which, p], rf.at[which, p],
            sibling,
        )

    own_copy = remote(x_ref, win.at[1 + 2 * core], ss, rs, sibling)
    part = wo_ref.shape[0] // 2
    wo_rows = pl.ds(pl.multiple_of(core * part, part), part)

    def full_rows(which):
        return pl.ds(pl.multiple_of((2 * which + core) * part, part), part)

    w_copy = remote(wo_ref.at[wo_rows], wof_ref.at[full_rows(t)], sw, rw, across)
    wf_copy = remote(wof_ref.at[full_rows(1 - t)], wof_ref.at[full_rows(1 - t)], sv, rv, sibling)

    def send(p):
        for side in (0, 1):

            @pl.when(exists[1 - side])
            def _():
                x_copy(side, p).start()

    for p in range(AHEAD):
        send(p)
    w_copy.start()
    own_copy.start()
    gain, shift = gain_ref[...].astype(F32), shift_ref[...].astype(F32)
    query_bias, value_bias = qb_ref[...].astype(F32), vb_ref[...].astype(F32)

    n_ref[...] = jnp.zeros(n_ref.shape, F32)

    def raise_norm(spot, values):
        for c in range(values.shape[1] // 128):
            part = values[:, c * 128 : c * 128 + 128]
            norm = jnp.max(jnp.sum(part * part, axis=1, keepdims=True), axis=0, keepdims=True)
            n_ref[spot, :] = jnp.maximum(n_ref[spot, :], norm)

    def project(values, slot, start, keep=False):
        attn = (norm_rows(values.astype(F32)) * gain + shift).astype(BF)
        out = pl.ds(pl.multiple_of(slot * height + start, 128), half)
        if keep:
            a_ref[pl.ds(pl.multiple_of(start, half), half), :] = attn
        query = (dot_nn(attn, wq_ref[...]) + query_bias) * HEAD_DIM**-0.5
        key = dot_nn(attn, wk_ref[...])
        q_ref[out, :] = query.astype(BF)
        k_ref[out, :] = key.astype(BF)
        raise_norm(slice(0, 8), query)
        raise_norm(slice(8, 16), key)
        v_ref[out, :] = (dot_nn(attn, wv_ref[...]) + value_bias).astype(BF)

    def project_half(slot, which):
        start = which * half
        project(win[slot, pl.ds(pl.multiple_of(start, half), half), :], slot, start)

    def project_block(slot):
        def step(i, carry):
            project_half(slot, i)
            return carry

        lax.fori_loop(0, 2, step, 0)

    def own_step(i, carry):
        project(x_ref[pl.ds(pl.multiple_of(i * half, half), half), :], REACH, i * half, True)
        return carry

    def pass_on(p):
        for side in (0, 1):

            @pl.when(exists[side])
            def _():
                x_copy(side, p).wait_recv()
                y_copy(side, p).start()

            @pl.when(jnp.logical_and(exists[side], core == 1 - side))
            def _():
                f_copy(0, p).start()

        if p + AHEAD < PIECES:
            send(p + AHEAD)

    lax.fori_loop(0, 2, own_step, 0)
    wof_ref[pl.ds(pl.multiple_of(t * 2 * part, part), 2 * part), :] = wo_ref[...]
    pass_on(0)
    w_copy.wait_recv()
    wf_copy.start()
    for p in range(1, PIECES // 2):
        pass_on(p)
    own_copy.wait_recv()
    project_block(3 - 2 * core)
    for p in range(PIECES // 2, PIECES):
        pass_on(p)
    for side in (0, 1):

        @pl.when(exists[side])
        def _():
            project_half(slots[side], t)

    for p in range(PIECES):
        for side in (0, 1):

            @pl.when(exists[side])
            def _():
                y_copy(side, p).wait_recv()

            @pl.when(jnp.logical_and(exists[side], core == 1 - side))
            def _():
                f_copy(1, p).start()

    for side in (0, 1):

        @pl.when(exists[side])
        def _():
            project_half(slots[side], 1 - t)

        @pl.when(jnp.logical_and(exists[side], core == side))
        def _():
            for which in (0, 1):
                for p in range(PIECES):
                    f_copy(which, p).wait_recv()
            project_block(1 + 2 * core)

    wf_copy.wait_recv()
    for copy in (own_copy, w_copy, wf_copy):
        copy.wait_send()
    for p in range(PIECES):
        for side in (0, 1):

            @pl.when(exists[1 - side])
            def _():
                x_copy(side, p).wait_send()

            @pl.when(exists[side])
            def _():
                y_copy(side, p).wait_send()

            @pl.when(jnp.logical_and(exists[side], core == 1 - side))
            def _():
                f_copy(0, p).wait_send()
                f_copy(1, p).wait_send()


def halo_qkv(x, wo, gain, shift, wq, wk, wv, qb, vb):
    height, width = x.shape
    cols = wq.shape[1]
    blocks = 2 * REACH + 1
    wide = jax.ShapeDtypeStruct((blocks * height, cols), BF)
    pair = DMA((2, PIECES))
    return pl.pallas_call(
        halo_kernel,
        out_shape=(
            wide, wide, wide,
            jax.ShapeDtypeStruct((height, width), BF),
            jax.ShapeDtypeStruct((2 * wo.shape[0], wo.shape[1]), BF),
            jax.ShapeDtypeStruct((16, 128), F32),
        ),
        in_specs=[whole()] * 9,
        out_specs=[whole()] * 6,
        scratch_shapes=[pltpu.VMEM((blocks, height, width), BF)]
        + [pair, pair, pair, pair, DMA, DMA, pair, pair, DMA, DMA, DMA, DMA],
        compiler_params=pltpu.CompilerParams(
            collective_id=0, has_side_effects=True, vmem_limit_bytes=VMEM_BYTES
        ),
        name="halo_qkv",
    )(x, wo, gain, shift, wq, wk, wv, qb, vb)


def split3(values):
    first = values.astype(BF).astype(F32)
    second = (values - first).astype(BF).astype(F32)
    return first, second, values - first - second


def code_tile(rows, keys_code):
    count = rows.shape[1]
    terms = split3(-rows)
    lane = lax.broadcasted_iota(jnp.int32, (128, count), 0)
    tall = jnp.zeros((128, count), F32)
    for h in range(8):
        for base, row in ((LOGS, h), (CENTRES, 8 + h)):
            for i in range(3):
                tall = jnp.where(lane == base + 3 * h + i, terms[i][row : row + 1], tall)
    wide = jnp.transpose(tall)
    column = lax.broadcasted_iota(jnp.int32, wide.shape, 1)
    same = jnp.logical_and(column < CLIPS, keys_code.astype(F32) == 0.0)
    return jnp.where(same, 1.0, wide).astype(BF)


def back_halo_kernel(x_ref, o_ref, lse_ref, kc_ref, xw_ref, qc_ref, st_ref, sw_ref, sx, rx, ss, rs, sf, rf):
    d, core, has_left, has_right = place()
    height, cols = x_ref.shape
    piece = height // PIECES
    sibling = {"dp": d + 1 - 2 * core}
    exists = (has_left, has_right)
    slots = (0, 2 * REACH)
    greet([(None, sibling), (has_left, {"dp": d - 2}), (has_right, {"dp": d + 2})])

    def refs(p):
        if p == PIECES:
            return st_ref, lambda slot: sw_ref.at[slot]
        span = pl.ds(p * piece, piece)
        return x_ref.at[span], lambda slot: xw_ref.at[slot, span]

    def x_copy(side, p):
        src, dst = refs(p)
        return remote(
            src, dst(slots[side]), sx.at[side, p], rx.at[side, p],
            {"dp": d + 2 if side == 0 else d - 2},
        )

    def s_copy(p):
        src, dst = refs(p)
        return remote(src, dst(1 + 2 * core), ss.at[p], rs.at[p], sibling)

    def f_copy(p):
        _, dst = refs(p)
        return remote(dst(4 - 4 * core), dst(3 - 2 * core), sf.at[p], rf.at[p], sibling)

    order = tuple(range(PIECES)) + (PIECES,)

    def send(p):
        for side in (0, 1):

            @pl.when(exists[1 - side])
            def _():
                x_copy(side, p).start()

        s_copy(p).start()

    for p in range(PIECES):
        send(p)
    picks = lax.broadcasted_iota(jnp.int32, (8, cols), 1) // HEAD_DIM
    picks = (picks == lax.broadcasted_iota(jnp.int32, (8, cols), 0)).astype(F32)
    product = x_ref[...].astype(F32) * o_ref[...].astype(F32)
    st_ref[0:8, :] = lse_ref[...]
    st_ref[8:16, :] = lax.dot_general(
        picks, product, (((1,), (1,)), ((), ())),
        precision=lax.Precision.HIGHEST, preferred_element_type=F32,
    )
    send(PIECES)
    xw_ref[REACH] = x_ref[...]
    sw_ref[REACH] = st_ref[...]

    def code(slot):
        def step(i, carry):
            rows = pl.ds(pl.multiple_of(slot * height + i * TILE, TILE), TILE)
            stats = sw_ref[slot, :, pl.ds(pl.multiple_of(i * TILE, TILE), TILE)]
            qc_ref[rows, :] = code_tile(stats, kc_ref[rows, :])
            return carry

        lax.fori_loop(0, height // TILE, step, 0)

    code(REACH)
    for p in order:
        for side in (0, 1):

            @pl.when(exists[side])
            def _():
                x_copy(side, p).wait_recv()

            @pl.when(jnp.logical_and(exists[side], core == 1 - side))
            def _():
                f_copy(p).start()

    for p in order:
        s_copy(p).wait()
        for side in (0, 1):

            @pl.when(exists[1 - side])
            def _():
                x_copy(side, p).wait_send()

            @pl.when(jnp.logical_and(exists[side], core == 1 - side))
            def _():
                f_copy(p).wait_send()

            @pl.when(jnp.logical_and(exists[side], core == side))
            def _():
                f_copy(p).wait_recv()

    code(3 - 2 * core)
    for side in (0, 1):

        @pl.when(exists[side])
        def _():
            code(slots[side])

        @pl.when(jnp.logical_and(exists[side], core == side))
        def _():
            code(1 + 2 * core)


def back_halo(x, o, lse, kc):
    blocks = 2 * REACH + 1
    height = x.shape[0]
    pair, line = DMA((2, PIECES + 1)), DMA((PIECES + 1,))
    return pl.pallas_call(
        back_halo_kernel,
        out_shape=(
            jax.ShapeDtypeStruct((blocks,) + x.shape, x.dtype),
            jax.ShapeDtypeStruct(kc.shape, BF),
        ),
        in_specs=[whole()] * 4,
        out_specs=[whole()] * 2,
        scratch_shapes=[
            pltpu.VMEM((16, height), F32), pltpu.VMEM((blocks, 16, height), F32),
            pair, pair, line, line, line, line,
        ],
        compiler_params=pltpu.CompilerParams(
            collective_id=1, has_side_effects=True, vmem_limit_bytes=VMEM_BYTES
        ),
        name="back_halo",
    )(x, o, lse, kc)


def tile_at(j):
    return pl.ds(pl.multiple_of(j * TILE, TILE), TILE)


def lanes_of(c):
    return pl.ds(c * 128, 128)


def beside(left, right):
    return jnp.concatenate([left, right], axis=1)


def stacked_heads(values, codes):
    lower = lax.broadcasted_iota(jnp.int32, values.shape, 1) < HEAD_DIM
    none = jnp.zeros_like(values)
    return jnp.concatenate(
        [beside(jnp.where(lower, values, none), codes[0]), beside(jnp.where(lower, none, values), codes[1])],
        axis=0,
    )


def heads_out(turned):
    pair = jnp.concatenate([turned[:HEAD_DIM, :TILE], turned[HEAD_DIM:, TILE:]], axis=0)
    return jnp.transpose(pair)


def within(lane, start):
    return jnp.logical_and(lane >= start, lane < start + 3)


def attend_kernel(b_ref, q_ref, k_ref, v_ref, kc_ref, n_ref, o_ref, lse_ref, r_ref, m_ref, l_ref, acc_ref):
    height, cols = o_ref.shape
    pairs, tiles = cols // 128, height // TILE
    steep = jnp.logical_not(jnp.max(n_ref[0:8, :]) * jnp.max(n_ref[8:16, :]) <= SAFE * SAFE)
    lane = lax.broadcasted_iota(jnp.int32, (TILE, 128), 1)

    def groups(values):
        return values.reshape(TILE // 8, 8, values.shape[1])

    def one(i, carry):
        lo, hi = b_ref[0, i], b_ref[1, i]
        own = pl.ds(pl.multiple_of(REACH * height + i * TILE, TILE), TILE)
        same = jnp.logical_and(lane < CLIPS, kc_ref[own, :].astype(F32) == 0.0)
        code = jnp.where(same, 1.0, 0.0).astype(BF)
        for c in range(pairs):
            r_ref[c] = stacked_heads(q_ref[own, lanes_of(c)], (code, code))
        acc_ref[...] = jnp.zeros(acc_ref.shape, F32)
        l_ref[...] = jnp.zeros(l_ref.shape, F32)
        m_ref[...] = jnp.zeros(m_ref.shape, F32)

        def score(j, c):
            return dot_nt(beside(k_ref[tile_at(j), lanes_of(c)], kc_ref[tile_at(j), :]), r_ref[c])

        def step(shift, j, carry):
            raised = []
            for c in range(pairs):
                s = score(j, c)
                e = jnp.exp(s - m_ref[c, 0:1, :] if shift else s)
                l_ref[c] += jnp.sum(groups(e), axis=0)
                raised.append(e.astype(BF))
            for c in range(pairs):
                acc_ref[c] += dot_tn(v_ref[tile_at(j), lanes_of(c)], raised[c])
            return carry

        @pl.when(jnp.logical_not(steep))
        def _():
            lax.fori_loop(lo, hi, functools.partial(step, False), 0)

        @pl.when(steep)
        def _():
            m_ref[...] = jnp.full(m_ref.shape, NEG, F32)

            def peak(j, carry):
                for c in range(pairs):
                    m_ref[c] = jnp.maximum(m_ref[c], jnp.max(groups(score(j, c)), axis=0))
                return carry

            lax.fori_loop(lo, hi, peak, 0)
            for c in range(pairs):
                m_ref[c] = jnp.broadcast_to(jnp.max(m_ref[c], axis=0, keepdims=True), m_ref.shape[1:])
            lax.fori_loop(lo, hi, functools.partial(step, True), 0)

        for c in range(pairs):
            total = jnp.sum(l_ref[c], axis=0, keepdims=True)
            o_ref[tile_at(i), lanes_of(c)] = heads_out(acc_ref[c] / total).astype(BF)
            logs = m_ref[c, 0:1, :] + jnp.log(total)
            lse_ref[2 * c : 2 * c + 1, tile_at(i)] = logs[:, :TILE]
            lse_ref[2 * c + 1 : 2 * c + 2, tile_at(i)] = logs[:, TILE:]
        return carry

    lse_ref[...] = jnp.zeros(lse_ref.shape, F32)
    lax.fori_loop(0, tiles, one, 0)


def local_call(kernel, name, out_shape, scratch, bounds, *values):
    grid = pltpu.PrefetchScalarGridSpec(
        num_scalar_prefetch=1,
        grid=(1,),
        in_specs=[whole()] * len(values),
        out_specs=jax.tree.map(lambda _: whole(), out_shape),
        scratch_shapes=scratch,
    )
    return pl.pallas_call(
        kernel,
        grid_spec=grid,
        out_shape=out_shape,
        compiler_params=pltpu.CompilerParams(vmem_limit_bytes=VMEM_BYTES),
        name=name,
    )(bounds, *values)


def attend(bounds, q, k, v, kc, norms, height):
    cols = k.shape[1]
    pairs = cols // 128
    out_shape = (jax.ShapeDtypeStruct((height, cols), BF), jax.ShapeDtypeStruct((8, height), F32))
    scratch = [
        pltpu.VMEM((pairs, 2 * TILE, 256), BF),
        pltpu.VMEM((pairs, 8, 2 * TILE), F32),
        pltpu.VMEM((pairs, 8, 2 * TILE), F32),
        pltpu.VMEM((pairs, 128, 2 * TILE), F32),
    ]
    return local_call(attend_kernel, "attend", out_shape, scratch, bounds, q, k, v, kc, norms)


def query_back_kernel(b_ref, q_ref, k_ref, v_ref, g_ref, kc_ref, qc_ref, dq_ref, r_ref, t_ref, acc_ref):
    height, cols = dq_ref.shape
    pairs, tiles = cols // 128, height // TILE
    lane = lax.broadcasted_iota(jnp.int32, (TILE, 128), 1)

    def one(i, carry):
        own = pl.ds(pl.multiple_of(REACH * height + i * TILE, TILE), TILE)
        code = qc_ref[own, :]
        none = jnp.zeros_like(code)
        for c in range(pairs):
            logs, centres = [], []
            for h in (2 * c, 2 * c + 1):
                logs.append(jnp.where(jnp.logical_or(lane < CLIPS, within(lane, LOGS + 3 * h)), code, none))
                centres.append(jnp.where(within(lane, CENTRES + 3 * h), code, none))
            r_ref[c] = stacked_heads(q_ref[own, lanes_of(c)], logs)
            t_ref[c] = stacked_heads(g_ref[own, lanes_of(c)], centres)
        acc_ref[...] = jnp.zeros(acc_ref.shape, F32)

        def step(j, carry):
            code = kc_ref[tile_at(j), :]
            steps = []
            for c in range(pairs):
                probs = jnp.exp(dot_nt(beside(k_ref[tile_at(j), lanes_of(c)], code), r_ref[c]))
                d_probs = dot_nt(beside(v_ref[tile_at(j), lanes_of(c)], code), t_ref[c])
                steps.append((probs * d_probs).astype(BF))
            for c in range(pairs):
                acc_ref[c] += dot_tn(k_ref[tile_at(j), lanes_of(c)], steps[c])
            return carry

        lax.fori_loop(b_ref[0, i], b_ref[1, i], step, 0)
        for c in range(pairs):
            dq_ref[tile_at(i), lanes_of(c)] = (heads_out(acc_ref[c]) * HEAD_DIM**-0.5).astype(BF)
        return carry

    lax.fori_loop(0, tiles, one, 0)


def query_back(bounds, q, k, v, g, kc, qc, height):
    cols = k.shape[1]
    pairs = cols // 128
    scratch = [pltpu.VMEM((pairs, 2 * TILE, 256), BF)] * 2 + [pltpu.VMEM((pairs, 128, 2 * TILE), F32)]
    out_shape = jax.ShapeDtypeStruct((height, cols), BF)
    return local_call(query_back_kernel, "query_back", out_shape, scratch, bounds, q, k, v, g, kc, qc)


def key_back_kernel(b_ref, q_ref, k_ref, v_ref, g_ref, kc_ref, qc_ref, dk_ref, dv_ref, r_ref, t_ref, ak_ref, av_ref):
    height, cols = dk_ref.shape
    pairs, tiles = cols // 128, height // TILE
    lane = lax.broadcasted_iota(jnp.int32, (TILE, 128), 1)

    def one(i, carry):
        own = pl.ds(pl.multiple_of(REACH * height + i * TILE, TILE), TILE)
        code = kc_ref[own, :]
        none, ones = jnp.zeros_like(code), jnp.ones_like(code)
        for c in range(pairs):
            logs, centres = [], []
            for h in (2 * c, 2 * c + 1):
                logs.append(jnp.where(lane < CLIPS, code, jnp.where(within(lane, LOGS + 3 * h), ones, none)))
                centres.append(jnp.where(within(lane, CENTRES + 3 * h), ones, none))
            r_ref[c] = stacked_heads(k_ref[own, lanes_of(c)], logs)
            t_ref[c] = stacked_heads(v_ref[own, lanes_of(c)], centres)
        ak_ref[...] = jnp.zeros(ak_ref.shape, F32)
        av_ref[...] = jnp.zeros(av_ref.shape, F32)

        def step(j, carry):
            code = qc_ref[tile_at(j), :]
            weights, steps = [], []
            for c in range(pairs):
                probs = jnp.exp(dot_nt(beside(q_ref[tile_at(j), lanes_of(c)], code), r_ref[c]))
                d_probs = dot_nt(beside(g_ref[tile_at(j), lanes_of(c)], code), t_ref[c])
                weights.append(probs.astype(BF))
                steps.append((probs * d_probs).astype(BF))
            for c in range(pairs):
                av_ref[c] += dot_tn(g_ref[tile_at(j), lanes_of(c)], weights[c])
                ak_ref[c] += dot_tn(q_ref[tile_at(j), lanes_of(c)], steps[c])
            return carry

        lax.fori_loop(b_ref[0, i], b_ref[1, i], step, 0)
        for c in range(pairs):
            dk_ref[tile_at(i), lanes_of(c)] = heads_out(ak_ref[c]).astype(BF)
            dv_ref[tile_at(i), lanes_of(c)] = heads_out(av_ref[c]).astype(BF)
        return carry

    lax.fori_loop(0, tiles, one, 0)


def key_back(bounds, q, k, v, g, kc, qc, height):
    cols = k.shape[1]
    pairs = cols // 128
    scratch = [pltpu.VMEM((pairs, 2 * TILE, 256), BF)] * 2 + [pltpu.VMEM((pairs, 128, 2 * TILE), F32)] * 2
    out_shape = (jax.ShapeDtypeStruct((height, cols), BF),) * 2
    return local_call(key_back_kernel, "key_back", out_shape, scratch, bounds, q, k, v, g, kc, qc)


def ring_kernel(arrays, *refs):
    given = refs[:arrays]
    outs = refs[arrays : 2 * arrays]
    sibs = refs[2 * arrays : 3 * arrays]
    bufs = refs[3 * arrays : 4 * arrays]
    ss, rs, sr, rr, sg, rg, sc, rc = refs[4 * arrays :]
    d = lax.axis_index("dp")
    n = lax.axis_size("dp") // 2
    chip = d // 2
    core = d - 2 * chip
    sibling = {"dp": d + 1 - 2 * core}
    odd = chip - 2 * (chip // 2)
    spot = (1 - odd) * (chip // 2) + odd * (n - 1 - chip // 2)
    here = (1 - core) * spot + core * (n - 1 - spot)

    def wrap(index):
        return lax.rem(index + 2 * n, n)

    def device_at(rank):
        walk = (1 - core) * rank + core * (n - 1 - rank)
        late = walk // (n // 2)
        return 2 * ((1 - late) * (2 * walk) + late * (2 * (n - walk) - 1)) + core

    after = {"dp": device_at(wrap(here + 1))}
    before = {"dp": device_at(wrap(here - 1))}
    greet([(None, sibling), (None, after), (None, before)])

    def spans(a, owner, j):
        rows, cols = given[a].shape[0] // 2, given[a].shape[1]
        count = cols // bufs[a].shape[2]
        high, wide = bufs[a].shape[1], bufs[a].shape[2]
        line = j // count
        row = pl.multiple_of(owner * rows + line * high, high)
        col = pl.multiple_of((j - line * count) * wide, wide)
        return pl.ds(row, high), pl.ds(col, wide)

    def s_copy(a):
        rows = given[a].shape[0] // 2
        span = pl.ds(pl.multiple_of((1 - core) * rows, rows), rows)
        return remote(given[a].at[span], sibs[a], ss.at[a], rs.at[a], sibling)

    def r_copy(a, s):
        return remote(bufs[a].at[s], bufs[a].at[s + 1], sr.at[a, s], rr.at[a, s], after)

    def g_copy(a, s):
        spot = outs[a].at[spans(a, core, wrap(here + 1 - s))]
        return remote(spot, spot, sg.at[a, s], rg.at[a, s], after)

    def c_copy(a, s):
        spot = outs[a].at[spans(a, core, wrap(here + 1 - s))]
        return remote(spot, spot, sc.at[a, s], rc.at[a, s], sibling)

    def terms(a, j):
        mine = given[a][spans(a, core, j)].astype(F32)
        return mine + sibs[a][spans(a, 0, j)].astype(F32)

    for a in range(arrays):
        s_copy(a).start()
    for a in range(arrays):
        s_copy(a).wait_recv()
        bufs[a][0] = terms(a, here).astype(bufs[a].dtype)
        r_copy(a, 0).start()

    def reduce_step(s, carry):
        for a in range(arrays):
            j = wrap(here - s)
            local = terms(a, j)
            r_copy(a, s - 1).wait_recv()
            bufs[a][s] = (bufs[a][s].astype(F32) + local).astype(bufs[a].dtype)
            r_copy(a, s).start()
        return carry

    lax.fori_loop(1, n - 1, reduce_step, 0)
    for a in range(arrays):
        j = wrap(here + 1)
        local = terms(a, j)
        r_copy(a, n - 2).wait_recv()
        done = (bufs[a][n - 1].astype(F32) + local).astype(bufs[a].dtype)
        outs[a][spans(a, core, j)] = done
        g_copy(a, 0).start()
        c_copy(a, 0).start()

    def gather_step(s, carry):
        for a in range(arrays):
            g_copy(a, s - 1).wait_recv()
            g_copy(a, s).start()
            c_copy(a, s).start()
        return carry

    lax.fori_loop(1, n - 1, gather_step, 0)
    for a in range(arrays):
        g_copy(a, n - 2).wait_recv()
        c_copy(a, n - 1).start()
    for a in range(arrays):
        s_copy(a).wait_send()
        c_copy(a, n - 1).wait()

    def settle(s, carry):
        for a in range(arrays):
            r_copy(a, s).wait_send()
            g_copy(a, s).wait_send()
            c_copy(a, s).wait()
        return carry

    lax.fori_loop(0, n - 1, settle, 0)


def ring_sum(values, ident):
    n = lax.axis_size("dp") // 2
    count = len(values)
    sibs, bufs = [], []
    for value in values:
        rows, cols = value.shape
        wide = min(cols, 384)
        sibs.append(pltpu.VMEM((rows // 2, cols), value.dtype))
        bufs.append(pltpu.VMEM((n, rows * cols // (2 * n * wide), wide), value.dtype))
    return pl.pallas_call(
        functools.partial(ring_kernel, count),
        out_shape=tuple(jax.ShapeDtypeStruct(v.shape, v.dtype) for v in values),
        in_specs=[whole()] * count,
        out_specs=[whole()] * count,
        scratch_shapes=sibs
        + bufs
        + [DMA((count,)), DMA((count,))]
        + [DMA((count, n - 1))] * 4
        + [DMA((count, n))] * 2,
        compiler_params=pltpu.CompilerParams(
            collective_id=ident, has_side_effects=True, vmem_limit_bytes=VMEM_BYTES
        ),
        name="ring_sum",
    )(*values)


def swapped(value):
    return lax.ppermute(value, "tensor", [(0, 1), (1, 0)])


def norm_back(grad, source, gain):
    middle = jnp.mean(source, axis=-1, keepdims=True)
    centred = source - middle
    inverse = lax.rsqrt(jnp.mean(centred * centred, axis=-1, keepdims=True) + 1e-05)
    n = centred * inverse
    t = grad * gain
    back = (t - jnp.mean(t, axis=-1, keepdims=True) - n * jnp.mean(t * n, axis=-1, keepdims=True)) * inverse
    return back, jnp.sum(grad * n, axis=0), jnp.sum(grad, axis=0)


def on_device(
    inputs, clip_ids, attn_gain, attn_shift, w_query, query_bias, w_key, w_value, value_bias,
    w_out, out_bias, mlp_gain, mlp_shift, w_fc1, fc1_bias, w_fc2, fc2_bias, cotangent,
):
    height, width = inputs.shape
    d = lax.axis_index("dp")
    t = lax.axis_index("tensor")
    reach = REACH * height

    padded = jnp.pad(clip_ids, (reach, reach), constant_values=-1)
    window = lax.dynamic_slice_in_dim(padded, d * height, height + 2 * reach)
    own = lax.dynamic_slice_in_dim(clip_ids, d * height, height)
    firsts, lasts = own[::TILE], own[TILE - 1 :: TILE]
    origin = d * height - reach
    begin = jnp.sum((clip_ids[None, :] < firsts[:, None]).astype(jnp.int32), axis=1) - origin
    end = jnp.sum((clip_ids[None, :] <= lasts[:, None]).astype(jnp.int32), axis=1) - origin
    bounds = jnp.stack([begin // TILE, (end + TILE - 1) // TILE])
    lane = jnp.arange(128, dtype=jnp.int32)[None, :]
    clip_far = jnp.where(window[:, None] == lane, 0.0, FAR)
    key_code = jnp.where(lane < CLIPS, clip_far, 1.0).astype(BF)

    row = lambda v: v[None, :]
    q, k, v, attn_input, w_out_full, norms = halo_qkv(
        inputs, w_out, row(attn_gain), row(attn_shift), w_query, w_key, w_value,
        row(query_bias), row(value_bias),
    )
    mixed, logs = attend(bounds, q, k, v, key_code, norms, height)
    other = swapped(mixed)
    w_mine = w_out
    w_other = lax.dynamic_slice_in_dim(w_out_full, (1 - t) * w_out.shape[0], w_out.shape[0])
    source = inputs.astype(F32)
    residual = source + dot_nn(mixed, w_mine) + dot_nn(other, w_other) + out_bias.astype(F32)
    mlp_input = (norm_rows(residual) * mlp_gain.astype(F32) + mlp_shift.astype(F32)).astype(BF)
    preact = dot_nn(mlp_input, w_fc1) + fc1_bias.astype(F32)
    cdf = 0.5 * (1.0 + lax.erf(preact * (2.0**-0.5)))
    pdf = jnp.exp(-0.5 * preact * preact) * 0.3989422804014327
    activated = (preact * cdf).astype(BF)
    slope = cdf + preact * pdf
    pre_grad = (dot_nt(cotangent, w_fc2) * slope).astype(BF)
    part = dot_nt(pre_grad, w_fc1).astype(BF)
    mlp_in_grad = part.astype(F32) + swapped(part).astype(F32)
    out_part = dot_nn(activated, w_fc2).astype(BF)
    layer_out = (
        residual + (out_part.astype(F32) + swapped(out_part).astype(F32)) + fc2_bias.astype(F32)
    ).astype(BF)
    cot = cotangent.astype(F32)
    resid_back, mlp_gain_grad, mlp_shift_grad = norm_back(mlp_in_grad, residual, mlp_gain.astype(F32))
    residual_grad = cot + resid_back
    attn_grad_low = residual_grad.astype(BF)
    mixed_grad = dot_nt(attn_grad_low, w_out).astype(BF)

    fc1_grad = dot_tn(mlp_input, pre_grad).astype(BF)
    fc2_grad = dot_tn(activated, cotangent).astype(BF)
    out_grad = dot_tn(attn_grad_low, mixed).astype(BF)
    fc2_bias_grad = jnp.sum(cot, axis=0)
    fc1_bias_grad = jnp.sum(pre_grad.astype(F32), axis=0)
    out_bias_grad = jnp.sum(attn_grad_low.astype(F32), axis=0)

    grad_win, query_code = back_halo(mixed_grad, mixed, logs, key_code)
    grad_win = grad_win.reshape(-1, grad_win.shape[2])
    query_low = query_back(bounds, q, k, v, grad_win, key_code, query_code, height)
    key_low, value_low = key_back(bounds, q, k, v, grad_win, key_code, query_code, height)

    attn_part = (
        dot_nt(query_low, w_query) + dot_nt(key_low, w_key) + dot_nt(value_low, w_value)
    ).astype(BF)
    attn_in_grad = attn_part.astype(F32) + swapped(attn_part).astype(F32)
    source_back, attn_gain_grad, attn_shift_grad = norm_back(attn_in_grad, source, attn_gain.astype(F32))
    inputs_grad = residual_grad + source_back
    query_bias_grad = jnp.sum(query_low.astype(F32), axis=0)
    value_bias_grad = jnp.sum(value_low.astype(F32), axis=0)
    attn_weights = jnp.concatenate(
        [
            dot_tn(attn_input, query_low).astype(BF),
            dot_tn(attn_input, key_low).astype(BF),
            dot_tn(attn_input, value_low).astype(BF),
            out_grad,
        ],
        axis=1,
    )
    vectors = [
        query_bias_grad, value_bias_grad, out_bias_grad, attn_gain_grad, attn_shift_grad,
        fc1_bias_grad, fc2_bias_grad, mlp_gain_grad, mlp_shift_grad,
    ]
    sizes = [vector.shape[0] for vector in vectors]
    room = lax.axis_size("dp") * 1024
    packed = jnp.pad(jnp.concatenate(vectors), (0, room - sum(sizes))).reshape(-1, 128)
    attn_sum, fc1_sum, fc2_sum, packed_sum = ring_sum([attn_weights, fc1_grad, fc2_grad, packed], 2)
    flat = packed_sum.reshape(-1)
    sums, start = [], 0
    for size in sizes:
        sums.append(flat[start : start + size])
        start += size
    (
        query_bias_grad, value_bias_grad, out_bias_grad, attn_gain_grad, attn_shift_grad,
        fc1_bias_grad, fc2_bias_grad, mlp_gain_grad, mlp_shift_grad,
    ) = sums
    cols = w_query.shape[1]
    pieces = [attn_sum[:, i * cols : (i + 1) * cols].astype(F32) for i in range(4)]
    return (
        layer_out, inputs_grad, attn_gain_grad, attn_shift_grad,
        pieces[0], query_bias_grad, pieces[1], pieces[2], value_bias_grad,
        pieces[3].T, out_bias_grad, mlp_gain_grad, mlp_shift_grad,
        fc1_sum.astype(F32), fc1_bias_grad, fc2_sum.astype(F32), fc2_bias_grad,
    )


def solution(mesh):
    rows, cols, split, every = P("dp", None), P(None, "tensor"), P("tensor"), P()
    tall = P("tensor", None)
    in_specs = (
        rows, every, every, every, cols, split, cols, cols, split, tall, every, every, every,
        cols, split, tall, every, rows,
    )
    out_specs = (
        rows, rows, every, every, cols, split, cols, cols, split, tall, every, every, every,
        cols, split, tall, every,
    )
    return jax.shard_map(on_device, mesh=mesh, in_specs=in_specs, out_specs=out_specs, check_vma=False)
```

```python
import functools

import jax
import jax.numpy as jnp
from jax import lax
from jax.experimental import pallas as pl
from jax.experimental.pallas import tpu as pltpu
from jax.sharding import PartitionSpec as P

HEAD_DIM = 64
REACH = 2
TILE = 256
PIECES = 6
AHEAD = 2
NEG = -3e38
CLIPS = 64
LOGS = 64
CENTRES = 96
FAR = -(2.0**100)
SAFE = 40.0
BF = jnp.bfloat16
F32 = jnp.float32
MESH = pl.DeviceIdType.MESH
VMEM = pltpu.VMEM
VMEM_BYTES = 26_000_000
MID_BYTES = 36_000_000
DMA = pltpu.SemaphoreType.DMA


def dot_nn(left, right):
    return jnp.dot(left, right, preferred_element_type=F32)


def dot_tn(left, right):
    return lax.dot_general(left, right, (((0,), (0,)), ((), ())), preferred_element_type=F32)


def dot_nt(left, right):
    return lax.dot_general(left, right, (((1,), (1,)), ((), ())), preferred_element_type=F32)


def whole():
    return pl.BlockSpec(memory_space=VMEM)


def remote(src, dst, send_sem, recv_sem, device):
    return pltpu.make_async_remote_copy(
        src_ref=src,
        dst_ref=dst,
        send_sem=send_sem,
        recv_sem=recv_sem,
        device_id=device,
        device_id_type=MESH,
    )


def place():
    d = lax.axis_index("dp")
    chip = d // 2
    core = d - 2 * chip
    has_left = chip > 0
    has_right = chip < lax.axis_size("dp") // 2 - 1
    return d, core, has_left, has_right


def greet(targets):
    barrier = pltpu.get_barrier_semaphore()
    count = 0
    for present, device in targets:
        if present is None:
            pl.semaphore_signal(barrier, inc=1, device_id=device, device_id_type=MESH)
            count = count + 1
        else:

            @pl.when(present)
            def _():
                pl.semaphore_signal(barrier, inc=1, device_id=device, device_id_type=MESH)

            count = count + present.astype(jnp.int32)
    pl.semaphore_wait(barrier, count)


def norm_rows(values):
    middle = jnp.mean(values, axis=-1, keepdims=True)
    centred = values - middle
    spread = jnp.mean(centred * centred, axis=-1, keepdims=True)
    return centred * lax.rsqrt(spread + 1e-05)


def halo_kernel(
    x_ref, wo_ref, gain_ref, shift_ref, wq_ref, wk_ref, wv_ref, qb_ref, vb_ref,
    q_ref, k_ref, v_ref, a_ref, wof_ref, n_ref,
    win, sx, rx, sy, ry, ss, rs, sf, rf, sw, rw, sv, rv,
):
    d, core, has_left, has_right = place()
    t = lax.axis_index("tensor")
    height = x_ref.shape[0]
    half = height // 2
    piece = half // PIECES
    sibling = {"dp": d + 1 - 2 * core}
    across = {"tensor": 1 - t}
    exists = (has_left, has_right)
    slots = (0, 2 * REACH)
    greet([(None, sibling), (None, across), (has_left, {"dp": d - 2}), (has_right, {"dp": d + 2})])

    def rows(which, p):
        return pl.ds(pl.multiple_of(which * half + p * piece, piece), piece)

    def x_copy(side, p):
        return remote(
            x_ref.at[rows(t, p)], win.at[slots[side], rows(t, p)], sx.at[side, p], rx.at[side, p],
            {"dp": d + 2 if side == 0 else d - 2},
        )

    def y_copy(side, p):
        spot = win.at[slots[side], rows(t, p)]
        return remote(spot, spot, sy.at[side, p], ry.at[side, p], across)

    def f_copy(which, p):
        span = rows(t if which == 0 else 1 - t, p)
        return remote(
            win.at[4 - 4 * core, span], win.at[3 - 2 * core, span], sf.at[which, p], rf.at[which, p],
            sibling,
        )

    own_copy = remote(x_ref, win.at[1 + 2 * core], ss, rs, sibling)
    part = wo_ref.shape[0] // 2
    wo_rows = pl.ds(pl.multiple_of(core * part, part), part)

    def full_rows(which):
        return pl.ds(pl.multiple_of((2 * which + core) * part, part), part)

    w_copy = remote(wo_ref.at[wo_rows], wof_ref.at[full_rows(t)], sw, rw, across)
    wf_copy = remote(wof_ref.at[full_rows(1 - t)], wof_ref.at[full_rows(1 - t)], sv, rv, sibling)

    def send(p):
        for side in (0, 1):

            @pl.when(exists[1 - side])
            def _():
                x_copy(side, p).start()

    for p in range(AHEAD):
        send(p)
    w_copy.start()
    own_copy.start()
    gain, shift = gain_ref[...].astype(F32), shift_ref[...].astype(F32)
    query_bias, value_bias = qb_ref[...].astype(F32), vb_ref[...].astype(F32)

    n_ref[...] = jnp.zeros(n_ref.shape, F32)

    def raise_norm(spot, values):
        for c in range(values.shape[1] // 128):
            part = values[:, c * 128 : c * 128 + 128]
            norm = jnp.max(jnp.sum(part * part, axis=1, keepdims=True), axis=0, keepdims=True)
            n_ref[spot, :] = jnp.maximum(n_ref[spot, :], norm)

    def project(values, slot, start, keep=False):
        attn = (norm_rows(values.astype(F32)) * gain + shift).astype(BF)
        out = pl.ds(pl.multiple_of(slot * height + start, 128), half)
        if keep:
            a_ref[pl.ds(pl.multiple_of(start, half), half), :] = attn
        query = (dot_nn(attn, wq_ref[...]) + query_bias) * HEAD_DIM**-0.5
        key = dot_nn(attn, wk_ref[...])
        q_ref[out, :] = query.astype(BF)
        k_ref[out, :] = key.astype(BF)
        raise_norm(slice(0, 8), query)
        raise_norm(slice(8, 16), key)
        v_ref[out, :] = (dot_nn(attn, wv_ref[...]) + value_bias).astype(BF)

    def project_half(slot, which):
        start = which * half
        project(win[slot, pl.ds(pl.multiple_of(start, half), half), :], slot, start)

    def project_block(slot):
        def step(i, carry):
            project_half(slot, i)
            return carry

        lax.fori_loop(0, 2, step, 0)

    def own_step(i, carry):
        project(x_ref[pl.ds(pl.multiple_of(i * half, half), half), :], REACH, i * half, True)
        return carry

    def pass_on(p):
        for side in (0, 1):

            @pl.when(exists[side])
            def _():
                x_copy(side, p).wait_recv()
                y_copy(side, p).start()

            @pl.when(jnp.logical_and(exists[side], core == 1 - side))
            def _():
                f_copy(0, p).start()

        if p + AHEAD < PIECES:
            send(p + AHEAD)

    lax.fori_loop(0, 2, own_step, 0)
    wof_ref[pl.ds(pl.multiple_of(t * 2 * part, part), 2 * part), :] = wo_ref[...]
    pass_on(0)
    w_copy.wait_recv()
    wf_copy.start()
    for p in range(1, PIECES // 2):
        pass_on(p)
    own_copy.wait_recv()
    project_block(3 - 2 * core)
    for p in range(PIECES // 2, PIECES):
        pass_on(p)
    for side in (0, 1):

        @pl.when(exists[side])
        def _():
            project_half(slots[side], t)

    for p in range(PIECES):
        for side in (0, 1):

            @pl.when(exists[side])
            def _():
                y_copy(side, p).wait_recv()

            @pl.when(jnp.logical_and(exists[side], core == 1 - side))
            def _():
                f_copy(1, p).start()

    for side in (0, 1):

        @pl.when(exists[side])
        def _():
            project_half(slots[side], 1 - t)

        @pl.when(jnp.logical_and(exists[side], core == side))
        def _():
            for which in (0, 1):
                for p in range(PIECES):
                    f_copy(which, p).wait_recv()
            project_block(1 + 2 * core)

    wf_copy.wait_recv()
    for copy in (own_copy, w_copy, wf_copy):
        copy.wait_send()
    for p in range(PIECES):
        for side in (0, 1):

            @pl.when(exists[1 - side])
            def _():
                x_copy(side, p).wait_send()

            @pl.when(exists[side])
            def _():
                y_copy(side, p).wait_send()

            @pl.when(jnp.logical_and(exists[side], core == 1 - side))
            def _():
                f_copy(0, p).wait_send()
                f_copy(1, p).wait_send()


def halo_qkv(x, wo, gain, shift, wq, wk, wv, qb, vb):
    height, width = x.shape
    cols = wq.shape[1]
    blocks = 2 * REACH + 1
    wide = jax.ShapeDtypeStruct((blocks * height, cols), BF)
    pair = DMA((2, PIECES))
    return pl.pallas_call(
        halo_kernel,
        out_shape=(
            wide, wide, wide,
            jax.ShapeDtypeStruct((height, width), BF),
            jax.ShapeDtypeStruct((2 * wo.shape[0], wo.shape[1]), BF),
            jax.ShapeDtypeStruct((16, 128), F32),
        ),
        in_specs=[whole()] * 9,
        out_specs=[whole()] * 6,
        scratch_shapes=[pltpu.VMEM((blocks, height, width), BF)]
        + [pair, pair, pair, pair, DMA, DMA, pair, pair, DMA, DMA, DMA, DMA],
        compiler_params=pltpu.CompilerParams(
            collective_id=0, has_side_effects=True, vmem_limit_bytes=VMEM_BYTES
        ),
        name="halo_qkv",
    )(x, wo, gain, shift, wq, wk, wv, qb, vb)


def split3(values):
    first = values.astype(BF).astype(F32)
    second = (values - first).astype(BF).astype(F32)
    return first, second, values - first - second


def code_tile(rows, keys_code):
    count = rows.shape[1]
    terms = split3(-rows)
    lane = lax.broadcasted_iota(jnp.int32, (128, count), 0)
    tall = jnp.zeros((128, count), F32)
    for h in range(8):
        for base, row in ((LOGS, h), (CENTRES, 8 + h)):
            for i in range(3):
                tall = jnp.where(lane == base + 3 * h + i, terms[i][row : row + 1], tall)
    wide = jnp.transpose(tall)
    column = lax.broadcasted_iota(jnp.int32, wide.shape, 1)
    same = jnp.logical_and(column < CLIPS, keys_code.astype(F32) == 0.0)
    return jnp.where(same, 1.0, wide).astype(BF)


def tile_at(j):
    return pl.ds(pl.multiple_of(j * TILE, TILE), TILE)


def lanes_of(c):
    return pl.ds(c * 128, 128)


def beside(left, right):
    return jnp.concatenate([left, right], axis=1)


def stacked_heads(values, codes):
    lower = lax.broadcasted_iota(jnp.int32, values.shape, 1) < HEAD_DIM
    none = jnp.zeros_like(values)
    return jnp.concatenate(
        [beside(jnp.where(lower, values, none), codes[0]), beside(jnp.where(lower, none, values), codes[1])],
        axis=0,
    )


def heads_out(turned):
    pair = jnp.concatenate([turned[:HEAD_DIM, :TILE], turned[HEAD_DIM:, TILE:]], axis=0)
    return jnp.transpose(pair)


def within(lane, start):
    return jnp.logical_and(lane >= start, lane < start + 3)


def attfinish_kernel(b_ref, q_ref, k_ref, v_ref, kc_ref, n_ref, o_ref, lse_ref, r_ref, m_ref, l_ref, acc_ref):
    height, cols = o_ref.shape
    pairs, tiles = cols // 128, height // TILE
    steep = jnp.logical_not(jnp.max(n_ref[0:8, :]) * jnp.max(n_ref[8:16, :]) <= SAFE * SAFE)
    lane = lax.broadcasted_iota(jnp.int32, (TILE, 128), 1)

    def groups(values):
        return values.reshape(TILE // 8, 8, values.shape[1])

    def one(i, carry):
        lo, hi = b_ref[0, i], b_ref[1, i]
        own = pl.ds(pl.multiple_of(REACH * height + i * TILE, TILE), TILE)
        same = jnp.logical_and(lane < CLIPS, kc_ref[own, :].astype(F32) == 0.0)
        code = jnp.where(same, 1.0, 0.0).astype(BF)
        for c in range(pairs):
            r_ref[c] = stacked_heads(q_ref[own, lanes_of(c)], (code, code))
        acc_ref[...] = jnp.zeros(acc_ref.shape, F32)
        l_ref[...] = jnp.zeros(l_ref.shape, F32)
        m_ref[...] = jnp.zeros(m_ref.shape, F32)

        def score(j, c):
            return dot_nt(beside(k_ref[tile_at(j), lanes_of(c)], kc_ref[tile_at(j), :]), r_ref[c])

        def step(shift, j, carry):
            raised = []
            for c in range(pairs):
                s = score(j, c)
                e = jnp.exp(s - m_ref[c, 0:1, :] if shift else s)
                l_ref[c] += jnp.sum(groups(e), axis=0)
                raised.append(e.astype(BF))
            for c in range(pairs):
                acc_ref[c] += dot_tn(v_ref[tile_at(j), lanes_of(c)], raised[c])
            return carry

        @pl.when(jnp.logical_not(steep))
        def _():
            lax.fori_loop(lo, hi, functools.partial(step, False), 0)

        @pl.when(steep)
        def _():
            m_ref[...] = jnp.full(m_ref.shape, NEG, F32)

            def peak(j, carry):
                for c in range(pairs):
                    m_ref[c] = jnp.maximum(m_ref[c], jnp.max(groups(score(j, c)), axis=0))
                return carry

            lax.fori_loop(lo, hi, peak, 0)
            for c in range(pairs):
                m_ref[c] = jnp.broadcast_to(jnp.max(m_ref[c], axis=0, keepdims=True), m_ref.shape[1:])
            lax.fori_loop(lo, hi, functools.partial(step, True), 0)

        for c in range(pairs):
            total = jnp.sum(l_ref[c], axis=0, keepdims=True)
            o_ref[tile_at(i), lanes_of(c)] = heads_out(acc_ref[c] / total).astype(BF)
            logs = m_ref[c, 0:1, :] + jnp.log(total)
            lse_ref[2 * c : 2 * c + 1, tile_at(i)] = logs[:, :TILE]
            lse_ref[2 * c + 1 : 2 * c + 2, tile_at(i)] = logs[:, TILE:]
        return carry

    lse_ref[...] = jnp.zeros(lse_ref.shape, F32)
    lax.fori_loop(0, tiles, one, 0)


def local_call(kernel, name, out_shape, scratch, bounds, *values):
    grid = pltpu.PrefetchScalarGridSpec(
        num_scalar_prefetch=1,
        grid=(1,),
        in_specs=[whole()] * len(values),
        out_specs=jax.tree.map(lambda _: whole(), out_shape),
        scratch_shapes=scratch,
    )
    return pl.pallas_call(
        kernel,
        grid_spec=grid,
        out_shape=out_shape,
        compiler_params=pltpu.CompilerParams(vmem_limit_bytes=VMEM_BYTES),
        name=name,
    )(bounds, *values)


def attend(bounds, q, k, v, kc, norms, height):
    cols = k.shape[1]
    pairs = cols // 128
    out_shape = (jax.ShapeDtypeStruct((height, cols), BF), jax.ShapeDtypeStruct((8, height), F32))
    scratch = [
        pltpu.VMEM((pairs, 2 * TILE, 256), BF),
        pltpu.VMEM((pairs, 8, 2 * TILE), F32),
        pltpu.VMEM((pairs, 8, 2 * TILE), F32),
        pltpu.VMEM((pairs, 128, 2 * TILE), F32),
    ]
    return local_call(attfinish_kernel, "attend", out_shape, scratch, bounds, q, k, v, kc, norms)


def query_back_kernel(b_ref, q_ref, k_ref, v_ref, g_ref, kc_ref, qc_ref, dq_ref, r_ref, t_ref, acc_ref):
    height, cols = dq_ref.shape
    pairs, tiles = cols // 128, height // TILE
    lane = lax.broadcasted_iota(jnp.int32, (TILE, 128), 1)

    def one(i, carry):
        own = pl.ds(pl.multiple_of(REACH * height + i * TILE, TILE), TILE)
        code = qc_ref[own, :]
        none = jnp.zeros_like(code)
        for c in range(pairs):
            logs, centres = [], []
            for h in (2 * c, 2 * c + 1):
                logs.append(jnp.where(jnp.logical_or(lane < CLIPS, within(lane, LOGS + 3 * h)), code, none))
                centres.append(jnp.where(within(lane, CENTRES + 3 * h), code, none))
            r_ref[c] = stacked_heads(q_ref[own, lanes_of(c)], logs)
            t_ref[c] = stacked_heads(g_ref[own, lanes_of(c)], centres)
        acc_ref[...] = jnp.zeros(acc_ref.shape, F32)

        def step(j, carry):
            code = kc_ref[tile_at(j), :]
            steps = []
            for c in range(pairs):
                probs = jnp.exp(dot_nt(beside(k_ref[tile_at(j), lanes_of(c)], code), r_ref[c]))
                d_probs = dot_nt(beside(v_ref[tile_at(j), lanes_of(c)], code), t_ref[c])
                steps.append((probs * d_probs).astype(BF))
            for c in range(pairs):
                acc_ref[c] += dot_tn(k_ref[tile_at(j), lanes_of(c)], steps[c])
            return carry

        lax.fori_loop(b_ref[0, i], b_ref[1, i], step, 0)
        for c in range(pairs):
            dq_ref[tile_at(i), lanes_of(c)] = (heads_out(acc_ref[c]) * HEAD_DIM**-0.5).astype(BF)
        return carry

    lax.fori_loop(0, tiles, one, 0)


def query_back(bounds, q, k, v, g, kc, qc, height):
    cols = k.shape[1]
    pairs = cols // 128
    scratch = [pltpu.VMEM((pairs, 2 * TILE, 256), BF)] * 2 + [pltpu.VMEM((pairs, 128, 2 * TILE), F32)]
    out_shape = jax.ShapeDtypeStruct((height, cols), BF)
    return local_call(query_back_kernel, "query_back", out_shape, scratch, bounds, q, k, v, g, kc, qc)


def key_back_kernel(b_ref, q_ref, k_ref, v_ref, g_ref, kc_ref, qc_ref, dk_ref, dv_ref, r_ref, t_ref, ak_ref, av_ref):
    height, cols = dk_ref.shape
    pairs, tiles = cols // 128, height // TILE
    lane = lax.broadcasted_iota(jnp.int32, (TILE, 128), 1)

    def one(i, carry):
        own = pl.ds(pl.multiple_of(REACH * height + i * TILE, TILE), TILE)
        code = kc_ref[own, :]
        none, ones = jnp.zeros_like(code), jnp.ones_like(code)
        for c in range(pairs):
            logs, centres = [], []
            for h in (2 * c, 2 * c + 1):
                logs.append(jnp.where(lane < CLIPS, code, jnp.where(within(lane, LOGS + 3 * h), ones, none)))
                centres.append(jnp.where(within(lane, CENTRES + 3 * h), ones, none))
            r_ref[c] = stacked_heads(k_ref[own, lanes_of(c)], logs)
            t_ref[c] = stacked_heads(v_ref[own, lanes_of(c)], centres)
        ak_ref[...] = jnp.zeros(ak_ref.shape, F32)
        av_ref[...] = jnp.zeros(av_ref.shape, F32)

        def step(j, carry):
            code = qc_ref[tile_at(j), :]
            weights, steps = [], []
            for c in range(pairs):
                probs = jnp.exp(dot_nt(beside(q_ref[tile_at(j), lanes_of(c)], code), r_ref[c]))
                d_probs = dot_nt(beside(g_ref[tile_at(j), lanes_of(c)], code), t_ref[c])
                weights.append(probs.astype(BF))
                steps.append((probs * d_probs).astype(BF))
            for c in range(pairs):
                av_ref[c] += dot_tn(g_ref[tile_at(j), lanes_of(c)], weights[c])
                ak_ref[c] += dot_tn(q_ref[tile_at(j), lanes_of(c)], steps[c])
            return carry

        lax.fori_loop(b_ref[0, i], b_ref[1, i], step, 0)
        for c in range(pairs):
            dk_ref[tile_at(i), lanes_of(c)] = heads_out(ak_ref[c]).astype(BF)
            dv_ref[tile_at(i), lanes_of(c)] = heads_out(av_ref[c]).astype(BF)
        return carry

    lax.fori_loop(0, tiles, one, 0)


def key_back(bounds, q, k, v, g, kc, qc, height):
    cols = k.shape[1]
    pairs = cols // 128
    scratch = [pltpu.VMEM((pairs, 2 * TILE, 256), BF)] * 2 + [pltpu.VMEM((pairs, 128, 2 * TILE), F32)] * 2
    out_shape = (jax.ShapeDtypeStruct((height, cols), BF),) * 2
    return local_call(key_back_kernel, "key_back", out_shape, scratch, bounds, q, k, v, g, kc, qc)


class Ring:
    def __init__(self, given, outs, sibs, bufs, sems):
        self.given, self.outs, self.sibs, self.bufs, self.sems = given, outs, sibs, bufs, sems
        d = lax.axis_index("dp")
        n = lax.axis_size("dp") // 2
        chip = d // 2
        core = d - 2 * chip
        odd = chip - 2 * (chip // 2)
        spot = (1 - odd) * (chip // 2) + odd * (n - 1 - chip // 2)
        self.here = (1 - core) * spot + core * (n - 1 - spot)
        self.n, self.core = n, core
        self.sibling = {"dp": d + 1 - 2 * core}
        self.after = {"dp": self.device_at(self.wrap(self.here + 1))}
        self.before = {"dp": self.device_at(self.wrap(self.here - 1))}
        self.all = range(len(given))

    def wrap(self, index):
        return lax.rem(index + 2 * self.n, self.n)

    def device_at(self, rank):
        n, core = self.n, self.core
        walk = (1 - core) * rank + core * (n - 1 - rank)
        late = walk // (n // 2)
        return 2 * ((1 - late) * (2 * walk) + late * (2 * (n - walk) - 1)) + core

    def spans(self, a, owner, j):
        rows, cols = self.given[a].shape[0] // 2, self.given[a].shape[1]
        high, wide = self.bufs[a].shape[1], self.bufs[a].shape[2]
        count = cols // wide
        line = j // count
        row = pl.multiple_of(owner * rows + line * high, high)
        col = pl.multiple_of((j - line * count) * wide, wide)
        return pl.ds(row, high), pl.ds(col, wide)

    def s_copy(self, a):
        rows = self.given[a].shape[0] // 2
        span = pl.ds(pl.multiple_of((1 - self.core) * rows, rows), rows)
        return remote(self.given[a].at[span], self.sibs[a], self.sems[0].at[a], self.sems[1].at[a], self.sibling)

    def r_copy(self, a, s):
        buf = self.bufs[a]
        return remote(buf.at[s], buf.at[s + 1], self.sems[2].at[a, s], self.sems[3].at[a, s], self.after)

    def out_spot(self, a, s):
        return self.outs[a].at[self.spans(a, self.core, self.wrap(self.here + 1 - s))]

    def g_copy(self, a, s):
        spot = self.out_spot(a, s)
        return remote(spot, spot, self.sems[4].at[a, s], self.sems[5].at[a, s], self.after)

    def c_copy(self, a, s):
        spot = self.out_spot(a, s)
        return remote(spot, spot, self.sems[6].at[a, s], self.sems[7].at[a, s], self.sibling)

    def terms(self, a, j):
        mine = self.given[a][self.spans(a, self.core, j)].astype(F32)
        return mine + self.sibs[a][self.spans(a, 0, j)].astype(F32)

    def swap(self):
        for a in self.all:
            self.s_copy(a).start()

    def first(self):
        for a in self.all:
            self.s_copy(a).wait_recv()
            self.bufs[a][0] = self.terms(a, self.here).astype(self.bufs[a].dtype)
            self.r_copy(a, 0).start()

    def reduce_step(self, s):
        for a in self.all:
            local = self.terms(a, self.wrap(self.here - s))
            self.r_copy(a, s - 1).wait_recv()
            self.bufs[a][s] = (self.bufs[a][s].astype(F32) + local).astype(self.bufs[a].dtype)
            self.r_copy(a, s).start()

    def turn(self):
        n = self.n
        for a in self.all:
            j = self.wrap(self.here + 1)
            local = self.terms(a, j)
            self.r_copy(a, n - 2).wait_recv()
            done = (self.bufs[a][n - 1].astype(F32) + local).astype(self.bufs[a].dtype)
            self.outs[a][self.spans(a, self.core, j)] = done
            self.g_copy(a, 0).start()
            self.c_copy(a, 0).start()

    def gather_step(self, s):
        for a in self.all:
            self.g_copy(a, s - 1).wait_recv()
            self.g_copy(a, s).start()
            self.c_copy(a, s).start()

    def last(self):
        n = self.n
        for a in self.all:
            self.g_copy(a, n - 2).wait_recv()
            self.c_copy(a, n - 1).start()

    def settle(self):
        n = self.n
        for a in self.all:
            self.s_copy(a).wait_send()
            self.c_copy(a, n - 1).wait()

        def step(s, carry):
            for a in self.all:
                self.r_copy(a, s).wait_send()
                self.g_copy(a, s).wait_send()
                self.c_copy(a, s).wait()
            return carry

        lax.fori_loop(0, n - 1, step, 0)


def between(step, begin, end, count):
    def body(s, carry):
        step(s)
        return carry

    if begin + count < end:
        lax.fori_loop(begin + count, end, body, 0)


def ring_scratch(shapes, n):
    count = len(shapes)
    sibs, bufs = [], []
    for rows, cols in shapes:
        wide = min(cols, 384)
        sibs.append(pltpu.VMEM((rows // 2, cols), BF))
        bufs.append(pltpu.VMEM((n, rows * cols // (2 * n * wide), wide), BF))
    sems = [DMA((count,))] * 2 + [DMA((count, n - 1))] * 4 + [DMA((count, n))] * 2
    return sibs + bufs, sems


def norm_back_rows(grad, values, gain):
    middle = jnp.mean(values, axis=-1, keepdims=True)
    centred = values - middle
    inverse = lax.rsqrt(jnp.mean(centred * centred, axis=-1, keepdims=True) + 1e-05)
    n = centred * inverse
    t = grad * gain
    back = (t - jnp.mean(t, axis=-1, keepdims=True) - n * jnp.mean(t * n, axis=-1, keepdims=True)) * inverse
    return back, grad * n


def column_sums(values):
    return jnp.sum(values, axis=0, keepdims=True)


def mid_kernel(
    part_ref, res_ref, cot_ref, gain_ref, wo_ref, o_ref, lse_ref, kc_ref, f1_ref, f2_ref,
    xw_ref, qc_ref, rg_ref, low_ref, vec_ref, g1_ref, g2_ref,
    oth_ref, st_ref, sw_ref, sib1, sib2, buf1, buf2,
    sy, ry, sx, rx, ss, rs, sf, rf, *ring_sems,
):
    d, core, has_left, has_right = place()
    t = lax.axis_index("tensor")
    height, cols = o_ref.shape
    piece = height // PIECES
    sibling = {"dp": d + 1 - 2 * core}
    across = {"tensor": 1 - t}
    exists = (has_left, has_right)
    slots = (0, 2 * REACH)
    ring = Ring((f1_ref, f2_ref), (g1_ref, g2_ref), (sib1, sib2), (buf1, buf2), ring_sems)
    n = ring.n
    greet([
        (None, sibling), (None, across), (has_left, {"dp": d - 2}), (has_right, {"dp": d + 2}),
        (None, ring.after), (None, ring.before),
    ])

    def y_copy(p):
        span = pl.ds(p * piece, piece)
        return remote(part_ref.at[span], oth_ref.at[span], sy.at[p], ry.at[p], across)

    def refs(p):
        if p == PIECES:
            return st_ref, lambda slot: sw_ref.at[slot]
        span = pl.ds(p * piece, piece)
        return xw_ref.at[REACH, span], lambda slot: xw_ref.at[slot, span]

    def x_copy(side, p):
        src, dst = refs(p)
        return remote(
            src, dst(slots[side]), sx.at[side, p], rx.at[side, p],
            {"dp": d + 2 if side == 0 else d - 2},
        )

    def s_copy(p):
        src, dst = refs(p)
        return remote(src, dst(1 + 2 * core), ss.at[p], rs.at[p], sibling)

    def f_copy(p):
        _, dst = refs(p)
        return remote(dst(4 - 4 * core), dst(3 - 2 * core), sf.at[p], rf.at[p], sibling)

    def send(p):
        for side in (0, 1):

            @pl.when(exists[1 - side])
            def _():
                x_copy(side, p).start()

        s_copy(p).start()

    def pass_on(p):
        for side in (0, 1):

            @pl.when(exists[side])
            def _():
                x_copy(side, p).wait_recv()

            @pl.when(jnp.logical_and(exists[side], core == 1 - side))
            def _():
                f_copy(p).start()

    for p in range(AHEAD):
        y_copy(p).start()
    ring.swap()
    gain = gain_ref[...].astype(F32)
    picks = lax.broadcasted_iota(jnp.int32, (8, cols), 1) // HEAD_DIM
    picks = (picks == lax.broadcasted_iota(jnp.int32, (8, cols), 0)).astype(F32)
    st_ref[0:8, :] = lse_ref[...]
    vec_ref[...] = jnp.zeros(vec_ref.shape, F32)

    def back(p):
        span = pl.ds(p * piece, piece)
        y_copy(p).wait_recv()
        if p + AHEAD < PIECES:
            y_copy(p + AHEAD).start()
        grad = part_ref[span, :].astype(F32) + oth_ref[span, :].astype(F32)
        turned, scaled = norm_back_rows(grad, res_ref[span, :], gain)
        total = cot_ref[span, :].astype(F32) + turned
        low = total.astype(BF)
        rg_ref[span, :] = total
        low_ref[span, :] = low
        vec_ref[0:1, :] += column_sums(scaled)
        vec_ref[1:2, :] += column_sums(grad)
        vec_ref[2:3, :] += column_sums(low.astype(F32))
        mixed_grad = dot_nt(low, wo_ref[...]).astype(BF)
        xw_ref[REACH, span, :] = mixed_grad
        product = mixed_grad.astype(F32) * o_ref[span, :].astype(F32)
        st_ref[8:16, span] = lax.dot_general(
            picks, product, (((1,), (1,)), ((), ())),
            precision=lax.Precision.HIGHEST, preferred_element_type=F32,
        )

    ring.first()
    for p in range(PIECES):
        back(p)
        if 1 + p < n - 1:
            ring.reduce_step(1 + p)
        send(p)
    send(PIECES)
    sw_ref[REACH] = st_ref[...]
    between(ring.reduce_step, 1, n - 1, PIECES)
    ring.turn()

    def code(slot):
        def step(i, carry):
            rows = pl.ds(pl.multiple_of(slot * height + i * TILE, TILE), TILE)
            stats = sw_ref[slot, :, pl.ds(pl.multiple_of(i * TILE, TILE), TILE)]
            qc_ref[rows, :] = code_tile(stats, kc_ref[rows, :])
            return carry

        lax.fori_loop(0, height // TILE, step, 0)

    for p in range(PIECES):
        pass_on(p)
        if 1 + p < n - 1:
            ring.gather_step(1 + p)
    pass_on(PIECES)
    between(ring.gather_step, 1, n - 1, PIECES)
    code(REACH)
    ring.last()
    for p in range(PIECES + 1):
        s_copy(p).wait()
        for side in (0, 1):

            @pl.when(exists[1 - side])
            def _():
                x_copy(side, p).wait_send()

            @pl.when(jnp.logical_and(exists[side], core == 1 - side))
            def _():
                f_copy(p).wait_send()

            @pl.when(jnp.logical_and(exists[side], core == side))
            def _():
                f_copy(p).wait_recv()

    code(3 - 2 * core)
    for side in (0, 1):

        @pl.when(exists[side])
        def _():
            code(slots[side])

        @pl.when(jnp.logical_and(exists[side], core == side))
        def _():
            code(1 + 2 * core)

    for p in range(PIECES):
        y_copy(p).wait_send()
    ring.settle()


def mid(part, residual, cotangent, gain, wo, o, lse, kc, f1, f2):
    blocks = 2 * REACH + 1
    height, width = part.shape
    n = lax.axis_size("dp") // 2
    pair, line = DMA((2, PIECES + 1)), DMA((PIECES + 1,))
    room, sems = ring_scratch((f1.shape, f2.shape), n)
    shape = jax.ShapeDtypeStruct
    return pl.pallas_call(
        mid_kernel,
        out_shape=(
            shape((blocks,) + o.shape, BF), shape(kc.shape, BF), shape(part.shape, F32),
            shape(part.shape, BF), shape((8, width), F32), shape(f1.shape, BF), shape(f2.shape, BF),
        ),
        in_specs=[whole()] * 10,
        out_specs=[whole()] * 7,
        scratch_shapes=[
            pltpu.VMEM(part.shape, BF), pltpu.VMEM((16, height), F32), pltpu.VMEM((blocks, 16, height), F32),
        ]
        + room
        + [DMA((PIECES,)), DMA((PIECES,)), pair, pair, line, line, line, line]
        + sems,
        compiler_params=pltpu.CompilerParams(
            collective_id=1, has_side_effects=True, vmem_limit_bytes=MID_BYTES
        ),
        name="mid",
    )(part, residual, cotangent, gain, wo, o, lse, kc, f1, f2)


def finish_kernel(
    rounds, dq_ref, dk_ref, dv_ref, wq_ref, wk_ref, wv_ref, a_ref, low_ref, o_ref, x_ref, rg_ref, gain_ref, vec_ref,
    ig_ref, g_ref, vs_ref,
    part_ref, oth_ref, own_ref, send_ref, got_ref, sib, buf, sy, ry, sd, rd, *ring_sems,
):
    d, core, _, _ = place()
    t = lax.axis_index("tensor")
    height, cols = dq_ref.shape
    width = x_ref.shape[1]
    piece = height // PIECES
    across = {"tensor": 1 - t}
    ring = Ring((own_ref,), (g_ref,), (sib,), (buf,), ring_sems)
    n = ring.n
    partners = []
    for r in range(rounds):
        bit = (d // 2**r) - 2 * (d // 2 ** (r + 1))
        partners.append({"dp": d + 2**r * (1 - 2 * bit)})
    greet([(None, across), (None, ring.after), (None, ring.before)] + [(None, p) for p in partners])

    def y_copy(p):
        span = pl.ds(p * piece, piece)
        return remote(part_ref.at[span], oth_ref.at[span], sy.at[p], ry.at[p], across)

    def d_copy(r):
        return remote(send_ref.at[r], got_ref.at[r], sd.at[r], rd.at[r], partners[r])

    def share(p):
        span = pl.ds(p * piece, piece)
        part = dot_nt(dq_ref[span, :], wq_ref[...]) + dot_nt(dk_ref[span, :], wk_ref[...])
        part_ref[span, :] = (part + dot_nt(dv_ref[span, :], wv_ref[...])).astype(BF)

    def weights(which):
        span = pl.ds(pl.multiple_of(which * (width // 2), width // 2), width // 2)
        attn = a_ref[:, span]
        for i, ref in enumerate((dq_ref, dk_ref, dv_ref)):
            own_ref[span, i * cols : (i + 1) * cols] = dot_tn(attn, ref[...]).astype(BF)
        own_ref[span, 3 * cols : 4 * cols] = dot_tn(low_ref[:, span], o_ref[...]).astype(BF)

    for p in range(AHEAD):
        share(p)
        y_copy(p).start()
    weights(1 - core)
    for p in range(AHEAD, PIECES):
        share(p)
    ring.swap()
    weights(core)
    gain = gain_ref[...].astype(F32)
    gains, shifts = [], []

    def back(p):
        span = pl.ds(p * piece, piece)
        y_copy(p).wait_recv()
        if p + AHEAD < PIECES:
            y_copy(p + AHEAD).start()
        grad = part_ref[span, :].astype(F32) + oth_ref[span, :].astype(F32)
        turned, scaled = norm_back_rows(grad, x_ref[span, :].astype(F32), gain)
        ig_ref[span, :] = rg_ref[span, :] + turned
        gains.append(column_sums(scaled))
        shifts.append(column_sums(grad))

    ring.first()
    for p in range(PIECES):
        back(p)
        if 1 + p < n - 1:
            ring.reduce_step(1 + p)
    between(ring.reduce_step, 1, n - 1, PIECES)
    send_ref[0] = vec_ref[...]
    send_ref[0, 6:7, 0:cols] = column_sums(dq_ref[...].astype(F32))
    send_ref[0, 6:7, cols : 2 * cols] = column_sums(dv_ref[...].astype(F32))
    send_ref[0, 7:8, :] = sum(gains[1:], gains[0])
    send_ref[0, 8:9, :] = sum(shifts[1:], shifts[0])
    ring.turn()
    d_copy(0).start()
    for s in range(max(rounds, PIECES)):
        if s < rounds:
            d_copy(s).wait_recv()
            total = send_ref[s] + got_ref[s]
            if s + 1 < rounds:
                send_ref[s + 1] = total
                d_copy(s + 1).start()
            else:
                vs_ref[...] = total
        if s < PIECES and 1 + s < n - 1:
            ring.gather_step(1 + s)
    between(ring.gather_step, 1, n - 1, PIECES)
    ring.last()
    for p in range(PIECES):
        y_copy(p).wait_send()
    for r in range(rounds):
        d_copy(r).wait_send()
    ring.settle()


def finish(dq, dk, dv, wq, wk, wv, attn, low, o, x, rg, gain, vectors):
    height, cols = dq.shape
    width = x.shape[1]
    size = lax.axis_size("dp")
    rounds = size.bit_length() - 1
    n = size // 2
    weights = (width, 4 * cols)
    room, sems = ring_scratch((weights,), n)
    shape = jax.ShapeDtypeStruct
    return pl.pallas_call(
        functools.partial(finish_kernel, rounds),
        out_shape=(shape((height, width), F32), shape(weights, BF), shape(vectors.shape, F32)),
        in_specs=[whole()] * 13,
        out_specs=[whole()] * 3,
        scratch_shapes=[
            pltpu.VMEM((height, width), BF), pltpu.VMEM((height, width), BF), pltpu.VMEM(weights, BF),
            pltpu.VMEM((rounds,) + vectors.shape, F32), pltpu.VMEM((rounds,) + vectors.shape, F32),
        ]
        + room
        + [DMA((PIECES,)), DMA((PIECES,)), DMA((rounds,)), DMA((rounds,))]
        + sems,
        compiler_params=pltpu.CompilerParams(
            collective_id=2, has_side_effects=True, vmem_limit_bytes=VMEM_BYTES
        ),
        name="finish",
    )(dq, dk, dv, wq, wk, wv, attn, low, o, x, rg, gain, vectors)


def swapped(value):
    return lax.ppermute(value, "tensor", [(0, 1), (1, 0)])


def on_device(
    inputs, clip_ids, attn_gain, attn_shift, w_query, query_bias, w_key, w_value, value_bias,
    w_out, out_bias, mlp_gain, mlp_shift, w_fc1, fc1_bias, w_fc2, fc2_bias, cotangent,
):
    height, width = inputs.shape
    d = lax.axis_index("dp")
    t = lax.axis_index("tensor")
    reach = REACH * height

    padded = jnp.pad(clip_ids, (reach, reach), constant_values=-1)
    window = lax.dynamic_slice_in_dim(padded, d * height, height + 2 * reach)
    own = lax.dynamic_slice_in_dim(clip_ids, d * height, height)
    firsts, lasts = own[::TILE], own[TILE - 1 :: TILE]
    origin = d * height - reach
    begin = jnp.sum((clip_ids[None, :] < firsts[:, None]).astype(jnp.int32), axis=1) - origin
    end = jnp.sum((clip_ids[None, :] <= lasts[:, None]).astype(jnp.int32), axis=1) - origin
    bounds = jnp.stack([begin // TILE, (end + TILE - 1) // TILE])
    lane = jnp.arange(128, dtype=jnp.int32)[None, :]
    clip_far = jnp.where(window[:, None] == lane, 0.0, FAR)
    key_code = jnp.where(lane < CLIPS, clip_far, 1.0).astype(BF)

    row = lambda v: v[None, :]
    q, k, v, attn_input, w_out_full, norms = halo_qkv(
        inputs, w_out, row(attn_gain), row(attn_shift), w_query, w_key, w_value,
        row(query_bias), row(value_bias),
    )
    mixed, logs = attend(bounds, q, k, v, key_code, norms, height)
    other = swapped(mixed)
    w_mine = w_out
    w_other = lax.dynamic_slice_in_dim(w_out_full, (1 - t) * w_out.shape[0], w_out.shape[0])
    source = inputs.astype(F32)
    residual = source + dot_nn(mixed, w_mine) + dot_nn(other, w_other) + out_bias.astype(F32)
    mlp_input = (norm_rows(residual) * mlp_gain.astype(F32) + mlp_shift.astype(F32)).astype(BF)
    preact = dot_nn(mlp_input, w_fc1) + fc1_bias.astype(F32)
    cdf = 0.5 * (1.0 + lax.erf(preact * (2.0**-0.5)))
    pdf = jnp.exp(-0.5 * preact * preact) * 0.3989422804014327
    activated = (preact * cdf).astype(BF)
    slope = cdf + preact * pdf
    pre_grad = (dot_nt(cotangent, w_fc2) * slope).astype(BF)
    part = dot_nt(pre_grad, w_fc1).astype(BF)
    out_part = dot_nn(activated, w_fc2).astype(BF)
    fc1_grad = dot_tn(mlp_input, pre_grad).astype(BF)
    fc2_grad = dot_tn(activated, cotangent).astype(BF)
    fc2_bias_grad = jnp.sum(cotangent.astype(F32), axis=0)
    fc1_bias_grad = jnp.sum(pre_grad.astype(F32), axis=0)
    grad_win, query_code, residual_grad, low, mid_vectors, fc1_sum, fc2_sum = mid(
        part, residual, cotangent, row(mlp_gain), w_out, mixed, logs, key_code, fc1_grad, fc2_grad
    )
    grad_win = grad_win.reshape(-1, grad_win.shape[2])
    out_part, query_code = lax.optimization_barrier((out_part, query_code))
    out_other = swapped(out_part)
    query_low = query_back(bounds, q, k, v, grad_win, key_code, query_code, height)
    key_low, value_low = key_back(bounds, q, k, v, grad_win, key_code, query_code, height)
    out_other, key_low = lax.optimization_barrier((out_other, key_low))
    layer_out = (
        residual + (out_part.astype(F32) + out_other.astype(F32)) + fc2_bias.astype(F32)
    ).astype(BF)
    vectors = jnp.concatenate(
        [mid_vectors[:3], row(fc2_bias_grad), fc1_bias_grad.reshape(2, width), jnp.zeros((10, width), F32)]
    )
    inputs_grad, attn_sum, sums = finish(
        query_low, key_low, value_low, w_query, w_key, w_value, attn_input, low, mixed, inputs,
        residual_grad, row(attn_gain), vectors,
    )
    cols = w_query.shape[1]
    pieces = [attn_sum[:, i * cols : (i + 1) * cols].astype(F32) for i in range(4)]
    return (
        layer_out, inputs_grad, sums[7], sums[8],
        pieces[0], sums[6, :cols], pieces[1], pieces[2], sums[6, cols:],
        pieces[3].T, sums[2], sums[0], sums[1],
        fc1_sum.astype(F32), sums[4:6].reshape(-1), fc2_sum.astype(F32), sums[3],
    )


def solution(mesh):
    rows, cols, split, every = P("dp", None), P(None, "tensor"), P("tensor"), P()
    tall = P("tensor", None)
    in_specs = (
        rows, every, every, every, cols, split, cols, cols, split, tall, every, every, every,
        cols, split, tall, every, rows,
    )
    out_specs = (
        rows, rows, every, every, cols, split, cols, cols, split, tall, every, every, every,
        cols, split, tall, every,
    )
    return jax.shard_map(on_device, mesh=mesh, in_specs=in_specs, out_specs=out_specs, check_vma=False)
```

```python
import functools

import jax
import jax.numpy as jnp
from jax import lax
from jax.experimental import pallas as pl
from jax.experimental.pallas import tpu as pltpu
from jax.sharding import PartitionSpec as P

HEAD_DIM = 64
REACH = 2
TILE = 256
PIECES = 6
AHEAD = 2
NEG = -3e38
CLIPS = 64
LOGS = 64
CENTRES = 96
FAR = -(2.0**100)
SAFE = 40.0
BF = jnp.bfloat16
F32 = jnp.float32
MESH = pl.DeviceIdType.MESH
VMEM = pltpu.VMEM
VMEM_BYTES = 26_000_000
MID_BYTES = 50_000_000
FINISH_BYTES = 32_000_000
PARTS = 3
STRIP = 128
STRIPS = 3
DMA = pltpu.SemaphoreType.DMA


def dot_nn(left, right):
    return jnp.dot(left, right, preferred_element_type=F32)


def dot_tn(left, right):
    return lax.dot_general(left, right, (((0,), (0,)), ((), ())), preferred_element_type=F32)


def dot_nt(left, right):
    return lax.dot_general(left, right, (((1,), (1,)), ((), ())), preferred_element_type=F32)


def whole():
    return pl.BlockSpec(memory_space=VMEM)


def remote(src, dst, send_sem, recv_sem, device):
    return pltpu.make_async_remote_copy(
        src_ref=src,
        dst_ref=dst,
        send_sem=send_sem,
        recv_sem=recv_sem,
        device_id=device,
        device_id_type=MESH,
    )


def place():
    d = lax.axis_index("dp")
    chip = d // 2
    core = d - 2 * chip
    has_left = chip > 0
    has_right = chip < lax.axis_size("dp") // 2 - 1
    return d, core, has_left, has_right


def greet(targets):
    barrier = pltpu.get_barrier_semaphore()
    count = 0
    for present, device in targets:
        if present is None:
            pl.semaphore_signal(barrier, inc=1, device_id=device, device_id_type=MESH)
            count = count + 1
        else:

            @pl.when(present)
            def _():
                pl.semaphore_signal(barrier, inc=1, device_id=device, device_id_type=MESH)

            count = count + present.astype(jnp.int32)
    pl.semaphore_wait(barrier, count)


def norm_rows(values):
    middle = jnp.mean(values, axis=-1, keepdims=True)
    centred = values - middle
    spread = jnp.mean(centred * centred, axis=-1, keepdims=True)
    return centred * lax.rsqrt(spread + 1e-05)


def halo_kernel(
    x_ref, wo_ref, gain_ref, shift_ref, wq_ref, wk_ref, wv_ref, qb_ref, vb_ref,
    q_ref, k_ref, v_ref, a_ref, wof_ref, n_ref,
    win, sx, rx, sy, ry, ss, rs, sf, rf, sw, rw, sv, rv,
):
    d, core, has_left, has_right = place()
    t = lax.axis_index("tensor")
    height = x_ref.shape[0]
    half = height // 2
    piece = half // PIECES
    sibling = {"dp": d + 1 - 2 * core}
    across = {"tensor": 1 - t}
    exists = (has_left, has_right)
    slots = (0, 2 * REACH)
    greet([(None, sibling), (None, across), (has_left, {"dp": d - 2}), (has_right, {"dp": d + 2})])

    def rows(which, p):
        return pl.ds(pl.multiple_of(which * half + p * piece, piece), piece)

    def x_copy(side, p):
        return remote(
            x_ref.at[rows(t, p)], win.at[slots[side], rows(t, p)], sx.at[side, p], rx.at[side, p],
            {"dp": d + 2 if side == 0 else d - 2},
        )

    def y_copy(side, p):
        spot = win.at[slots[side], rows(t, p)]
        return remote(spot, spot, sy.at[side, p], ry.at[side, p], across)

    def f_copy(which, p):
        span = rows(t if which == 0 else 1 - t, p)
        return remote(
            win.at[4 - 4 * core, span], win.at[3 - 2 * core, span], sf.at[which, p], rf.at[which, p],
            sibling,
        )

    own_copy = remote(x_ref, win.at[1 + 2 * core], ss, rs, sibling)
    part = wo_ref.shape[0] // 2
    wo_rows = pl.ds(pl.multiple_of(core * part, part), part)

    def full_rows(which):
        return pl.ds(pl.multiple_of((2 * which + core) * part, part), part)

    w_copy = remote(wo_ref.at[wo_rows], wof_ref.at[full_rows(t)], sw, rw, across)
    wf_copy = remote(wof_ref.at[full_rows(1 - t)], wof_ref.at[full_rows(1 - t)], sv, rv, sibling)

    def send(p):
        for side in (0, 1):

            @pl.when(exists[1 - side])
            def _():
                x_copy(side, p).start()

    for p in range(AHEAD):
        send(p)
    w_copy.start()
    own_copy.start()
    gain, shift = gain_ref[...].astype(F32), shift_ref[...].astype(F32)
    query_bias, value_bias = qb_ref[...].astype(F32), vb_ref[...].astype(F32)

    n_ref[...] = jnp.zeros(n_ref.shape, F32)

    def raise_norm(spot, values):
        for c in range(values.shape[1] // 128):
            part = values[:, c * 128 : c * 128 + 128]
            norm = jnp.max(jnp.sum(part * part, axis=1, keepdims=True), axis=0, keepdims=True)
            n_ref[spot, :] = jnp.maximum(n_ref[spot, :], norm)

    def project(values, slot, start, keep=False):
        attn = (norm_rows(values.astype(F32)) * gain + shift).astype(BF)
        out = pl.ds(pl.multiple_of(slot * height + start, 128), half)
        if keep:
            a_ref[pl.ds(pl.multiple_of(start, half), half), :] = attn
        query = (dot_nn(attn, wq_ref[...]) + query_bias) * HEAD_DIM**-0.5
        key = dot_nn(attn, wk_ref[...])
        q_ref[out, :] = query.astype(BF)
        k_ref[out, :] = key.astype(BF)
        raise_norm(slice(0, 8), query)
        raise_norm(slice(8, 16), key)
        v_ref[out, :] = (dot_nn(attn, wv_ref[...]) + value_bias).astype(BF)

    def project_half(slot, which):
        start = which * half
        project(win[slot, pl.ds(pl.multiple_of(start, half), half), :], slot, start)

    def project_block(slot):
        def step(i, carry):
            project_half(slot, i)
            return carry

        lax.fori_loop(0, 2, step, 0)

    def own_step(i, carry):
        project(x_ref[pl.ds(pl.multiple_of(i * half, half), half), :], REACH, i * half, True)
        return carry

    def pass_on(p):
        for side in (0, 1):

            @pl.when(exists[side])
            def _():
                x_copy(side, p).wait_recv()
                y_copy(side, p).start()

            @pl.when(jnp.logical_and(exists[side], core == 1 - side))
            def _():
                f_copy(0, p).start()

        if p + AHEAD < PIECES:
            send(p + AHEAD)

    lax.fori_loop(0, 2, own_step, 0)
    wof_ref[pl.ds(pl.multiple_of(t * 2 * part, part), 2 * part), :] = wo_ref[...]
    pass_on(0)
    w_copy.wait_recv()
    wf_copy.start()
    for p in range(1, PIECES // 2):
        pass_on(p)
    own_copy.wait_recv()
    project_block(3 - 2 * core)
    for p in range(PIECES // 2, PIECES):
        pass_on(p)
    for side in (0, 1):

        @pl.when(exists[side])
        def _():
            project_half(slots[side], t)

    for p in range(PIECES):
        for side in (0, 1):

            @pl.when(exists[side])
            def _():
                y_copy(side, p).wait_recv()

            @pl.when(jnp.logical_and(exists[side], core == 1 - side))
            def _():
                f_copy(1, p).start()

    for side in (0, 1):

        @pl.when(exists[side])
        def _():
            project_half(slots[side], 1 - t)

        @pl.when(jnp.logical_and(exists[side], core == side))
        def _():
            for which in (0, 1):
                for p in range(PIECES):
                    f_copy(which, p).wait_recv()
            project_block(1 + 2 * core)

    wf_copy.wait_recv()
    for copy in (own_copy, w_copy, wf_copy):
        copy.wait_send()
    for p in range(PIECES):
        for side in (0, 1):

            @pl.when(exists[1 - side])
            def _():
                x_copy(side, p).wait_send()

            @pl.when(exists[side])
            def _():
                y_copy(side, p).wait_send()

            @pl.when(jnp.logical_and(exists[side], core == 1 - side))
            def _():
                f_copy(0, p).wait_send()
                f_copy(1, p).wait_send()


def halo_qkv(x, wo, gain, shift, wq, wk, wv, qb, vb):
    height, width = x.shape
    cols = wq.shape[1]
    blocks = 2 * REACH + 1
    wide = jax.ShapeDtypeStruct((blocks * height, cols), BF)
    pair = DMA((2, PIECES))
    return pl.pallas_call(
        halo_kernel,
        out_shape=(
            wide, wide, wide,
            jax.ShapeDtypeStruct((height, width), BF),
            jax.ShapeDtypeStruct((2 * wo.shape[0], wo.shape[1]), BF),
            jax.ShapeDtypeStruct((16, 128), F32),
        ),
        in_specs=[whole()] * 9,
        out_specs=[whole()] * 6,
        scratch_shapes=[pltpu.VMEM((blocks, height, width), BF)]
        + [pair, pair, pair, pair, DMA, DMA, pair, pair, DMA, DMA, DMA, DMA],
        compiler_params=pltpu.CompilerParams(
            collective_id=0, has_side_effects=True, vmem_limit_bytes=VMEM_BYTES
        ),
        name="halo_qkv",
    )(x, wo, gain, shift, wq, wk, wv, qb, vb)


def split3(values):
    first = values.astype(BF).astype(F32)
    second = (values - first).astype(BF).astype(F32)
    return first, second, values - first - second


def code_tile(rows, keys_code):
    count = rows.shape[1]
    terms = split3(-rows)
    lane = lax.broadcasted_iota(jnp.int32, (128, count), 0)
    tall = jnp.zeros((128, count), F32)
    for h in range(8):
        for base, row in ((LOGS, h), (CENTRES, 8 + h)):
            for i in range(3):
                tall = jnp.where(lane == base + 3 * h + i, terms[i][row : row + 1], tall)
    wide = jnp.transpose(tall)
    column = lax.broadcasted_iota(jnp.int32, wide.shape, 1)
    same = jnp.logical_and(column < CLIPS, keys_code.astype(F32) == 0.0)
    return jnp.where(same, 1.0, wide).astype(BF)


def tile_at(j):
    return pl.ds(pl.multiple_of(j * TILE, TILE), TILE)


def lanes_of(c):
    return pl.ds(c * 128, 128)


def beside(left, right):
    return jnp.concatenate([left, right], axis=1)


def stacked_heads(values, codes):
    lower = lax.broadcasted_iota(jnp.int32, values.shape, 1) < HEAD_DIM
    none = jnp.zeros_like(values)
    return jnp.concatenate(
        [beside(jnp.where(lower, values, none), codes[0]), beside(jnp.where(lower, none, values), codes[1])],
        axis=0,
    )


def heads_out(turned):
    pair = jnp.concatenate([turned[:HEAD_DIM, :TILE], turned[HEAD_DIM:, TILE:]], axis=0)
    return jnp.transpose(pair)


def within(lane, start):
    return jnp.logical_and(lane >= start, lane < start + 3)


def attfinish_kernel(b_ref, q_ref, k_ref, v_ref, kc_ref, n_ref, o_ref, lse_ref, r_ref, m_ref, l_ref, acc_ref):
    height, cols = o_ref.shape
    pairs, tiles = cols // 128, height // TILE
    steep = jnp.logical_not(jnp.max(n_ref[0:8, :]) * jnp.max(n_ref[8:16, :]) <= SAFE * SAFE)
    lane = lax.broadcasted_iota(jnp.int32, (TILE, 128), 1)

    def groups(values):
        return values.reshape(TILE // 8, 8, values.shape[1])

    def one(i, carry):
        lo, hi = b_ref[0, i], b_ref[1, i]
        own = pl.ds(pl.multiple_of(REACH * height + i * TILE, TILE), TILE)
        same = jnp.logical_and(lane < CLIPS, kc_ref[own, :].astype(F32) == 0.0)
        code = jnp.where(same, 1.0, 0.0).astype(BF)
        for c in range(pairs):
            r_ref[c] = stacked_heads(q_ref[own, lanes_of(c)], (code, code))
        acc_ref[...] = jnp.zeros(acc_ref.shape, F32)
        l_ref[...] = jnp.zeros(l_ref.shape, F32)
        m_ref[...] = jnp.zeros(m_ref.shape, F32)

        def score(j, c):
            return dot_nt(beside(k_ref[tile_at(j), lanes_of(c)], kc_ref[tile_at(j), :]), r_ref[c])

        def step(shift, j, carry):
            raised = []
            for c in range(pairs):
                s = score(j, c)
                e = jnp.exp(s - m_ref[c, 0:1, :] if shift else s)
                l_ref[c] += jnp.sum(groups(e), axis=0)
                raised.append(e.astype(BF))
            for c in range(pairs):
                acc_ref[c] += dot_tn(v_ref[tile_at(j), lanes_of(c)], raised[c])
            return carry

        @pl.when(jnp.logical_not(steep))
        def _():
            lax.fori_loop(lo, hi, functools.partial(step, False), 0)

        @pl.when(steep)
        def _():
            m_ref[...] = jnp.full(m_ref.shape, NEG, F32)

            def peak(j, carry):
                for c in range(pairs):
                    m_ref[c] = jnp.maximum(m_ref[c], jnp.max(groups(score(j, c)), axis=0))
                return carry

            lax.fori_loop(lo, hi, peak, 0)
            for c in range(pairs):
                m_ref[c] = jnp.broadcast_to(jnp.max(m_ref[c], axis=0, keepdims=True), m_ref.shape[1:])
            lax.fori_loop(lo, hi, functools.partial(step, True), 0)

        for c in range(pairs):
            total = jnp.sum(l_ref[c], axis=0, keepdims=True)
            o_ref[tile_at(i), lanes_of(c)] = heads_out(acc_ref[c] / total).astype(BF)
            logs = m_ref[c, 0:1, :] + jnp.log(total)
            lse_ref[2 * c : 2 * c + 1, tile_at(i)] = logs[:, :TILE]
            lse_ref[2 * c + 1 : 2 * c + 2, tile_at(i)] = logs[:, TILE:]
        return carry

    lse_ref[...] = jnp.zeros(lse_ref.shape, F32)
    lax.fori_loop(0, tiles, one, 0)


def local_call(kernel, name, out_shape, scratch, bounds, *values):
    grid = pltpu.PrefetchScalarGridSpec(
        num_scalar_prefetch=1,
        grid=(1,),
        in_specs=[whole()] * len(values),
        out_specs=jax.tree.map(lambda _: whole(), out_shape),
        scratch_shapes=scratch,
    )
    return pl.pallas_call(
        kernel,
        grid_spec=grid,
        out_shape=out_shape,
        compiler_params=pltpu.CompilerParams(vmem_limit_bytes=VMEM_BYTES),
        name=name,
    )(bounds, *values)


def attend(bounds, q, k, v, kc, norms, height):
    cols = k.shape[1]
    pairs = cols // 128
    out_shape = (jax.ShapeDtypeStruct((height, cols), BF), jax.ShapeDtypeStruct((8, height), F32))
    scratch = [
        pltpu.VMEM((pairs, 2 * TILE, 256), BF),
        pltpu.VMEM((pairs, 8, 2 * TILE), F32),
        pltpu.VMEM((pairs, 8, 2 * TILE), F32),
        pltpu.VMEM((pairs, 128, 2 * TILE), F32),
    ]
    return local_call(attfinish_kernel, "attend", out_shape, scratch, bounds, q, k, v, kc, norms)


def query_back_kernel(b_ref, q_ref, k_ref, v_ref, g_ref, kc_ref, qc_ref, dq_ref, r_ref, t_ref, acc_ref):
    height, cols = dq_ref.shape
    pairs, tiles = cols // 128, height // TILE
    lane = lax.broadcasted_iota(jnp.int32, (TILE, 128), 1)

    def one(i, carry):
        own = pl.ds(pl.multiple_of(REACH * height + i * TILE, TILE), TILE)
        code = qc_ref[own, :]
        none = jnp.zeros_like(code)
        for c in range(pairs):
            logs, centres = [], []
            for h in (2 * c, 2 * c + 1):
                logs.append(jnp.where(jnp.logical_or(lane < CLIPS, within(lane, LOGS + 3 * h)), code, none))
                centres.append(jnp.where(within(lane, CENTRES + 3 * h), code, none))
            r_ref[c] = stacked_heads(q_ref[own, lanes_of(c)], logs)
            t_ref[c] = stacked_heads(g_ref[own, lanes_of(c)], centres)
        acc_ref[...] = jnp.zeros(acc_ref.shape, F32)

        def step(j, carry):
            code = kc_ref[tile_at(j), :]
            steps = []
            for c in range(pairs):
                probs = jnp.exp(dot_nt(beside(k_ref[tile_at(j), lanes_of(c)], code), r_ref[c]))
                d_probs = dot_nt(beside(v_ref[tile_at(j), lanes_of(c)], code), t_ref[c])
                steps.append((probs * d_probs).astype(BF))
            for c in range(pairs):
                acc_ref[c] += dot_tn(k_ref[tile_at(j), lanes_of(c)], steps[c])
            return carry

        lax.fori_loop(b_ref[0, i], b_ref[1, i], step, 0)
        for c in range(pairs):
            dq_ref[tile_at(i), lanes_of(c)] = (heads_out(acc_ref[c]) * HEAD_DIM**-0.5).astype(BF)
        return carry

    lax.fori_loop(0, tiles, one, 0)


def query_back(bounds, q, k, v, g, kc, qc, height):
    cols = k.shape[1]
    pairs = cols // 128
    scratch = [pltpu.VMEM((pairs, 2 * TILE, 256), BF)] * 2 + [pltpu.VMEM((pairs, 128, 2 * TILE), F32)]
    out_shape = jax.ShapeDtypeStruct((height, cols), BF)
    return local_call(query_back_kernel, "query_back", out_shape, scratch, bounds, q, k, v, g, kc, qc)


def key_back_kernel(b_ref, q_ref, k_ref, v_ref, g_ref, kc_ref, qc_ref, dk_ref, dv_ref, r_ref, t_ref, ak_ref, av_ref):
    height, cols = dk_ref.shape
    pairs, tiles = cols // 128, height // TILE
    lane = lax.broadcasted_iota(jnp.int32, (TILE, 128), 1)

    def one(i, carry):
        own = pl.ds(pl.multiple_of(REACH * height + i * TILE, TILE), TILE)
        code = kc_ref[own, :]
        none, ones = jnp.zeros_like(code), jnp.ones_like(code)
        for c in range(pairs):
            logs, centres = [], []
            for h in (2 * c, 2 * c + 1):
                logs.append(jnp.where(lane < CLIPS, code, jnp.where(within(lane, LOGS + 3 * h), ones, none)))
                centres.append(jnp.where(within(lane, CENTRES + 3 * h), ones, none))
            r_ref[c] = stacked_heads(k_ref[own, lanes_of(c)], logs)
            t_ref[c] = stacked_heads(v_ref[own, lanes_of(c)], centres)
        ak_ref[...] = jnp.zeros(ak_ref.shape, F32)
        av_ref[...] = jnp.zeros(av_ref.shape, F32)

        def step(j, carry):
            code = qc_ref[tile_at(j), :]
            weights, steps = [], []
            for c in range(pairs):
                probs = jnp.exp(dot_nt(beside(q_ref[tile_at(j), lanes_of(c)], code), r_ref[c]))
                d_probs = dot_nt(beside(g_ref[tile_at(j), lanes_of(c)], code), t_ref[c])
                weights.append(probs.astype(BF))
                steps.append((probs * d_probs).astype(BF))
            for c in range(pairs):
                av_ref[c] += dot_tn(g_ref[tile_at(j), lanes_of(c)], weights[c])
                ak_ref[c] += dot_tn(q_ref[tile_at(j), lanes_of(c)], steps[c])
            return carry

        lax.fori_loop(b_ref[0, i], b_ref[1, i], step, 0)
        for c in range(pairs):
            dk_ref[tile_at(i), lanes_of(c)] = heads_out(ak_ref[c]).astype(BF)
            dv_ref[tile_at(i), lanes_of(c)] = heads_out(av_ref[c]).astype(BF)
        return carry

    lax.fori_loop(0, tiles, one, 0)


def key_back(bounds, q, k, v, g, kc, qc, height):
    cols = k.shape[1]
    pairs = cols // 128
    scratch = [pltpu.VMEM((pairs, 2 * TILE, 256), BF)] * 2 + [pltpu.VMEM((pairs, 128, 2 * TILE), F32)] * 2
    out_shape = (jax.ShapeDtypeStruct((height, cols), BF),) * 2
    return local_call(key_back_kernel, "key_back", out_shape, scratch, bounds, q, k, v, g, kc, qc)


class Ring:
    def __init__(self):
        d = lax.axis_index("dp")
        n = lax.axis_size("dp") // 2
        chip = d // 2
        core = d - 2 * chip
        odd = chip - 2 * (chip // 2)
        spot = (1 - odd) * (chip // 2) + odd * (n - 1 - chip // 2)
        self.here = (1 - core) * spot + core * (n - 1 - spot)
        self.n, self.core = n, core
        self.sibling = {"dp": d + 1 - 2 * core}
        self.after = {"dp": self.device_at(self.wrap(self.here + 1))}
        self.before = {"dp": self.device_at(self.wrap(self.here - 1))}

    def wrap(self, index):
        return lax.rem(index + 2 * self.n, self.n)

    def device_at(self, rank):
        n, core = self.n, self.core
        walk = (1 - core) * rank + core * (n - 1 - rank)
        late = walk // (n // 2)
        return 2 * ((1 - late) * (2 * walk) + late * (2 * (n - walk) - 1)) + core

    def spans(self, shape, i, owner, j):
        rows, cols = shape[0] // 2, shape[1]
        wide = STRIPS * STRIP
        high, count = rows * cols // (self.n * wide), cols // wide
        line = j // count
        row = pl.multiple_of(owner * rows + line * high, high)
        col = pl.multiple_of((j - line * count) * wide + i * STRIP, STRIP)
        return pl.ds(row, high), pl.ds(col, STRIP)


def units(arrays):
    return [(a, i, pl.ds(i * STRIP, STRIP), a * STRIPS + i) for a in range(arrays) for i in range(STRIPS)]


class Reduce:
    def __init__(self, ring, given, sibs, bufs, sems):
        self.ring, self.given, self.sibs, self.bufs, self.sems = ring, given, sibs, bufs, sems
        self.units = units(len(given))

    def s_copy(self, a):
        rows = self.given[a].shape[0] // 2
        span = pl.ds(pl.multiple_of((1 - self.ring.core) * rows, rows), rows)
        return remote(
            self.given[a].at[span], self.sibs[a], self.sems[0].at[a], self.sems[1].at[a], self.ring.sibling
        )

    def r_copy(self, u, s):
        a, _, strip, e = u
        src, dst = self.bufs[a].at[s, :, strip], self.bufs[a].at[s + 1, :, strip]
        return remote(src, dst, self.sems[2].at[e, s], self.sems[3].at[e, s], self.ring.after)

    def terms(self, u, j):
        a, i, _, _ = u
        shape, core = self.given[a].shape, self.ring.core
        mine = self.given[a][self.ring.spans(shape, i, core, j)].astype(F32)
        return mine + self.sibs[a][self.ring.spans(shape, i, 0, j)].astype(F32)

    def swap(self, a):
        self.s_copy(a).start()

    def first(self, a):
        self.s_copy(a).wait_recv()
        for u in self.units:
            if u[0] == a:
                self.bufs[a][0, :, u[2]] = self.terms(u, self.ring.here).astype(BF)
                self.r_copy(u, 0).start()

    def step(self, s, onward=True):
        for u in self.units:
            a, _, strip, _ = u
            local = self.terms(u, self.ring.wrap(self.ring.here - s))
            self.r_copy(u, s - 1).wait_recv()
            self.bufs[a][s, :, strip] = (self.bufs[a][s, :, strip].astype(F32) + local).astype(BF)
            if onward:
                self.r_copy(u, s).start()

    def turn(self):
        self.step(self.ring.n - 1, False)

    def settle(self):
        for a in range(len(self.given)):
            self.s_copy(a).wait_send()

        def step(s, carry):
            for u in self.units:
                self.r_copy(u, s).wait_send()
            return carry

        lax.fori_loop(0, self.ring.n - 1, step, 0)


class Gather:
    def __init__(self, ring, outs, sems):
        self.ring, self.outs, self.sems = ring, outs, sems
        self.units = units(len(outs))

    def spot(self, u, s):
        out, ring = self.outs[u[0]], self.ring
        return out.at[ring.spans(out.shape, u[1], ring.core, ring.wrap(ring.here + 1 - s))]

    def g_copy(self, u, s):
        spot, e = self.spot(u, s), u[3]
        return remote(spot, spot, self.sems[0].at[e, s], self.sems[1].at[e, s], self.ring.after)

    def c_copy(self, u, s):
        spot, e = self.spot(u, s), u[3]
        return remote(spot, spot, self.sems[2].at[e, s], self.sems[3].at[e, s], self.ring.sibling)

    def begin(self, sources):
        for u in self.units:
            a, _, strip, _ = u
            self.spot(u, 0)[...] = sources[a][:, strip]
            self.g_copy(u, 0).start()
            self.c_copy(u, 0).start()

    def step(self, s):
        for u in self.units:
            self.g_copy(u, s - 1).wait_recv()
            self.g_copy(u, s).start()
            self.c_copy(u, s).start()

    def last(self):
        n = self.ring.n
        for u in self.units:
            self.g_copy(u, n - 2).wait_recv()
            self.c_copy(u, n - 1).start()

    def settle(self):
        n = self.ring.n
        for u in self.units:
            self.c_copy(u, n - 1).wait()

        def step(s, carry):
            for u in self.units:
                self.g_copy(u, s).wait_send()
                self.c_copy(u, s).wait()
            return carry

        lax.fori_loop(0, n - 1, step, 0)


def between(step, begin, end, count):
    def body(s, carry):
        step(s)
        return carry

    if begin + count < end:
        lax.fori_loop(begin + count, end, body, 0)


def chunk_rows(shape, n):
    return shape[0] * shape[1] // (2 * n * STRIPS * STRIP)


def reduce_scratch(shapes, n):
    count = len(shapes)
    sibs = [pltpu.VMEM((rows // 2, cols), BF) for rows, cols in shapes]
    bufs = [pltpu.VMEM((n, chunk_rows(shape, n), STRIPS * STRIP), BF) for shape in shapes]
    return sibs + bufs, [DMA((count,))] * 2 + [DMA((count * STRIPS, n - 1))] * 2


def gather_sems(count, n):
    return [DMA((count * STRIPS, n - 1))] * 2 + [DMA((count * STRIPS, n))] * 2


def norm_back_rows(grad, values, gain):
    middle = jnp.mean(values, axis=-1, keepdims=True)
    centred = values - middle
    inverse = lax.rsqrt(jnp.mean(centred * centred, axis=-1, keepdims=True) + 1e-05)
    n = centred * inverse
    t = grad * gain
    back = (t - jnp.mean(t, axis=-1, keepdims=True) - n * jnp.mean(t * n, axis=-1, keepdims=True)) * inverse
    return back, grad * n


def column_sums(values):
    return jnp.sum(values, axis=0, keepdims=True)


def mid_kernel(
    x_ref, cot_ref, mix_ref, lse_ref, kc_ref, wof_ref, ob_ref, gain_ref, shift_ref, w1_ref, b1_ref, w2_ref,
    xw_ref, qc_ref, rg_ref, low_ref, vec_ref, own1_ref, own2_ref, res_ref, outp_ref,
    om_ref, dact_ref, mi_ref, act_ref, pg_ref, part_ref, oth_ref, f1_ref, f2_ref, st_ref, sw_ref,
    sib1, sib2, buf1, buf2,
    sm, rm, sy, ry, sx, rx, ss, rs, sf, rf, *ring_sems,
):
    d, core, has_left, has_right = place()
    t = lax.axis_index("tensor")
    height, cols = mix_ref.shape
    width, hidden = w1_ref.shape
    rows = height // PARTS
    sibling = {"dp": d + 1 - 2 * core}
    across = {"tensor": 1 - t}
    exists = (has_left, has_right)
    slots = (0, 2 * REACH)
    ring = Ring()
    reduce = Reduce(ring, (f1_ref, f2_ref), (sib1, sib2), (buf1, buf2), ring_sems)
    n = ring.n
    greet([
        (None, sibling), (None, across), (has_left, {"dp": d - 2}), (has_right, {"dp": d + 2}),
        (None, ring.after), (None, ring.before),
    ])

    def span(p):
        return pl.ds(pl.multiple_of(p * rows, rows), rows)

    def m_copy(p):
        return remote(mix_ref.at[span(p)], om_ref.at[span(p)], sm.at[p], rm.at[p], across)

    def y_copy(p):
        return remote(part_ref.at[span(p)], oth_ref.at[span(p)], sy.at[p], ry.at[p], across)

    def refs(p):
        if p == PARTS:
            return st_ref, lambda slot: sw_ref.at[slot]
        return xw_ref.at[REACH, span(p)], lambda slot: xw_ref.at[slot, span(p)]

    def x_copy(side, p):
        src, dst = refs(p)
        return remote(
            src, dst(slots[side]), sx.at[side, p], rx.at[side, p],
            {"dp": d + 2 if side == 0 else d - 2},
        )

    def s_copy(p):
        src, dst = refs(p)
        return remote(src, dst(1 + 2 * core), ss.at[p], rs.at[p], sibling)

    def f_copy(p):
        _, dst = refs(p)
        return remote(dst(4 - 4 * core), dst(3 - 2 * core), sf.at[p], rf.at[p], sibling)

    def send(p):
        for side in (0, 1):

            @pl.when(exists[1 - side])
            def _():
                x_copy(side, p).start()

        s_copy(p).start()

    def pass_on(p):
        for side in (0, 1):

            @pl.when(exists[side])
            def _():
                x_copy(side, p).wait_recv()

            @pl.when(jnp.logical_and(exists[side], core == 1 - side))
            def _():
                f_copy(p).start()

    for p in range(PARTS):
        m_copy(p).start()
    gain, shift = gain_ref[...].astype(F32), shift_ref[...].astype(F32)
    out_bias, fc1_bias = ob_ref[...].astype(F32), b1_ref[...].astype(F32)
    heads = pl.ds(pl.multiple_of(t * cols, cols), cols)
    others = pl.ds(pl.multiple_of((1 - t) * cols, cols), cols)
    picks = lax.broadcasted_iota(jnp.int32, (8, cols), 1) // HEAD_DIM
    picks = (picks == lax.broadcasted_iota(jnp.int32, (8, cols), 0)).astype(F32)
    st_ref[0:8, :] = lse_ref[...]
    vec_ref[...] = jnp.zeros(vec_ref.shape, F32)

    def early(p, carry):
        cot = cot_ref[span(p), :]
        dact_ref[span(p), :] = dot_nt(cot, w2_ref[...])
        vec_ref[3:4, :] += column_sums(cot.astype(F32))
        res_ref[span(p), :] = x_ref[span(p), :].astype(F32) + dot_nn(mix_ref[span(p), :], wof_ref[heads, :]) + out_bias
        return carry

    lax.fori_loop(0, PARTS, early, 0)

    def forward(p, carry):
        m_copy(p).wait_recv()
        residual = res_ref[span(p), :] + dot_nn(om_ref[span(p), :], wof_ref[others, :])
        res_ref[span(p), :] = residual
        mlp_input = (norm_rows(residual) * gain + shift).astype(BF)
        mi_ref[span(p), :] = mlp_input
        for i in range(hidden // width):
            part = slice(i * width, (i + 1) * width)
            preact = dot_nn(mlp_input, w1_ref[:, part]) + fc1_bias[:, part]
            cdf = 0.5 * (1.0 + lax.erf(preact * (2.0**-0.5)))
            pdf = jnp.exp(-0.5 * preact * preact) * 0.3989422804014327
            act_ref[span(p), part] = (preact * cdf).astype(BF)
            pre_grad = (dact_ref[span(p), part] * (cdf + preact * pdf)).astype(BF)
            pg_ref[span(p), part] = pre_grad
            vec_ref[4 + i : 5 + i, :] += column_sums(pre_grad.astype(F32))
        part_ref[span(p), :] = dot_nt(pg_ref[span(p), :], w1_ref[...]).astype(BF)
        y_copy(p).start()
        return carry

    lax.fori_loop(0, PARTS, forward, 0)

    def weights(which):
        half = pl.ds(pl.multiple_of(which * (width // 2), width // 2), width // 2)
        f1_ref[half, :] = dot_tn(mi_ref[:, half], pg_ref[...]).astype(BF)
        half = pl.ds(pl.multiple_of(which * (hidden // 2), hidden // 2), hidden // 2)
        f2_ref[half, :] = dot_tn(act_ref[:, half], cot_ref[...]).astype(BF)

    weights(1 - core)
    reduce.swap(0)
    reduce.swap(1)
    weights(core)

    def back(p):
        y_copy(p).wait_recv()
        grad = part_ref[span(p), :].astype(F32) + oth_ref[span(p), :].astype(F32)
        turned, scaled = norm_back_rows(grad, res_ref[span(p), :], gain)
        total = cot_ref[span(p), :].astype(F32) + turned
        low = total.astype(BF)
        rg_ref[span(p), :] = total
        low_ref[span(p), :] = low
        vec_ref[0:1, :] += column_sums(scaled)
        vec_ref[1:2, :] += column_sums(grad)
        vec_ref[2:3, :] += column_sums(low.astype(F32))
        mixed_grad = dot_nt(low, wof_ref[heads, :]).astype(BF)
        xw_ref[REACH, span(p), :] = mixed_grad
        product = mixed_grad.astype(F32) * mix_ref[span(p), :].astype(F32)
        st_ref[8:16, p * rows : (p + 1) * rows] = lax.dot_general(
            picks, product, (((1,), (1,)), ((), ())),
            precision=lax.Precision.HIGHEST, preferred_element_type=F32,
        )

    def code(slot):
        def step(i, carry):
            spot = pl.ds(pl.multiple_of(slot * height + i * TILE, TILE), TILE)
            stats = sw_ref[slot, :, pl.ds(pl.multiple_of(i * TILE, TILE), TILE)]
            qc_ref[spot, :] = code_tile(stats, kc_ref[spot, :])
            return carry

        lax.fori_loop(0, height // TILE, step, 0)

    def ring_step(s):
        if s < n - 1:
            reduce.step(s)

    reduce.first(0)
    reduce.first(1)
    for p in range(PARTS):
        back(p)
        ring_step(1 + p)
        send(p)
    send(PARTS)
    sw_ref[REACH] = st_ref[...]
    for p in range(PARTS):
        ring_step(1 + PARTS + p)
        pass_on(p)
        if p == 0:
            outp_ref[...] = dot_nn(act_ref[...], w2_ref[...]).astype(BF)
    pass_on(PARTS)
    between(reduce.step, 1, n - 1, 2 * PARTS)
    code(REACH)
    reduce.turn()
    own1_ref[...] = buf1[n - 1]
    own2_ref[...] = buf2[n - 1]
    for p in range(PARTS + 1):
        s_copy(p).wait()
        for side in (0, 1):

            @pl.when(exists[1 - side])
            def _():
                x_copy(side, p).wait_send()

            @pl.when(jnp.logical_and(exists[side], core == 1 - side))
            def _():
                f_copy(p).wait_send()

            @pl.when(jnp.logical_and(exists[side], core == side))
            def _():
                f_copy(p).wait_recv()

    code(3 - 2 * core)
    for side in (0, 1):

        @pl.when(exists[side])
        def _():
            code(slots[side])

        @pl.when(jnp.logical_and(exists[side], core == side))
        def _():
            code(1 + 2 * core)

    for p in range(PARTS):
        m_copy(p).wait_send()
        y_copy(p).wait_send()
    reduce.settle()


def mid(x, cot, mix, lse, kc, wof, out_bias, gain, shift, w1, b1, w2):
    blocks = 2 * REACH + 1
    height, width = x.shape
    hidden = w1.shape[1]
    n = lax.axis_size("dp") // 2
    pair, line, some = DMA((2, PARTS + 1)), DMA((PARTS + 1,)), DMA((PARTS,))
    room, sems = reduce_scratch((w1.shape, w2.shape), n)
    shape = jax.ShapeDtypeStruct
    chunks = [shape((chunk_rows(w.shape, n), STRIPS * STRIP), BF) for w in (w1, w2)]
    return pl.pallas_call(
        mid_kernel,
        out_shape=(
            shape((blocks,) + mix.shape, BF), shape(kc.shape, BF), shape(x.shape, F32), shape(x.shape, BF),
            shape((16, width), F32), *chunks, shape(x.shape, F32), shape(x.shape, BF),
        ),
        in_specs=[whole()] * 12,
        out_specs=[whole()] * 9,
        scratch_shapes=[
            pltpu.VMEM(mix.shape, BF), pltpu.VMEM((height, hidden), F32), pltpu.VMEM(x.shape, BF),
            pltpu.VMEM((height, hidden), BF), pltpu.VMEM((height, hidden), BF), pltpu.VMEM(x.shape, BF),
            pltpu.VMEM(x.shape, BF), pltpu.VMEM(w1.shape, BF), pltpu.VMEM(w2.shape, BF),
            pltpu.VMEM((16, height), F32), pltpu.VMEM((blocks, 16, height), F32),
        ]
        + room
        + [some, some, some, some, pair, pair, line, line, line, line]
        + sems,
        compiler_params=pltpu.CompilerParams(
            collective_id=1, has_side_effects=True, vmem_limit_bytes=MID_BYTES
        ),
        name="mid",
    )(x, cot, mix, lse, kc, wof, out_bias, gain, shift, w1, b1, w2)


def finish_kernel(
    rounds, dq_ref, dk_ref, dv_ref, wq_ref, wk_ref, wv_ref, a_ref, low_ref, o_ref, x_ref, rg_ref, gain_ref, vec_ref,
    own1_ref, own2_ref,
    ig_ref, g_ref, vs_ref, g1_ref, g2_ref,
    part_ref, oth_ref, own_ref, send_ref, got_ref, sib, buf, sy, ry, sd, rd, *ring_sems,
):
    d, core, _, _ = place()
    t = lax.axis_index("tensor")
    height, cols = dq_ref.shape
    width = x_ref.shape[1]
    piece = height // PIECES
    across = {"tensor": 1 - t}
    ring = Ring()
    reduce = Reduce(ring, (own_ref,), (sib,), (buf,), ring_sems[:4])
    gather = Gather(ring, (g_ref,), ring_sems[4:8])
    wide = Gather(ring, (g1_ref, g2_ref), ring_sems[8:])
    n = ring.n
    partners = []
    for r in range(rounds):
        bit = (d // 2**r) - 2 * (d // 2 ** (r + 1))
        partners.append({"dp": d + 2**r * (1 - 2 * bit)})
    greet([(None, across), (None, ring.after), (None, ring.before)] + [(None, p) for p in partners])

    def y_copy(p):
        span = pl.ds(p * piece, piece)
        return remote(part_ref.at[span], oth_ref.at[span], sy.at[p], ry.at[p], across)

    def d_copy(r):
        return remote(send_ref.at[r], got_ref.at[r], sd.at[r], rd.at[r], partners[r])

    def share(p):
        span = pl.ds(p * piece, piece)
        part = dot_nt(dq_ref[span, :], wq_ref[...]) + dot_nt(dk_ref[span, :], wk_ref[...])
        part_ref[span, :] = (part + dot_nt(dv_ref[span, :], wv_ref[...])).astype(BF)

    def weights(which):
        span = pl.ds(pl.multiple_of(which * (width // 2), width // 2), width // 2)
        attn = a_ref[:, span]
        for i, ref in enumerate((dq_ref, dk_ref, dv_ref)):
            own_ref[span, i * cols : (i + 1) * cols] = dot_tn(attn, ref[...]).astype(BF)
        own_ref[span, 3 * cols : 4 * cols] = dot_tn(low_ref[:, span], o_ref[...]).astype(BF)

    def wide_step(s):
        if s < n - 1:
            wide.step(s)

    for p in range(AHEAD):
        share(p)
        y_copy(p).start()
    wide.begin((own1_ref, own2_ref))
    weights(1 - core)
    reduce.swap(0)
    for p in range(AHEAD, PIECES):
        share(p)
    wide_step(1)
    weights(core)
    gain = gain_ref[...].astype(F32)
    gains, shifts = [], []

    def back(p):
        span = pl.ds(p * piece, piece)
        y_copy(p).wait_recv()
        if p + AHEAD < PIECES:
            y_copy(p + AHEAD).start()
        grad = part_ref[span, :].astype(F32) + oth_ref[span, :].astype(F32)
        turned, scaled = norm_back_rows(grad, x_ref[span, :].astype(F32), gain)
        ig_ref[span, :] = rg_ref[span, :] + turned
        gains.append(column_sums(scaled))
        shifts.append(column_sums(grad))

    reduce.first(0)
    wide_step(2)
    for p in range(PIECES):
        back(p)
        if 1 + p < n - 1:
            reduce.step(1 + p)
        wide_step(3 + p)
    between(reduce.step, 1, n - 1, PIECES)
    between(wide.step, 1, n - 1, PIECES + 2)
    wide.last()
    send_ref[0] = vec_ref[...]
    send_ref[0, 6:7, 0:cols] = column_sums(dq_ref[...].astype(F32))
    send_ref[0, 6:7, cols : 2 * cols] = column_sums(dv_ref[...].astype(F32))
    send_ref[0, 7:8, :] = sum(gains[1:], gains[0])
    send_ref[0, 8:9, :] = sum(shifts[1:], shifts[0])
    reduce.turn()
    gather.begin((buf.at[n - 1],))
    d_copy(0).start()
    for s in range(max(rounds, PIECES)):
        if s < rounds:
            d_copy(s).wait_recv()
            total = send_ref[s] + got_ref[s]
            if s + 1 < rounds:
                send_ref[s + 1] = total
                d_copy(s + 1).start()
            else:
                vs_ref[...] = total
        if s < PIECES and 1 + s < n - 1:
            gather.step(1 + s)
    between(gather.step, 1, n - 1, PIECES)
    gather.last()
    for p in range(PIECES):
        y_copy(p).wait_send()
    for r in range(rounds):
        d_copy(r).wait_send()
    reduce.settle()
    wide.settle()
    gather.settle()


def finish(dq, dk, dv, wq, wk, wv, attn, low, o, x, rg, gain, vectors, own1, own2, shapes):
    height, cols = dq.shape
    width = x.shape[1]
    size = lax.axis_size("dp")
    rounds = size.bit_length() - 1
    n = size // 2
    weights = (width, 4 * cols)
    room, sems = reduce_scratch((weights,), n)
    shape = jax.ShapeDtypeStruct
    return pl.pallas_call(
        functools.partial(finish_kernel, rounds),
        out_shape=(
            shape((height, width), F32), shape(weights, BF), shape(vectors.shape, F32),
            *[shape(dims, BF) for dims in shapes],
        ),
        in_specs=[whole()] * 15,
        out_specs=[whole()] * 5,
        scratch_shapes=[
            pltpu.VMEM((height, width), BF), pltpu.VMEM((height, width), BF), pltpu.VMEM(weights, BF),
            pltpu.VMEM((rounds,) + vectors.shape, F32), pltpu.VMEM((rounds,) + vectors.shape, F32),
        ]
        + room
        + [DMA((PIECES,)), DMA((PIECES,)), DMA((rounds,)), DMA((rounds,))]
        + sems
        + gather_sems(1, n)
        + gather_sems(2, n),
        compiler_params=pltpu.CompilerParams(
            collective_id=2, has_side_effects=True, vmem_limit_bytes=FINISH_BYTES
        ),
        name="finish",
    )(dq, dk, dv, wq, wk, wv, attn, low, o, x, rg, gain, vectors, own1, own2)


def swapped(value):
    return lax.ppermute(value, "tensor", [(0, 1), (1, 0)])


def on_device(
    inputs, clip_ids, attn_gain, attn_shift, w_query, query_bias, w_key, w_value, value_bias,
    w_out, out_bias, mlp_gain, mlp_shift, w_fc1, fc1_bias, w_fc2, fc2_bias, cotangent,
):
    height, width = inputs.shape
    d = lax.axis_index("dp")
    reach = REACH * height

    padded = jnp.pad(clip_ids, (reach, reach), constant_values=-1)
    window = lax.dynamic_slice_in_dim(padded, d * height, height + 2 * reach)
    own = lax.dynamic_slice_in_dim(clip_ids, d * height, height)
    firsts, lasts = own[::TILE], own[TILE - 1 :: TILE]
    origin = d * height - reach
    begin = jnp.sum((clip_ids[None, :] < firsts[:, None]).astype(jnp.int32), axis=1) - origin
    end = jnp.sum((clip_ids[None, :] <= lasts[:, None]).astype(jnp.int32), axis=1) - origin
    bounds = jnp.stack([begin // TILE, (end + TILE - 1) // TILE])
    lane = jnp.arange(128, dtype=jnp.int32)[None, :]
    clip_far = jnp.where(window[:, None] == lane, 0.0, FAR)
    key_code = jnp.where(lane < CLIPS, clip_far, 1.0).astype(BF)

    row = lambda v: v[None, :]
    q, k, v, attn_input, w_out_full, norms = halo_qkv(
        inputs, w_out, row(attn_gain), row(attn_shift), w_query, w_key, w_value,
        row(query_bias), row(value_bias),
    )
    mixed, logs = attend(bounds, q, k, v, key_code, norms, height)
    grad_win, query_code, residual_grad, low, vectors, own1, own2, residual, out_part = mid(
        inputs, cotangent, mixed, logs, key_code, w_out_full, row(out_bias), row(mlp_gain), row(mlp_shift),
        w_fc1, row(fc1_bias), w_fc2,
    )
    grad_win = grad_win.reshape(-1, grad_win.shape[2])
    out_part, query_code = lax.optimization_barrier((out_part, query_code))
    out_other = swapped(out_part)
    query_low = query_back(bounds, q, k, v, grad_win, key_code, query_code, height)
    key_low, value_low = key_back(bounds, q, k, v, grad_win, key_code, query_code, height)
    out_other, key_low = lax.optimization_barrier((out_other, key_low))
    layer_out = (
        residual + (out_part.astype(F32) + out_other.astype(F32)) + fc2_bias.astype(F32)
    ).astype(BF)
    inputs_grad, attn_sum, sums, fc1_sum, fc2_sum = finish(
        query_low, key_low, value_low, w_query, w_key, w_value, attn_input, low, mixed, inputs,
        residual_grad, row(attn_gain), vectors, own1, own2, (w_fc1.shape, w_fc2.shape),
    )
    cols = w_query.shape[1]
    pieces = [attn_sum[:, i * cols : (i + 1) * cols].astype(F32) for i in range(4)]
    return (
        layer_out, inputs_grad, sums[7], sums[8],
        pieces[0], sums[6, :cols], pieces[1], pieces[2], sums[6, cols:],
        pieces[3].T, sums[2], sums[0], sums[1],
        fc1_sum.astype(F32), sums[4:6].reshape(-1), fc2_sum.astype(F32), sums[3],
    )


def solution(mesh):
    rows, cols, split, every = P("dp", None), P(None, "tensor"), P("tensor"), P()
    tall = P("tensor", None)
    in_specs = (
        rows, every, every, every, cols, split, cols, cols, split, tall, every, every, every,
        cols, split, tall, every, rows,
    )
    out_specs = (
        rows, rows, every, every, cols, split, cols, cols, split, tall, every, every, every,
        cols, split, tall, every,
    )
    return jax.shard_map(on_device, mesh=mesh, in_specs=in_specs, out_specs=out_specs, check_vma=False)
```

```python
import functools

import jax
import jax.numpy as jnp
from jax import lax
from jax.experimental import pallas as pl
from jax.experimental.pallas import tpu as pltpu
from jax.sharding import PartitionSpec as P

HEAD_DIM = 64
REACH = 2
TILE = 256
PIECES = 6
AHEAD = 2
NEG = -3e38
CLIPS = 64
LOGS = 64
CENTRES = 96
FAR = -(2.0**100)
SAFE = 40.0
BF = jnp.bfloat16
F32 = jnp.float32
MESH = pl.DeviceIdType.MESH
VMEM = pltpu.VMEM
VMEM_BYTES = 26_000_000
MID_BYTES = 50_000_000
FINISH_BYTES = 38_000_000
PARTS = 3
STRIP = 128
STRIPS = 3
DMA = pltpu.SemaphoreType.DMA


def dot_nn(left, right):
    return jnp.dot(left, right, preferred_element_type=F32)


def dot_tn(left, right):
    return lax.dot_general(left, right, (((0,), (0,)), ((), ())), preferred_element_type=F32)


def dot_nt(left, right):
    return lax.dot_general(left, right, (((1,), (1,)), ((), ())), preferred_element_type=F32)


def whole():
    return pl.BlockSpec(memory_space=VMEM)


def far():
    return pl.BlockSpec(memory_space=pltpu.HBM)


def in_hbm(value):
    return pltpu.with_memory_space_constraint(value, pltpu.HBM)


def remote(src, dst, send_sem, recv_sem, device):
    return pltpu.make_async_remote_copy(
        src_ref=src,
        dst_ref=dst,
        send_sem=send_sem,
        recv_sem=recv_sem,
        device_id=device,
        device_id_type=MESH,
    )


def place():
    d = lax.axis_index("dp")
    chip = d // 2
    core = d - 2 * chip
    has_left = chip > 0
    has_right = chip < lax.axis_size("dp") // 2 - 1
    return d, core, has_left, has_right


def greet(targets):
    barrier = pltpu.get_barrier_semaphore()
    count = 0
    for present, device in targets:
        if present is None:
            pl.semaphore_signal(barrier, inc=1, device_id=device, device_id_type=MESH)
            count = count + 1
        else:

            @pl.when(present)
            def _():
                pl.semaphore_signal(barrier, inc=1, device_id=device, device_id_type=MESH)

            count = count + present.astype(jnp.int32)
    pl.semaphore_wait(barrier, count)


def norm_rows(values):
    middle = jnp.mean(values, axis=-1, keepdims=True)
    centred = values - middle
    spread = jnp.mean(centred * centred, axis=-1, keepdims=True)
    return centred * lax.rsqrt(spread + 1e-05)


def halo_kernel(
    x_ref, wo_ref, wq_ref, wk_ref, wv_ref, vec_ref, lab_ref,
    q_ref, k_ref, v_ref, a_ref, wof_ref, n_ref, kc_ref,
    win, wq, wk, wv, load, sx, rx, sy, ry, ss, rs, sf, rf, sw, rw, sv, rv,
):
    d, core, has_left, has_right = place()
    t = lax.axis_index("tensor")
    height = x_ref.shape[0]
    cols = wq_ref.shape[1]
    half = height // 2
    piece = half // PIECES
    sibling = {"dp": d + 1 - 2 * core}
    across = {"tensor": 1 - t}
    exists = (has_left, has_right)
    slots = (0, 2 * REACH)
    part = wo_ref.shape[0] // 2
    wo_rows = pl.ds(pl.multiple_of(core * part, part), part)
    mine = pl.ds(pl.multiple_of(t * 2 * part, part), 2 * part)
    loads = [
        pltpu.make_async_copy(src, dst, load.at[i])
        for i, (src, dst) in enumerate(
            ((x_ref, win.at[REACH]), (wq_ref, wq), (wk_ref, wk), (wv_ref, wv), (wo_ref, wof_ref.at[mine]))
        )
    ]
    for copy in loads:
        copy.start()
    greet([(None, sibling), (None, across), (has_left, {"dp": d - 2}), (has_right, {"dp": d + 2})])

    def rows(which, p):
        return pl.ds(pl.multiple_of(which * half + p * piece, piece), piece)

    def x_copy(side, p):
        return remote(
            x_ref.at[rows(t, p)], win.at[slots[side], rows(t, p)], sx.at[side, p], rx.at[side, p],
            {"dp": d + 2 if side == 0 else d - 2},
        )

    def y_copy(side, p):
        spot = win.at[slots[side], rows(t, p)]
        return remote(spot, spot, sy.at[side, p], ry.at[side, p], across)

    def f_copy(which, p):
        span = rows(t if which == 0 else 1 - t, p)
        return remote(
            win.at[4 - 4 * core, span], win.at[3 - 2 * core, span], sf.at[which, p], rf.at[which, p],
            sibling,
        )

    own_copy = remote(x_ref, win.at[1 + 2 * core], ss, rs, sibling)

    def full_rows(which):
        return pl.ds(pl.multiple_of((2 * which + core) * part, part), part)

    w_copy = remote(wo_ref.at[wo_rows], wof_ref.at[full_rows(t)], sw, rw, across)
    wf_copy = remote(wof_ref.at[full_rows(1 - t)], wof_ref.at[full_rows(1 - t)], sv, rv, sibling)

    def send(p):
        for side in (0, 1):

            @pl.when(exists[1 - side])
            def _():
                x_copy(side, p).start()

    for p in range(AHEAD):
        send(p)
    w_copy.start()
    own_copy.start()
    vec = vec_ref[...].astype(F32)
    gain, shift = vec[0:1], vec[1:2]
    query_bias, value_bias = vec[2:3, :cols], vec[2:3, cols:]
    n_ref[...] = jnp.zeros(n_ref.shape, F32)

    def code(r, carry):
        labels = jnp.transpose(jnp.broadcast_to(lab_ref[pl.ds(r, 1), :], (128, 128)))
        lane = lax.broadcasted_iota(jnp.int32, (128, 128), 1)
        far = jnp.where(labels == lane.astype(F32), 0.0, FAR)
        kc_ref[pl.ds(pl.multiple_of(r * 128, 128), 128), :] = jnp.where(lane < CLIPS, far, 1.0).astype(BF)
        return carry

    lax.fori_loop(0, lab_ref.shape[0], code, 0)

    def raise_norm(spot, values):
        for c in range(cols // 128):
            span = values[:, c * 128 : c * 128 + 128]
            norm = jnp.max(jnp.sum(span * span, axis=1, keepdims=True), axis=0, keepdims=True)
            n_ref[spot, :] = jnp.maximum(n_ref[spot, :], norm)

    def project(slot, start):
        spot = pl.ds(pl.multiple_of(start, half), half)
        attn = (norm_rows(win[slot, spot, :].astype(F32)) * gain + shift).astype(BF)
        out = pl.ds(pl.multiple_of(slot * height + start, half), half)

        @pl.when(slot == REACH)
        def _():
            a_ref[spot, :] = attn

        query = (dot_nn(attn, wq[...]) + query_bias) * HEAD_DIM**-0.5
        key = dot_nn(attn, wk[...])
        q_ref[out, :] = query.astype(BF)
        k_ref[out, :] = key.astype(BF)
        raise_norm(slice(0, 8), query)
        raise_norm(slice(8, 16), key)
        v_ref[out, :] = (dot_nn(attn, wv[...]) + value_bias).astype(BF)

    def pass_on(p):
        for side in (0, 1):

            @pl.when(exists[side])
            def _():
                x_copy(side, p).wait_recv()
                y_copy(side, p).start()

            @pl.when(jnp.logical_and(exists[side], core == 1 - side))
            def _():
                f_copy(0, p).start()

        if p + AHEAD < PIECES:
            send(p + AHEAD)

    for copy in loads:
        copy.wait()

    def half_block(i, carry):
        @pl.when(i == 2)
        def _():
            pass_on(0)
            w_copy.wait_recv()
            wf_copy.start()
            for p in range(1, PIECES // 2):
                pass_on(p)
            own_copy.wait_recv()

        @pl.when(i == 4)
        def _():
            for p in range(PIECES // 2, PIECES):
                pass_on(p)

        @pl.when(i == 6)
        def _():
            for p in range(PIECES):
                for side in (0, 1):

                    @pl.when(exists[side])
                    def _():
                        y_copy(side, p).wait_recv()

                    @pl.when(jnp.logical_and(exists[side], core == 1 - side))
                    def _():
                        f_copy(1, p).start()

        @pl.when(i == 8)
        def _():
            for side in (0, 1):

                @pl.when(jnp.logical_and(exists[side], core == side))
                def _():
                    for which in (0, 1):
                        for p in range(PIECES):
                            f_copy(which, p).wait_recv()

        stage = i // 2
        odd = i - 2 * stage
        left, right = has_left.astype(jnp.int32), has_right.astype(jnp.int32)
        near = (1 - core) * left + core * right
        outer = (1 - odd) * left + odd * right

        def pick(values):
            total = 0
            for index, value in enumerate(values):
                total = total + (stage == index).astype(jnp.int32) * value
            return total

        slot = pick((REACH, 3 - 2 * core, 4 * odd, 4 * odd, 1 + 2 * core))
        which = pick((odd, odd, t, 1 - t, odd))

        @pl.when(pick((1, 1, outer, outer, near)) == 1)
        def _():
            project(slot, which * half)

        return carry

    lax.fori_loop(0, 10, half_block, 0)
    wf_copy.wait_recv()
    for copy in (own_copy, w_copy, wf_copy):
        copy.wait_send()
    for p in range(PIECES):
        for side in (0, 1):

            @pl.when(exists[1 - side])
            def _():
                x_copy(side, p).wait_send()

            @pl.when(exists[side])
            def _():
                y_copy(side, p).wait_send()

            @pl.when(jnp.logical_and(exists[side], core == 1 - side))
            def _():
                f_copy(0, p).wait_send()
                f_copy(1, p).wait_send()


def halo_qkv(x, wo, wq, wk, wv, vec, labels):
    height, width = x.shape
    cols = wq.shape[1]
    blocks = 2 * REACH + 1
    shape = jax.ShapeDtypeStruct
    wide = shape((blocks * height, cols), BF)
    pair = DMA((2, PIECES))
    return pl.pallas_call(
        halo_kernel,
        out_shape=(
            wide, wide, wide, shape((height, width), BF), shape((2 * wo.shape[0], wo.shape[1]), BF),
            shape((16, 128), F32), shape((blocks * height, 128), BF),
        ),
        in_specs=[far()] * 5 + [whole()] * 2,
        out_specs=[whole()] * 7,
        scratch_shapes=[pltpu.VMEM((blocks, height, width), BF)]
        + [pltpu.VMEM(wq.shape, BF)] * 3
        + [DMA((5,)), pair, pair, pair, pair, DMA, DMA, pair, pair, DMA, DMA, DMA, DMA],
        compiler_params=pltpu.CompilerParams(
            collective_id=0, has_side_effects=True, vmem_limit_bytes=VMEM_BYTES
        ),
        name="halo_qkv",
    )(*[in_hbm(value) for value in (x, wo, wq, wk, wv)], vec, labels)


def split3(values):
    first = values.astype(BF).astype(F32)
    second = (values - first).astype(BF).astype(F32)
    return first, second, values - first - second


def code_tile(rows, keys_code):
    count = rows.shape[1]
    terms = split3(-rows)
    lane = lax.broadcasted_iota(jnp.int32, (128, count), 0)
    tall = jnp.zeros((128, count), F32)
    for h in range(8):
        for base, row in ((LOGS, h), (CENTRES, 8 + h)):
            for i in range(3):
                tall = jnp.where(lane == base + 3 * h + i, terms[i][row : row + 1], tall)
    wide = jnp.transpose(tall)
    column = lax.broadcasted_iota(jnp.int32, wide.shape, 1)
    same = jnp.logical_and(column < CLIPS, keys_code.astype(F32) == 0.0)
    return jnp.where(same, 1.0, wide).astype(BF)


def tile_at(j):
    return pl.ds(pl.multiple_of(j * TILE, TILE), TILE)


def lanes_of(c):
    return pl.ds(c * 128, 128)


def beside(left, right):
    return jnp.concatenate([left, right], axis=1)


def stacked_heads(values, codes):
    lower = lax.broadcasted_iota(jnp.int32, values.shape, 1) < HEAD_DIM
    none = jnp.zeros_like(values)
    return jnp.concatenate(
        [beside(jnp.where(lower, values, none), codes[0]), beside(jnp.where(lower, none, values), codes[1])],
        axis=0,
    )


def heads_out(turned):
    pair = jnp.concatenate([turned[:HEAD_DIM, :TILE], turned[HEAD_DIM:, TILE:]], axis=0)
    return jnp.transpose(pair)


def within(lane, start):
    return jnp.logical_and(lane >= start, lane < start + 3)


def attfinish_kernel(b_ref, q_ref, k_ref, v_ref, kc_ref, n_ref, o_ref, lse_ref, r_ref, m_ref, l_ref, acc_ref):
    height, cols = o_ref.shape
    pairs, tiles = cols // 128, height // TILE
    steep = jnp.logical_not(jnp.max(n_ref[0:8, :]) * jnp.max(n_ref[8:16, :]) <= SAFE * SAFE)
    lane = lax.broadcasted_iota(jnp.int32, (TILE, 128), 1)

    def groups(values):
        return values.reshape(TILE // 8, 8, values.shape[1])

    def one(i, carry):
        lo, hi = b_ref[0, i], b_ref[1, i]
        own = pl.ds(pl.multiple_of(REACH * height + i * TILE, TILE), TILE)
        same = jnp.logical_and(lane < CLIPS, kc_ref[own, :].astype(F32) == 0.0)
        code = jnp.where(same, 1.0, 0.0).astype(BF)
        for c in range(pairs):
            r_ref[c] = stacked_heads(q_ref[own, lanes_of(c)], (code, code))
        acc_ref[...] = jnp.zeros(acc_ref.shape, F32)
        l_ref[...] = jnp.zeros(l_ref.shape, F32)
        m_ref[...] = jnp.zeros(m_ref.shape, F32)

        def score(j, c):
            return dot_nt(beside(k_ref[tile_at(j), lanes_of(c)], kc_ref[tile_at(j), :]), r_ref[c])

        def step(shift, j, carry):
            raised = []
            for c in range(pairs):
                s = score(j, c)
                e = jnp.exp(s - m_ref[c, 0:1, :] if shift else s)
                l_ref[c] += jnp.sum(groups(e), axis=0)
                raised.append(e.astype(BF))
            for c in range(pairs):
                acc_ref[c] += dot_tn(v_ref[tile_at(j), lanes_of(c)], raised[c])
            return carry

        @pl.when(jnp.logical_not(steep))
        def _():
            lax.fori_loop(lo, hi, functools.partial(step, False), 0)

        @pl.when(steep)
        def _():
            m_ref[...] = jnp.full(m_ref.shape, NEG, F32)

            def peak(j, carry):
                for c in range(pairs):
                    m_ref[c] = jnp.maximum(m_ref[c], jnp.max(groups(score(j, c)), axis=0))
                return carry

            lax.fori_loop(lo, hi, peak, 0)
            for c in range(pairs):
                m_ref[c] = jnp.broadcast_to(jnp.max(m_ref[c], axis=0, keepdims=True), m_ref.shape[1:])
            lax.fori_loop(lo, hi, functools.partial(step, True), 0)

        for c in range(pairs):
            total = jnp.sum(l_ref[c], axis=0, keepdims=True)
            o_ref[tile_at(i), lanes_of(c)] = heads_out(acc_ref[c] / total).astype(BF)
            logs = m_ref[c, 0:1, :] + jnp.log(total)
            lse_ref[2 * c : 2 * c + 1, tile_at(i)] = logs[:, :TILE]
            lse_ref[2 * c + 1 : 2 * c + 2, tile_at(i)] = logs[:, TILE:]
        return carry

    lse_ref[...] = jnp.zeros(lse_ref.shape, F32)
    lax.fori_loop(0, tiles, one, 0)


def local_call(kernel, name, out_shape, scratch, bounds, *values):
    grid = pltpu.PrefetchScalarGridSpec(
        num_scalar_prefetch=1,
        grid=(1,),
        in_specs=[whole()] * len(values),
        out_specs=jax.tree.map(lambda _: whole(), out_shape),
        scratch_shapes=scratch,
    )
    return pl.pallas_call(
        kernel,
        grid_spec=grid,
        out_shape=out_shape,
        compiler_params=pltpu.CompilerParams(vmem_limit_bytes=VMEM_BYTES),
        name=name,
    )(bounds, *values)


def attend(bounds, q, k, v, kc, norms, height):
    cols = k.shape[1]
    pairs = cols // 128
    out_shape = (jax.ShapeDtypeStruct((height, cols), BF), jax.ShapeDtypeStruct((8, height), F32))
    scratch = [
        pltpu.VMEM((pairs, 2 * TILE, 256), BF),
        pltpu.VMEM((pairs, 8, 2 * TILE), F32),
        pltpu.VMEM((pairs, 8, 2 * TILE), F32),
        pltpu.VMEM((pairs, 128, 2 * TILE), F32),
    ]
    return local_call(attfinish_kernel, "attend", out_shape, scratch, bounds, q, k, v, kc, norms)


def query_back_kernel(b_ref, q_ref, k_ref, v_ref, g_ref, kc_ref, qc_ref, dq_ref, r_ref, t_ref, acc_ref):
    height, cols = dq_ref.shape
    pairs, tiles = cols // 128, height // TILE
    lane = lax.broadcasted_iota(jnp.int32, (TILE, 128), 1)

    def one(i, carry):
        own = pl.ds(pl.multiple_of(REACH * height + i * TILE, TILE), TILE)
        code = qc_ref[own, :]
        none = jnp.zeros_like(code)
        for c in range(pairs):
            logs, centres = [], []
            for h in (2 * c, 2 * c + 1):
                logs.append(jnp.where(jnp.logical_or(lane < CLIPS, within(lane, LOGS + 3 * h)), code, none))
                centres.append(jnp.where(within(lane, CENTRES + 3 * h), code, none))
            r_ref[c] = stacked_heads(q_ref[own, lanes_of(c)], logs)
            t_ref[c] = stacked_heads(g_ref[own, lanes_of(c)], centres)
        acc_ref[...] = jnp.zeros(acc_ref.shape, F32)

        def step(j, carry):
            code = kc_ref[tile_at(j), :]
            steps = []
            for c in range(pairs):
                probs = jnp.exp(dot_nt(beside(k_ref[tile_at(j), lanes_of(c)], code), r_ref[c]))
                d_probs = dot_nt(beside(v_ref[tile_at(j), lanes_of(c)], code), t_ref[c])
                steps.append((probs * d_probs).astype(BF))
            for c in range(pairs):
                acc_ref[c] += dot_tn(k_ref[tile_at(j), lanes_of(c)], steps[c])
            return carry

        lax.fori_loop(b_ref[0, i], b_ref[1, i], step, 0)
        for c in range(pairs):
            dq_ref[tile_at(i), lanes_of(c)] = (heads_out(acc_ref[c]) * HEAD_DIM**-0.5).astype(BF)
        return carry

    lax.fori_loop(0, tiles, one, 0)


def query_back(bounds, q, k, v, g, kc, qc, height):
    cols = k.shape[1]
    pairs = cols // 128
    scratch = [pltpu.VMEM((pairs, 2 * TILE, 256), BF)] * 2 + [pltpu.VMEM((pairs, 128, 2 * TILE), F32)]
    out_shape = jax.ShapeDtypeStruct((height, cols), BF)
    return local_call(query_back_kernel, "query_back", out_shape, scratch, bounds, q, k, v, g, kc, qc)


def key_back_kernel(b_ref, q_ref, k_ref, v_ref, g_ref, kc_ref, qc_ref, dk_ref, dv_ref, r_ref, t_ref, ak_ref, av_ref):
    height, cols = dk_ref.shape
    pairs, tiles = cols // 128, height // TILE
    lane = lax.broadcasted_iota(jnp.int32, (TILE, 128), 1)

    def one(i, carry):
        own = pl.ds(pl.multiple_of(REACH * height + i * TILE, TILE), TILE)
        code = kc_ref[own, :]
        none, ones = jnp.zeros_like(code), jnp.ones_like(code)
        for c in range(pairs):
            logs, centres = [], []
            for h in (2 * c, 2 * c + 1):
                logs.append(jnp.where(lane < CLIPS, code, jnp.where(within(lane, LOGS + 3 * h), ones, none)))
                centres.append(jnp.where(within(lane, CENTRES + 3 * h), ones, none))
            r_ref[c] = stacked_heads(k_ref[own, lanes_of(c)], logs)
            t_ref[c] = stacked_heads(v_ref[own, lanes_of(c)], centres)
        ak_ref[...] = jnp.zeros(ak_ref.shape, F32)
        av_ref[...] = jnp.zeros(av_ref.shape, F32)

        def step(j, carry):
            code = qc_ref[tile_at(j), :]
            weights, steps = [], []
            for c in range(pairs):
                probs = jnp.exp(dot_nt(beside(q_ref[tile_at(j), lanes_of(c)], code), r_ref[c]))
                d_probs = dot_nt(beside(g_ref[tile_at(j), lanes_of(c)], code), t_ref[c])
                weights.append(probs.astype(BF))
                steps.append((probs * d_probs).astype(BF))
            for c in range(pairs):
                av_ref[c] += dot_tn(g_ref[tile_at(j), lanes_of(c)], weights[c])
                ak_ref[c] += dot_tn(q_ref[tile_at(j), lanes_of(c)], steps[c])
            return carry

        lax.fori_loop(b_ref[0, i], b_ref[1, i], step, 0)
        for c in range(pairs):
            dk_ref[tile_at(i), lanes_of(c)] = heads_out(ak_ref[c]).astype(BF)
            dv_ref[tile_at(i), lanes_of(c)] = heads_out(av_ref[c]).astype(BF)
        return carry

    lax.fori_loop(0, tiles, one, 0)


def key_back(bounds, q, k, v, g, kc, qc, height):
    cols = k.shape[1]
    pairs = cols // 128
    scratch = [pltpu.VMEM((pairs, 2 * TILE, 256), BF)] * 2 + [pltpu.VMEM((pairs, 128, 2 * TILE), F32)] * 2
    out_shape = (jax.ShapeDtypeStruct((height, cols), BF),) * 2
    return local_call(key_back_kernel, "key_back", out_shape, scratch, bounds, q, k, v, g, kc, qc)


class Ring:
    def __init__(self):
        d = lax.axis_index("dp")
        n = lax.axis_size("dp") // 2
        chip = d // 2
        core = d - 2 * chip
        odd = chip - 2 * (chip // 2)
        spot = (1 - odd) * (chip // 2) + odd * (n - 1 - chip // 2)
        self.here = (1 - core) * spot + core * (n - 1 - spot)
        self.n, self.core, self.hops = n, core, n // 2
        self.sibling = {"dp": d + 1 - 2 * core}
        self.after = {"dp": self.device_at(self.wrap(self.here + 1))}
        self.before = {"dp": self.device_at(self.wrap(self.here - 1))}

    def wrap(self, index):
        return lax.rem(index + 2 * self.n, self.n)

    def device_at(self, rank):
        n, core = self.n, self.core
        walk = (1 - core) * rank + core * (n - 1 - rank)
        late = walk // (n // 2)
        return 2 * ((1 - late) * (2 * walk) + late * (2 * (n - walk) - 1)) + core

    def spans(self, shape, i, owner, j):
        rows, cols = shape[0] // 2, shape[1]
        wide = STRIPS * STRIP
        high, count = rows * cols // (self.n * wide), cols // wide
        line = j // count
        row = pl.multiple_of(owner * rows + line * high, high)
        col = pl.multiple_of((j - line * count) * wide + i * STRIP, STRIP)
        return pl.ds(row, high), pl.ds(col, STRIP)


def units(arrays):
    return [(a, i, pl.ds(i * STRIP, STRIP), a * STRIPS + i) for a in range(arrays) for i in range(STRIPS)]


class Reduce:
    def __init__(self, ring, given, sibs, bufs, sems):
        self.ring, self.given, self.sibs, self.bufs, self.sems = ring, given, sibs, bufs, sems
        self.units = units(len(given))

    def s_copy(self, a):
        rows = self.given[a].shape[0] // 2
        span = pl.ds(pl.multiple_of((1 - self.ring.core) * rows, rows), rows)
        return remote(
            self.given[a].at[span], self.sibs[a], self.sems[0].at[a], self.sems[1].at[a], self.ring.sibling
        )

    def ways(self):
        ring = self.ring
        return (
            (0, ring.hops, lambda s: ring.wrap(ring.here + ring.hops - s), ring.after),
            (ring.hops + 1, ring.hops - 1, lambda s: ring.wrap(ring.here - ring.hops + 1 + s), ring.before),
        )

    def r_copy(self, u, way, s):
        a, _, strip, e = u
        base, _, _, target = way
        k = (s if base == 0 else self.ring.hops + s)
        src, dst = self.bufs[a].at[base + s, :, strip], self.bufs[a].at[base + s + 1, :, strip]
        return remote(src, dst, self.sems[2].at[e, k], self.sems[3].at[e, k], target)

    def terms(self, u, j):
        a, i, _, _ = u
        shape, core = self.given[a].shape, self.ring.core
        mine = self.given[a][self.ring.spans(shape, i, core, j)].astype(F32)
        return mine + self.sibs[a][self.ring.spans(shape, i, 0, j)].astype(F32)

    def swap(self, a):
        self.s_copy(a).start()

    def first(self, a):
        self.s_copy(a).wait_recv()
        for u in self.units:
            if u[0] == a:
                for way in self.ways():
                    self.bufs[a][way[0], :, u[2]] = self.terms(u, way[2](0)).astype(BF)
                    self.r_copy(u, way, 0).start()

    def step(self, s, both=True):
        for u in self.units:
            a, _, strip, _ = u
            for way in self.ways()[: 2 if both else 1]:
                slot = way[0] + s
                local = self.terms(u, way[2](s))
                self.r_copy(u, way, s - 1).wait_recv()
                self.bufs[a][slot, :, strip] = (self.bufs[a][slot, :, strip].astype(F32) + local).astype(BF)
                self.r_copy(u, way, s).start()

    def turn(self):
        hops = self.ring.hops
        for u in self.units:
            a, _, strip, _ = u
            local = self.terms(u, self.ring.here)
            ahead, back = self.ways()
            self.r_copy(u, back, hops - 2).wait_recv()
            local = local + self.bufs[a][2 * hops, :, strip].astype(F32)
            self.r_copy(u, ahead, hops - 1).wait_recv()
            self.bufs[a][hops, :, strip] = (self.bufs[a][hops, :, strip].astype(F32) + local).astype(BF)

    def settle(self):
        for a in range(len(self.given)):
            self.s_copy(a).wait_send()
        for way in self.ways():

            def step(s, carry):
                for u in self.units:
                    self.r_copy(u, way, s).wait_send()
                return carry

            lax.fori_loop(0, way[1], step, 0)


class Gather:
    def __init__(self, ring, outs, sems):
        self.ring, self.outs, self.sems = ring, outs, sems
        self.units = units(len(outs))

    def spot(self, u, j):
        out, ring = self.outs[u[0]], self.ring
        return out.at[ring.spans(out.shape, u[1], ring.core, ring.wrap(ring.here + j))]

    def g_copy(self, u, way, s):
        ring = self.ring
        spot = self.spot(u, -s if way == 0 else s)
        k = s if way == 0 else ring.hops + s
        target = ring.after if way == 0 else ring.before
        return remote(spot, spot, self.sems[0].at[u[3], k], self.sems[1].at[u[3], k], target)

    def c_copy(self, u, way, s):
        spot = self.spot(u, -s if way == 0 else s)
        k = s if way == 0 else self.ring.hops + s
        return remote(spot, spot, self.sems[2].at[u[3], k], self.sems[3].at[u[3], k], self.ring.sibling)

    def begin(self, sources):
        for u in self.units:
            a, _, strip, _ = u
            self.spot(u, 0)[...] = sources[a][:, strip]
            self.g_copy(u, 0, 0).start()
            self.g_copy(u, 1, 0).start()
            self.c_copy(u, 0, 0).start()

    def step(self, s):
        for u in self.units:
            for way in (0, 1):
                self.g_copy(u, way, s - 1).wait_recv()
                self.g_copy(u, way, s).start()
                self.c_copy(u, way, s).start()

    def last(self):
        hops = self.ring.hops
        for u in self.units:
            self.g_copy(u, 0, hops - 2).wait_recv()
            self.g_copy(u, 0, hops - 1).start()
            self.c_copy(u, 0, hops - 1).start()
            self.g_copy(u, 1, hops - 2).wait_recv()
            self.c_copy(u, 1, hops - 1).start()
        for u in self.units:
            self.g_copy(u, 0, hops - 1).wait_recv()
            self.c_copy(u, 0, hops).start()

    def settle(self):
        hops = self.ring.hops
        for way in (0, 1):

            def sent(s, carry):
                for u in self.units:
                    self.g_copy(u, way, s).wait_send()
                return carry

            def copied(s, carry):
                for u in self.units:
                    self.c_copy(u, way, s).wait()
                return carry

            lax.fori_loop(0, hops - way, sent, 0)
            lax.fori_loop(way, hops + 1 - way, copied, 0)


def between(step, done, hops):
    def body(s, carry):
        step(s)
        return carry

    if done < hops - 1:
        lax.fori_loop(done, hops - 1, body, 0)


def chunk_rows(shape, n):
    return shape[0] * shape[1] // (2 * n * STRIPS * STRIP)


def reduce_scratch(shapes, n):
    count = len(shapes)
    sibs = [pltpu.VMEM((rows // 2, cols), BF) for rows, cols in shapes]
    bufs = [pltpu.VMEM((n + 1, chunk_rows(shape, n), STRIPS * STRIP), BF) for shape in shapes]
    return sibs + bufs, [DMA((count,))] * 2 + [DMA((count * STRIPS, n - 1))] * 2


def gather_sems(count, n):
    return [DMA((count * STRIPS, n - 1))] * 2 + [DMA((count * STRIPS, n))] * 2


def norm_back_rows(grad, values, gain):
    middle = jnp.mean(values, axis=-1, keepdims=True)
    centred = values - middle
    inverse = lax.rsqrt(jnp.mean(centred * centred, axis=-1, keepdims=True) + 1e-05)
    n = centred * inverse
    t = grad * gain
    back = (t - jnp.mean(t, axis=-1, keepdims=True) - n * jnp.mean(t * n, axis=-1, keepdims=True)) * inverse
    return back, grad * n


def column_sums(values):
    return jnp.sum(values, axis=0, keepdims=True)


def mid_kernel(
    x_ref, cot_ref, mix_ref, lse_ref, kc_ref, wof_ref, row_ref, w1_ref, w2_ref,
    xw_ref, qc_ref, rg_ref, low_ref, vec_ref, own1_ref, own2_ref, res_ref, outp_ref,
    om_ref, dact_ref, mi_ref, act_ref, pg_ref, part_ref, oth_ref, f1_ref, f2_ref, st_ref, sw_ref,
    sib1, sib2, buf1, buf2,
    sm, rm, sy, ry, sx, rx, ss, rs, sf, rf, *ring_sems,
):
    d, core, has_left, has_right = place()
    t = lax.axis_index("tensor")
    height, cols = mix_ref.shape
    width, hidden = w1_ref.shape
    rows = height // PARTS
    sibling = {"dp": d + 1 - 2 * core}
    across = {"tensor": 1 - t}
    exists = (has_left, has_right)
    slots = (0, 2 * REACH)
    ring = Ring()
    reduce = Reduce(ring, (f1_ref, f2_ref), (sib1, sib2), (buf1, buf2), ring_sems)
    hops = ring.hops
    greet([
        (None, sibling), (None, across), (has_left, {"dp": d - 2}), (has_right, {"dp": d + 2}),
        (None, ring.after), (None, ring.before),
    ])

    def span(p):
        return pl.ds(pl.multiple_of(p * rows, rows), rows)

    def m_copy(p):
        return remote(mix_ref.at[span(p)], om_ref.at[span(p)], sm.at[p], rm.at[p], across)

    def y_copy(p):
        return remote(part_ref.at[span(p)], oth_ref.at[span(p)], sy.at[p], ry.at[p], across)

    def refs(p):
        if p == PARTS:
            return st_ref, lambda slot: sw_ref.at[slot]
        return xw_ref.at[REACH, span(p)], lambda slot: xw_ref.at[slot, span(p)]

    def x_copy(side, p):
        src, dst = refs(p)
        return remote(
            src, dst(slots[side]), sx.at[side, p], rx.at[side, p],
            {"dp": d + 2 if side == 0 else d - 2},
        )

    def s_copy(p):
        src, dst = refs(p)
        return remote(src, dst(1 + 2 * core), ss.at[p], rs.at[p], sibling)

    def f_copy(p):
        _, dst = refs(p)
        return remote(dst(4 - 4 * core), dst(3 - 2 * core), sf.at[p], rf.at[p], sibling)

    def send(p):
        for side in (0, 1):

            @pl.when(exists[1 - side])
            def _():
                x_copy(side, p).start()

        s_copy(p).start()

    def pass_on(p):
        for side in (0, 1):

            @pl.when(exists[side])
            def _():
                x_copy(side, p).wait_recv()

            @pl.when(jnp.logical_and(exists[side], core == 1 - side))
            def _():
                f_copy(p).start()

    for p in range(PARTS):
        m_copy(p).start()
    vec = row_ref[...].astype(F32)
    out_bias, gain, shift = vec[3:4], vec[4:5], vec[5:6]
    heads = pl.ds(pl.multiple_of(t * cols, cols), cols)
    others = pl.ds(pl.multiple_of((1 - t) * cols, cols), cols)
    picks = lax.broadcasted_iota(jnp.int32, (8, cols), 1) // HEAD_DIM
    picks = (picks == lax.broadcasted_iota(jnp.int32, (8, cols), 0)).astype(F32)
    st_ref[0:8, :] = lse_ref[...]
    vec_ref[...] = jnp.zeros(vec_ref.shape, F32)

    def early(p, carry):
        cot = cot_ref[span(p), :]
        dact_ref[span(p), :] = dot_nt(cot, w2_ref[...])
        vec_ref[3:4, :] += column_sums(cot.astype(F32))
        res_ref[span(p), :] = x_ref[span(p), :].astype(F32) + dot_nn(mix_ref[span(p), :], wof_ref[heads, :]) + out_bias
        return carry

    lax.fori_loop(0, PARTS, early, 0)

    def forward(p, carry):
        m_copy(p).wait_recv()
        residual = res_ref[span(p), :] + dot_nn(om_ref[span(p), :], wof_ref[others, :])
        res_ref[span(p), :] = residual
        mlp_input = (norm_rows(residual) * gain + shift).astype(BF)
        mi_ref[span(p), :] = mlp_input
        for i in range(hidden // width):
            part = slice(i * width, (i + 1) * width)
            preact = dot_nn(mlp_input, w1_ref[:, part]) + vec[6 + i : 7 + i]
            cdf = 0.5 * (1.0 + lax.erf(preact * (2.0**-0.5)))
            pdf = jnp.exp(-0.5 * preact * preact) * 0.3989422804014327
            act_ref[span(p), part] = (preact * cdf).astype(BF)
            pre_grad = (dact_ref[span(p), part] * (cdf + preact * pdf)).astype(BF)
            pg_ref[span(p), part] = pre_grad
            vec_ref[4 + i : 5 + i, :] += column_sums(pre_grad.astype(F32))
        part_ref[span(p), :] = dot_nt(pg_ref[span(p), :], w1_ref[...]).astype(BF)
        y_copy(p).start()
        return carry

    lax.fori_loop(0, PARTS, forward, 0)

    def weights(which):
        half = pl.ds(pl.multiple_of(which * (width // 2), width // 2), width // 2)
        f1_ref[half, :] = dot_tn(mi_ref[:, half], pg_ref[...]).astype(BF)
        half = pl.ds(pl.multiple_of(which * (hidden // 2), hidden // 2), hidden // 2)
        f2_ref[half, :] = dot_tn(act_ref[:, half], cot_ref[...]).astype(BF)

    def back(p):
        y_copy(p).wait_recv()
        grad = part_ref[span(p), :].astype(F32) + oth_ref[span(p), :].astype(F32)
        turned, scaled = norm_back_rows(grad, res_ref[span(p), :], gain)
        total = cot_ref[span(p), :].astype(F32) + turned
        low = total.astype(BF)
        rg_ref[span(p), :] = total
        low_ref[span(p), :] = low
        vec_ref[0:1, :] += column_sums(scaled)
        vec_ref[1:2, :] += column_sums(grad)
        vec_ref[2:3, :] += column_sums(low.astype(F32))
        mixed_grad = dot_nt(low, wof_ref[heads, :]).astype(BF)
        xw_ref[REACH, span(p), :] = mixed_grad
        product = mixed_grad.astype(F32) * mix_ref[span(p), :].astype(F32)
        st_ref[8:16, p * rows : (p + 1) * rows] = lax.dot_general(
            picks, product, (((1,), (1,)), ((), ())),
            precision=lax.Precision.HIGHEST, preferred_element_type=F32,
        )

    def code(slot):
        def step(i, carry):
            spot = pl.ds(pl.multiple_of(slot * height + i * TILE, TILE), TILE)
            stats = sw_ref[slot, :, pl.ds(pl.multiple_of(i * TILE, TILE), TILE)]
            qc_ref[spot, :] = code_tile(stats, kc_ref[spot, :])
            return carry

        lax.fori_loop(0, height // TILE, step, 0)

    def ring_step(s):
        if s < hops - 1:
            reduce.step(s)

    back(0)
    send(0)
    weights(1 - core)
    reduce.swap(0)
    reduce.swap(1)
    back(1)
    send(1)
    weights(core)
    reduce.first(0)
    reduce.first(1)
    back(2)
    send(2)
    send(PARTS)
    sw_ref[REACH] = st_ref[...]
    ring_step(1)
    pass_on(0)
    outp_ref[...] = dot_nn(act_ref[...], w2_ref[...]).astype(BF)
    ring_step(2)
    pass_on(1)
    between(reduce.step, 3, hops)
    reduce.step(hops - 1, False)
    pass_on(2)
    pass_on(PARTS)
    code(REACH)
    reduce.turn()
    own1_ref[...] = buf1[hops]
    own2_ref[...] = buf2[hops]
    for p in range(PARTS + 1):
        s_copy(p).wait()
        for side in (0, 1):

            @pl.when(exists[1 - side])
            def _():
                x_copy(side, p).wait_send()

            @pl.when(jnp.logical_and(exists[side], core == 1 - side))
            def _():
                f_copy(p).wait_send()

            @pl.when(jnp.logical_and(exists[side], core == side))
            def _():
                f_copy(p).wait_recv()

    code(3 - 2 * core)
    for side in (0, 1):

        @pl.when(exists[side])
        def _():
            code(slots[side])

        @pl.when(jnp.logical_and(exists[side], core == side))
        def _():
            code(1 + 2 * core)

    for p in range(PARTS):
        m_copy(p).wait_send()
        y_copy(p).wait_send()
    reduce.settle()


def mid(x, cot, mix, lse, kc, wof, vec, w1, w2):
    blocks = 2 * REACH + 1
    height, width = x.shape
    hidden = w1.shape[1]
    n = lax.axis_size("dp") // 2
    pair, line, some = DMA((2, PARTS + 1)), DMA((PARTS + 1,)), DMA((PARTS,))
    room, sems = reduce_scratch((w1.shape, w2.shape), n)
    shape = jax.ShapeDtypeStruct
    chunks = [shape((chunk_rows(w.shape, n), STRIPS * STRIP), BF) for w in (w1, w2)]
    return pl.pallas_call(
        mid_kernel,
        out_shape=(
            shape((blocks,) + mix.shape, BF), shape(kc.shape, BF), shape(x.shape, F32), shape(x.shape, BF),
            shape((16, width), F32), *chunks, shape(x.shape, F32), shape(x.shape, BF),
        ),
        in_specs=[whole()] * 9,
        out_specs=[whole()] * 9,
        scratch_shapes=[
            pltpu.VMEM(mix.shape, BF), pltpu.VMEM((height, hidden), F32), pltpu.VMEM(x.shape, BF),
            pltpu.VMEM((height, hidden), BF), pltpu.VMEM((height, hidden), BF), pltpu.VMEM(x.shape, BF),
            pltpu.VMEM(x.shape, BF), pltpu.VMEM(w1.shape, BF), pltpu.VMEM(w2.shape, BF),
            pltpu.VMEM((16, height), F32), pltpu.VMEM((blocks, 16, height), F32),
        ]
        + room
        + [some, some, some, some, pair, pair, line, line, line, line]
        + sems,
        compiler_params=pltpu.CompilerParams(
            collective_id=1, has_side_effects=True, vmem_limit_bytes=MID_BYTES
        ),
        name="mid",
    )(x, cot, mix, lse, kc, wof, vec, w1, w2)


def finish_kernel(
    rounds, dq_ref, dk_ref, dv_ref, wq_ref, wk_ref, wv_ref, a_ref, low_ref, o_ref, x_ref, rg_ref, row_ref, vec_ref,
    own1_ref, own2_ref, res_hbm, outp_hbm, outo_hbm,
    ig_ref, g_ref, vs_ref, g1_ref, g2_ref, lo_ref,
    part_ref, oth_ref, own_ref, send_ref, got_ref, res_ref, outp_ref, outo_ref, sib, buf,
    load, sy, ry, sd, rd, *ring_sems,
):
    d, core, _, _ = place()
    t = lax.axis_index("tensor")
    height, cols = dq_ref.shape
    width = x_ref.shape[1]
    piece = height // PIECES
    across = {"tensor": 1 - t}
    loads = [
        pltpu.make_async_copy(src, dst, load.at[i])
        for i, (src, dst) in enumerate(((res_hbm, res_ref), (outp_hbm, outp_ref), (outo_hbm, outo_ref)))
    ]
    for copy in loads:
        copy.start()
    ring = Ring()
    reduce = Reduce(ring, (own_ref,), (sib,), (buf,), ring_sems[:4])
    gather = Gather(ring, (g_ref,), ring_sems[4:8])
    wide = Gather(ring, (g1_ref, g2_ref), ring_sems[8:])
    hops = ring.hops
    partners = []
    for r in range(rounds):
        bit = (d // 2**r) - 2 * (d // 2 ** (r + 1))
        partners.append({"dp": d + 2**r * (1 - 2 * bit)})
    greet([(None, across), (None, ring.after), (None, ring.before)] + [(None, p) for p in partners])

    def y_copy(p):
        span = pl.ds(p * piece, piece)
        return remote(part_ref.at[span], oth_ref.at[span], sy.at[p], ry.at[p], across)

    def d_copy(r):
        return remote(send_ref.at[r], got_ref.at[r], sd.at[r], rd.at[r], partners[r])

    def share(p):
        span = pl.ds(p * piece, piece)
        part = dot_nt(dq_ref[span, :], wq_ref[...]) + dot_nt(dk_ref[span, :], wk_ref[...])
        part_ref[span, :] = (part + dot_nt(dv_ref[span, :], wv_ref[...])).astype(BF)

    def weights(which):
        span = pl.ds(pl.multiple_of(which * (width // 2), width // 2), width // 2)
        attn = a_ref[:, span]
        for i, ref in enumerate((dq_ref, dk_ref, dv_ref)):
            own_ref[span, i * cols : (i + 1) * cols] = dot_tn(attn, ref[...]).astype(BF)
        own_ref[span, 3 * cols : 4 * cols] = dot_tn(low_ref[:, span], o_ref[...]).astype(BF)

    def wide_step(s):
        if s < hops - 1:
            wide.step(s)

    for p in range(AHEAD):
        share(p)
        y_copy(p).start()
    wide.begin((own1_ref, own2_ref))
    weights(1 - core)
    reduce.swap(0)
    for p in range(AHEAD, PIECES):
        share(p)
    wide_step(1)
    weights(core)
    vec = row_ref[...].astype(F32)
    gain, fc2_bias = vec[0:1], vec[8:9]
    gains, shifts = [], []

    def back(p):
        span = pl.ds(p * piece, piece)
        y_copy(p).wait_recv()
        if p + AHEAD < PIECES:
            y_copy(p + AHEAD).start()
        grad = part_ref[span, :].astype(F32) + oth_ref[span, :].astype(F32)
        turned, scaled = norm_back_rows(grad, x_ref[span, :].astype(F32), gain)
        ig_ref[span, :] = rg_ref[span, :] + turned
        gains.append(column_sums(scaled))
        shifts.append(column_sums(grad))

    def reduce_step(s):
        if s < hops - 1:
            reduce.step(s)

    def gather_step(s):
        if s < hops - 1:
            gather.step(s)

    def layer_out(p):
        span = pl.ds(p * piece, piece)
        total = outp_ref[span, :].astype(F32) + outo_ref[span, :].astype(F32)
        lo_ref[span, :] = (res_ref[span, :] + total + fc2_bias).astype(BF)

    def double(s):
        if s < rounds:
            d_copy(s).wait_recv()
            total = send_ref[s] + got_ref[s]
            if s + 1 < rounds:
                send_ref[s + 1] = total
                d_copy(s + 1).start()
            else:
                vs_ref[...] = total

    reduce.first(0)
    back(0)
    wide_step(2)
    reduce_step(1)
    back(1)
    reduce_step(2)
    back(2)
    between(reduce.step, 3, hops)
    between(wide.step, 3, hops)
    reduce.step(hops - 1, False)
    back(3)
    wide.last()
    reduce.turn()
    gather.begin((buf.at[hops],))
    back(4)
    gather_step(1)
    back(5)
    send_ref[0] = vec_ref[...]
    send_ref[0, 6:7, 0:cols] = column_sums(dq_ref[...].astype(F32))
    send_ref[0, 6:7, cols : 2 * cols] = column_sums(dv_ref[...].astype(F32))
    send_ref[0, 7:8, :] = sum(gains[1:], gains[0])
    send_ref[0, 8:9, :] = sum(shifts[1:], shifts[0])
    d_copy(0).start()
    gather_step(2)
    for copy in loads:
        copy.wait()
    layer_out(0)
    double(0)
    layer_out(1)
    between(gather.step, 3, hops)
    double(1)
    layer_out(2)
    gather.last()
    double(2)
    layer_out(3)
    layer_out(4)
    layer_out(5)
    for s in range(3, rounds):
        double(s)
    for p in range(PIECES):
        y_copy(p).wait_send()
    for r in range(rounds):
        d_copy(r).wait_send()
    reduce.settle()
    wide.settle()
    gather.settle()


def finish(dq, dk, dv, wq, wk, wv, attn, low, o, x, rg, gain, vectors, own1, own2, res, outp, outo, shapes):
    height, cols = dq.shape
    width = x.shape[1]
    size = lax.axis_size("dp")
    rounds = size.bit_length() - 1
    n = size // 2
    weights = (width, 4 * cols)
    room, sems = reduce_scratch((weights,), n)
    shape = jax.ShapeDtypeStruct
    return pl.pallas_call(
        functools.partial(finish_kernel, rounds),
        out_shape=(
            shape((height, width), F32), shape(weights, BF), shape(vectors.shape, F32),
            *[shape(dims, BF) for dims in shapes], shape((height, width), BF),
        ),
        in_specs=[whole()] * 15 + [far()] * 3,
        out_specs=[whole()] * 6,
        scratch_shapes=[
            pltpu.VMEM((height, width), BF), pltpu.VMEM((height, width), BF), pltpu.VMEM(weights, BF),
            pltpu.VMEM((rounds,) + vectors.shape, F32), pltpu.VMEM((rounds,) + vectors.shape, F32),
            pltpu.VMEM((height, width), F32), pltpu.VMEM((height, width), BF), pltpu.VMEM((height, width), BF),
        ]
        + room
        + [DMA((3,)), DMA((PIECES,)), DMA((PIECES,)), DMA((rounds,)), DMA((rounds,))]
        + sems
        + gather_sems(1, n)
        + gather_sems(2, n),
        compiler_params=pltpu.CompilerParams(
            collective_id=2, has_side_effects=True, vmem_limit_bytes=FINISH_BYTES
        ),
        name="finish",
    )(dq, dk, dv, wq, wk, wv, attn, low, o, x, rg, gain, vectors, own1, own2, res, outp, outo)


def widen_kernel(a_ref, f1_ref, f2_ref, q_ref, k_ref, v_ref, o_ref, g1_ref, g2_ref):
    cols = q_ref.shape[1]
    for i, ref in enumerate((q_ref, k_ref, v_ref)):
        ref[...] = a_ref[:, i * cols : (i + 1) * cols].astype(F32)
    o_ref[...] = jnp.transpose(a_ref[:, 3 * cols :].astype(F32))
    g1_ref[...] = f1_ref[...].astype(F32)
    g2_ref[...] = f2_ref[...].astype(F32)


def widen(attn, f1, f2):
    width = attn.shape[0]
    cols, steps = attn.shape[1] // 4, width // 128
    shape = jax.ShapeDtypeStruct

    def block(array):
        return pl.BlockSpec((array.shape[0] // steps, array.shape[1]), lambda i: (i, 0))

    thin = shape((width, cols), F32)
    outs = (thin, thin, thin, shape((cols, width), F32), shape(f1.shape, F32), shape(f2.shape, F32))
    return pl.pallas_call(
        widen_kernel,
        grid=(steps,),
        out_shape=outs,
        in_specs=[block(attn), block(f1), block(f2)],
        out_specs=[block(thin)] * 3
        + [pl.BlockSpec((cols, 128), lambda i: (0, i)), block(f1), block(f2)],
        compiler_params=pltpu.CompilerParams(vmem_limit_bytes=VMEM_BYTES),
        name="widen",
    )(attn, f1, f2)


def swapped(value):
    return lax.ppermute(value, "tensor", [(0, 1), (1, 0)])


def on_device(
    inputs, clip_ids, attn_gain, attn_shift, w_query, query_bias, w_key, w_value, value_bias,
    w_out, out_bias, mlp_gain, mlp_shift, w_fc1, fc1_bias, w_fc2, fc2_bias, cotangent,
):
    height = inputs.shape[0]
    d = lax.axis_index("dp")
    reach = REACH * height
    cols = w_query.shape[1]

    padded = jnp.pad(clip_ids, (reach, 0), constant_values=-1)
    padded = jnp.pad(padded, (0, reach), constant_values=1 << 20)
    window = lax.dynamic_slice_in_dim(padded, d * height, height + 2 * reach)
    own = window[reach : reach + height]
    firsts, lasts = own[::TILE], own[TILE - 1 :: TILE]
    begin = jnp.sum((window[None, :] < firsts[:, None]).astype(jnp.int32), axis=1)
    end = jnp.sum((window[None, :] <= lasts[:, None]).astype(jnp.int32), axis=1)
    bounds = jnp.stack([begin // TILE, (end + TILE - 1) // TILE])
    labels = window.astype(F32).reshape(-1, 128)
    split = jnp.pad(query_bias, (0, cols)) + jnp.pad(value_bias, (cols, 0))
    width = inputs.shape[1]
    rows = [attn_gain, attn_shift, split, out_bias, mlp_gain, mlp_shift, fc1_bias[:width], fc1_bias[width:], fc2_bias]
    line = lax.broadcasted_iota(jnp.int32, (16, width), 0)
    vec = jnp.zeros((16, width), BF)
    for i, values in enumerate(rows):
        vec = jnp.where(line == i, values[None, :], vec)

    q, k, v, attn_input, w_out_full, norms, key_code = halo_qkv(
        inputs, w_out, w_query, w_key, w_value, vec, labels
    )
    mixed, logs = attend(bounds, q, k, v, key_code, norms, height)
    grad_win, query_code, residual_grad, low, vectors, own1, own2, residual, out_part = mid(
        inputs, cotangent, mixed, logs, key_code, w_out_full, vec, w_fc1, w_fc2
    )
    grad_win = grad_win.reshape(-1, grad_win.shape[2])
    out_part, query_code = lax.optimization_barrier((out_part, query_code))
    out_other = swapped(out_part)
    query_low = query_back(bounds, q, k, v, grad_win, key_code, query_code, height)
    key_low, value_low = key_back(bounds, q, k, v, grad_win, key_code, query_code, height)
    out_other, key_low = lax.optimization_barrier((out_other, key_low))
    inputs_grad, attn_sum, sums, fc1_sum, fc2_sum, layer_out = finish(
        query_low, key_low, value_low, w_query, w_key, w_value, attn_input, low, mixed, inputs,
        residual_grad, vec, vectors, own1, own2, residual, out_part, out_other, (w_fc1.shape, w_fc2.shape),
    )
    q_grad, k_grad, v_grad, o_grad, fc1_grad, fc2_grad = widen(attn_sum, fc1_sum, fc2_sum)
    return (
        layer_out, inputs_grad, sums[7], sums[8],
        q_grad, sums[6, :cols], k_grad, v_grad, sums[6, cols:],
        o_grad, sums[2], sums[0], sums[1],
        fc1_grad, sums[4:6].reshape(-1), fc2_grad, sums[3],
    )


def solution(mesh):
    rows, cols, split, every = P("dp", None), P(None, "tensor"), P("tensor"), P()
    tall = P("tensor", None)
    in_specs = (
        rows, every, every, every, cols, split, cols, cols, split, tall, every, every, every,
        cols, split, tall, every, rows,
    )
    out_specs = (
        rows, rows, every, every, cols, split, cols, cols, split, tall, every, every, every,
        cols, split, tall, every,
    )
    return jax.shard_map(on_device, mesh=mesh, in_specs=in_specs, out_specs=out_specs, check_vma=False)
```

```python
import functools

import jax
import jax.numpy as jnp
from jax import lax
from jax.experimental import pallas as pl
from jax.experimental.pallas import tpu as pltpu
from jax.sharding import PartitionSpec as P

HEAD_DIM = 64
REACH = 2
TILE = 256
PIECES = 6
AHEAD = 2
NEG = -3e38
CLIPS = 64
LOGS = 64
CENTRES = 96
FAR = -(2.0**100)
SAFE = 40.0
BF = jnp.bfloat16
F32 = jnp.float32
MESH = pl.DeviceIdType.MESH
VMEM = pltpu.VMEM
VMEM_BYTES = 10_000_000
MID_BYTES = 28_000_000
FINISH_BYTES = 16_000_000
PARTS = 3
WIDEN_BYTES = 16_000_000
STRIP = 128
STRIPS = 3
DMA = pltpu.SemaphoreType.DMA


def dot_nn(left, right):
    return jnp.dot(left, right, preferred_element_type=F32)


def dot_tn(left, right):
    return lax.dot_general(left, right, (((0,), (0,)), ((), ())), preferred_element_type=F32)


def dot_nt(left, right):
    return lax.dot_general(left, right, (((1,), (1,)), ((), ())), preferred_element_type=F32)


def whole():
    return pl.BlockSpec(memory_space=VMEM)


def far():
    return pl.BlockSpec(memory_space=pltpu.HBM)


def in_hbm(value):
    return pltpu.with_memory_space_constraint(value, pltpu.HBM)


def remote(src, dst, send_sem, recv_sem, device):
    return pltpu.make_async_remote_copy(
        src_ref=src,
        dst_ref=dst,
        send_sem=send_sem,
        recv_sem=recv_sem,
        device_id=device,
        device_id_type=MESH,
    )


def place():
    d = lax.axis_index("dp")
    chip = d // 2
    core = d - 2 * chip
    has_left = chip > 0
    has_right = chip < lax.axis_size("dp") // 2 - 1
    return d, core, has_left, has_right


def greet(targets):
    barrier = pltpu.get_barrier_semaphore()
    count = 0
    for present, device in targets:
        if present is None:
            pl.semaphore_signal(barrier, inc=1, device_id=device, device_id_type=MESH)
            count = count + 1
        else:

            @pl.when(present)
            def _():
                pl.semaphore_signal(barrier, inc=1, device_id=device, device_id_type=MESH)

            count = count + present.astype(jnp.int32)
    pl.semaphore_wait(barrier, count)


def norm_rows(values):
    middle = jnp.mean(values, axis=-1, keepdims=True)
    centred = values - middle
    spread = jnp.mean(centred * centred, axis=-1, keepdims=True)
    return centred * lax.rsqrt(spread + 1e-05)


def halo_kernel(
    x_ref, wo_ref, wq_ref, wk_ref, wv_ref, vec_ref, lab_ref,
    q_ref, k_ref, v_ref, a_ref, wof_ref, n_ref, kc_ref,
    win, wq, wk, wv, load, sx, rx, sy, ry, ss, rs, sf, rf, sw, rw, sv, rv,
):
    d, core, has_left, has_right = place()
    t = lax.axis_index("tensor")
    height = x_ref.shape[0]
    cols = wq_ref.shape[1]
    half = height // 2
    piece = half // PIECES
    sibling = {"dp": d + 1 - 2 * core}
    across = {"tensor": 1 - t}
    exists = (has_left, has_right)
    slots = (0, 2 * REACH)
    part = wo_ref.shape[0] // 2
    wo_rows = pl.ds(pl.multiple_of(core * part, part), part)
    mine = pl.ds(pl.multiple_of(t * 2 * part, part), 2 * part)
    loads = [
        pltpu.make_async_copy(src, dst, load.at[i])
        for i, (src, dst) in enumerate(
            ((x_ref, win.at[REACH]), (wq_ref, wq), (wk_ref, wk), (wv_ref, wv), (wo_ref, wof_ref.at[mine]))
        )
    ]
    for copy in loads:
        copy.start()
    greet([(None, sibling), (None, across), (has_left, {"dp": d - 2}), (has_right, {"dp": d + 2})])

    def rows(which, p):
        return pl.ds(pl.multiple_of(which * half + p * piece, piece), piece)

    def x_copy(side, p):
        return remote(
            x_ref.at[rows(t, p)], win.at[slots[side], rows(t, p)], sx.at[side, p], rx.at[side, p],
            {"dp": d + 2 if side == 0 else d - 2},
        )

    def y_copy(side, p):
        spot = win.at[slots[side], rows(t, p)]
        return remote(spot, spot, sy.at[side, p], ry.at[side, p], across)

    def f_copy(which, p):
        span = rows(t if which == 0 else 1 - t, p)
        return remote(
            win.at[4 - 4 * core, span], win.at[3 - 2 * core, span], sf.at[which, p], rf.at[which, p],
            sibling,
        )

    own_copy = remote(x_ref, win.at[1 + 2 * core], ss, rs, sibling)

    def full_rows(which):
        return pl.ds(pl.multiple_of((2 * which + core) * part, part), part)

    w_copy = remote(wo_ref.at[wo_rows], wof_ref.at[full_rows(t)], sw, rw, across)
    wf_copy = remote(wof_ref.at[full_rows(1 - t)], wof_ref.at[full_rows(1 - t)], sv, rv, sibling)

    def send(p):
        for side in (0, 1):

            @pl.when(exists[1 - side])
            def _():
                x_copy(side, p).start()

    for p in range(AHEAD):
        send(p)
    w_copy.start()
    own_copy.start()
    vec = vec_ref[...].astype(F32)
    gain, shift = vec[0:1], vec[1:2]
    query_bias, value_bias = vec[2:3, :cols], vec[2:3, cols:]
    n_ref[...] = jnp.zeros(n_ref.shape, F32)

    def code(r, carry):
        labels = jnp.transpose(jnp.broadcast_to(lab_ref[pl.ds(r, 1), :], (128, 128)))
        lane = lax.broadcasted_iota(jnp.int32, (128, 128), 1)
        far = jnp.where(labels == lane.astype(F32), 0.0, FAR)
        kc_ref[pl.ds(pl.multiple_of(r * 128, 128), 128), :] = jnp.where(lane < CLIPS, far, 1.0).astype(BF)
        return carry

    lax.fori_loop(0, lab_ref.shape[0], code, 0)

    def raise_norm(spot, values):
        for c in range(cols // 128):
            span = values[:, c * 128 : c * 128 + 128]
            norm = jnp.max(jnp.sum(span * span, axis=1, keepdims=True), axis=0, keepdims=True)
            n_ref[spot, :] = jnp.maximum(n_ref[spot, :], norm)

    def project(slot, start):
        spot = pl.ds(pl.multiple_of(start, half // 2), half // 2)
        attn = (norm_rows(win[slot, spot, :].astype(F32)) * gain + shift).astype(BF)
        out = pl.ds(pl.multiple_of(slot * height + start, half // 2), half // 2)

        @pl.when(slot == REACH)
        def _():
            a_ref[spot, :] = attn

        query = (dot_nn(attn, wq[...]) + query_bias) * HEAD_DIM**-0.5
        key = dot_nn(attn, wk[...])
        q_ref[out, :] = query.astype(BF)
        k_ref[out, :] = key.astype(BF)
        raise_norm(slice(0, 8), query)
        raise_norm(slice(8, 16), key)
        v_ref[out, :] = (dot_nn(attn, wv[...]) + value_bias).astype(BF)

    def pass_on(p):
        for side in (0, 1):

            @pl.when(exists[side])
            def _():
                x_copy(side, p).wait_recv()
                y_copy(side, p).start()

            @pl.when(jnp.logical_and(exists[side], core == 1 - side))
            def _():
                f_copy(0, p).start()

        if p + AHEAD < PIECES:
            send(p + AHEAD)

    for copy in loads:
        copy.wait()

    low, high = range(PIECES // 2), range(PIECES // 2, PIECES)

    def forwarded(which, pieces):
        for side in (0, 1):

            @pl.when(jnp.logical_and(exists[side], core == side))
            def _():
                for p in pieces:
                    f_copy(which, p).wait_recv()

    def crossed(pieces):
        for p in pieces:
            for side in (0, 1):

                @pl.when(exists[side])
                def _():
                    y_copy(side, p).wait_recv()

                @pl.when(jnp.logical_and(exists[side], core == 1 - side))
                def _():
                    f_copy(1, p).start()

    def own_arrived():
        own_copy.wait_recv()
        w_copy.wait_recv()
        wf_copy.start()

    waits = {
        3: [lambda: pass_on(0)],
        4: [own_arrived],
        6: [lambda: pass_on(1)],
        8: [lambda: pass_on(2)] + [lambda p=p: pass_on(p) for p in range(3, PIECES // 2)],
        10: [lambda: forwarded(0, low)],
        11: [lambda: pass_on(high[0]), lambda: crossed(low)],
        13: [lambda: pass_on(high[1]), lambda: forwarded(1, low)],
        14: [lambda p=p: pass_on(p) for p in high[2:]],
        16: [lambda: forwarded(0, high)],
        17: [lambda: crossed(high)],
        19: [lambda: forwarded(1, high)],
    }
    left, right = has_left.astype(jnp.int32), has_right.astype(jnp.int32)
    near = (1 - core) * left + core * right

    def quarter(i, carry):
        for at, acts in waits.items():

            @pl.when(i == at)
            def _():
                for act in acts:
                    act()

        turn = (i - 8) // 3
        place_in = i - 8 - 3 * turn
        late = (i >= 8).astype(jnp.int32)
        second = (i >= 4).astype(jnp.int32)
        first, middle = (place_in == 0).astype(jnp.int32), (place_in == 1).astype(jnp.int32)
        third = 1 - first - middle
        early_slot = (1 - second) * REACH + second * (3 - 2 * core)
        late_slot = middle * 2 * REACH + third * (1 + 2 * core)
        slot = (1 - late) * early_slot + late * late_slot
        there = first * left + middle * right + third * near
        odd = turn - 2 * (turn // 2)
        late_part = 2 * ((1 - odd) * t + odd * (1 - t)) + turn // 2
        part_of = (1 - late) * (i - 4 * second) + late * late_part

        @pl.when((1 - late) + late * there == 1)
        def _():
            project(slot, part_of * (half // 2))

        return carry

    lax.fori_loop(0, 20, quarter, 0)
    wf_copy.wait_recv()
    for copy in (own_copy, w_copy, wf_copy):
        copy.wait_send()
    for p in range(PIECES):
        for side in (0, 1):

            @pl.when(exists[1 - side])
            def _():
                x_copy(side, p).wait_send()

            @pl.when(exists[side])
            def _():
                y_copy(side, p).wait_send()

            @pl.when(jnp.logical_and(exists[side], core == 1 - side))
            def _():
                f_copy(0, p).wait_send()
                f_copy(1, p).wait_send()


def halo_qkv(x, wo, wq, wk, wv, vec, labels):
    height, width = x.shape
    cols = wq.shape[1]
    blocks = 2 * REACH + 1
    shape = jax.ShapeDtypeStruct
    wide = shape((blocks * height, cols), BF)
    pair = DMA((2, PIECES))
    return pl.pallas_call(
        halo_kernel,
        out_shape=(
            wide, wide, wide, shape((height, width), BF), shape((2 * wo.shape[0], wo.shape[1]), BF),
            shape((16, 128), F32), shape((blocks * height, 128), BF),
        ),
        in_specs=[far()] * 5 + [whole()] * 2,
        out_specs=[whole()] * 7,
        scratch_shapes=[pltpu.VMEM((blocks, height, width), BF)]
        + [pltpu.VMEM(wq.shape, BF)] * 3
        + [DMA((5,)), pair, pair, pair, pair, DMA, DMA, pair, pair, DMA, DMA, DMA, DMA],
        compiler_params=pltpu.CompilerParams(
            collective_id=0, has_side_effects=True, vmem_limit_bytes=VMEM_BYTES
        ),
        name="halo_qkv",
    )(*[in_hbm(value) for value in (x, wo, wq, wk, wv)], vec, labels)


def split3(values):
    first = values.astype(BF).astype(F32)
    second = (values - first).astype(BF).astype(F32)
    return first, second, values - first - second


def code_tile(rows, keys_code):
    count = rows.shape[1]
    terms = split3(-rows)
    lane = lax.broadcasted_iota(jnp.int32, (128, count), 0)
    tall = jnp.zeros((128, count), F32)
    for h in range(8):
        for base, row in ((LOGS, h), (CENTRES, 8 + h)):
            for i in range(3):
                tall = jnp.where(lane == base + 3 * h + i, terms[i][row : row + 1], tall)
    wide = jnp.transpose(tall)
    column = lax.broadcasted_iota(jnp.int32, wide.shape, 1)
    same = jnp.logical_and(column < CLIPS, keys_code.astype(F32) == 0.0)
    return jnp.where(same, 1.0, wide).astype(BF)


def tile_at(j):
    return pl.ds(pl.multiple_of(j * TILE, TILE), TILE)


def lanes_of(c):
    return pl.ds(c * 128, 128)


def beside(left, right):
    return jnp.concatenate([left, right], axis=1)


def stacked_heads(values, codes):
    lower = lax.broadcasted_iota(jnp.int32, values.shape, 1) < HEAD_DIM
    none = jnp.zeros_like(values)
    return jnp.concatenate(
        [beside(jnp.where(lower, values, none), codes[0]), beside(jnp.where(lower, none, values), codes[1])],
        axis=0,
    )


def heads_out(turned):
    pair = jnp.concatenate([turned[:HEAD_DIM, :TILE], turned[HEAD_DIM:, TILE:]], axis=0)
    return jnp.transpose(pair)


def within(lane, start):
    return jnp.logical_and(lane >= start, lane < start + 3)


def attfinish_kernel(b_ref, q_ref, k_ref, v_ref, kc_ref, n_ref, o_ref, lse_ref, r_ref, m_ref, l_ref, acc_ref):
    height, cols = o_ref.shape
    pairs, tiles = cols // 128, height // TILE
    steep = jnp.logical_not(jnp.max(n_ref[0:8, :]) * jnp.max(n_ref[8:16, :]) <= SAFE * SAFE)
    lane = lax.broadcasted_iota(jnp.int32, (TILE, 128), 1)

    def groups(values):
        return values.reshape(TILE // 8, 8, values.shape[1])

    def one(i, carry):
        lo, hi = b_ref[0, i], b_ref[1, i]
        own = pl.ds(pl.multiple_of(REACH * height + i * TILE, TILE), TILE)
        same = jnp.logical_and(lane < CLIPS, kc_ref[own, :].astype(F32) == 0.0)
        code = jnp.where(same, 1.0, 0.0).astype(BF)
        for c in range(pairs):
            r_ref[c] = stacked_heads(q_ref[own, lanes_of(c)], (code, code))
        acc_ref[...] = jnp.zeros(acc_ref.shape, F32)
        l_ref[...] = jnp.zeros(l_ref.shape, F32)
        m_ref[...] = jnp.zeros(m_ref.shape, F32)

        def score(j, c):
            return dot_nt(beside(k_ref[tile_at(j), lanes_of(c)], kc_ref[tile_at(j), :]), r_ref[c])

        def step(shift, j, carry):
            raised = []
            for c in range(pairs):
                s = score(j, c)
                e = jnp.exp(s - m_ref[c, 0:1, :] if shift else s)
                l_ref[c] += jnp.sum(groups(e), axis=0)
                raised.append(e.astype(BF))
            for c in range(pairs):
                acc_ref[c] += dot_tn(v_ref[tile_at(j), lanes_of(c)], raised[c])
            return carry

        @pl.when(jnp.logical_not(steep))
        def _():
            lax.fori_loop(lo, hi, functools.partial(step, False), 0)

        @pl.when(steep)
        def _():
            m_ref[...] = jnp.full(m_ref.shape, NEG, F32)

            def peak(j, carry):
                for c in range(pairs):
                    m_ref[c] = jnp.maximum(m_ref[c], jnp.max(groups(score(j, c)), axis=0))
                return carry

            lax.fori_loop(lo, hi, peak, 0)
            for c in range(pairs):
                m_ref[c] = jnp.broadcast_to(jnp.max(m_ref[c], axis=0, keepdims=True), m_ref.shape[1:])
            lax.fori_loop(lo, hi, functools.partial(step, True), 0)

        for c in range(pairs):
            total = jnp.sum(l_ref[c], axis=0, keepdims=True)
            o_ref[tile_at(i), lanes_of(c)] = heads_out(acc_ref[c] / total).astype(BF)
            logs = m_ref[c, 0:1, :] + jnp.log(total)
            lse_ref[2 * c : 2 * c + 1, tile_at(i)] = logs[:, :TILE]
            lse_ref[2 * c + 1 : 2 * c + 2, tile_at(i)] = logs[:, TILE:]
        return carry

    lse_ref[...] = jnp.zeros(lse_ref.shape, F32)
    lax.fori_loop(0, tiles, one, 0)


def local_call(kernel, name, out_shape, scratch, bounds, *values):
    grid = pltpu.PrefetchScalarGridSpec(
        num_scalar_prefetch=1,
        grid=(1,),
        in_specs=[whole()] * len(values),
        out_specs=jax.tree.map(lambda _: whole(), out_shape),
        scratch_shapes=scratch,
    )
    return pl.pallas_call(
        kernel,
        grid_spec=grid,
        out_shape=out_shape,
        compiler_params=pltpu.CompilerParams(vmem_limit_bytes=VMEM_BYTES),
        name=name,
    )(bounds, *values)


def attend(bounds, q, k, v, kc, norms, height):
    cols = k.shape[1]
    pairs = cols // 128
    out_shape = (jax.ShapeDtypeStruct((height, cols), BF), jax.ShapeDtypeStruct((8, height), F32))
    scratch = [
        pltpu.VMEM((pairs, 2 * TILE, 256), BF),
        pltpu.VMEM((pairs, 8, 2 * TILE), F32),
        pltpu.VMEM((pairs, 8, 2 * TILE), F32),
        pltpu.VMEM((pairs, 128, 2 * TILE), F32),
    ]
    return local_call(attfinish_kernel, "attend", out_shape, scratch, bounds, q, k, v, kc, norms)


def query_back_kernel(b_ref, q_ref, k_ref, v_ref, g_ref, kc_ref, qc_ref, dq_ref, r_ref, t_ref, acc_ref):
    height, cols = dq_ref.shape
    pairs, tiles = cols // 128, height // TILE
    lane = lax.broadcasted_iota(jnp.int32, (TILE, 128), 1)

    def one(i, carry):
        own = pl.ds(pl.multiple_of(REACH * height + i * TILE, TILE), TILE)
        code = qc_ref[own, :]
        none = jnp.zeros_like(code)
        for c in range(pairs):
            logs, centres = [], []
            for h in (2 * c, 2 * c + 1):
                logs.append(jnp.where(jnp.logical_or(lane < CLIPS, within(lane, LOGS + 3 * h)), code, none))
                centres.append(jnp.where(within(lane, CENTRES + 3 * h), code, none))
            r_ref[c] = stacked_heads(q_ref[own, lanes_of(c)], logs)
            t_ref[c] = stacked_heads(g_ref[own, lanes_of(c)], centres)
        acc_ref[...] = jnp.zeros(acc_ref.shape, F32)

        def step(j, carry):
            code = kc_ref[tile_at(j), :]
            steps = []
            for c in range(pairs):
                probs = jnp.exp(dot_nt(beside(k_ref[tile_at(j), lanes_of(c)], code), r_ref[c]))
                d_probs = dot_nt(beside(v_ref[tile_at(j), lanes_of(c)], code), t_ref[c])
                steps.append((probs * d_probs).astype(BF))
            for c in range(pairs):
                acc_ref[c] += dot_tn(k_ref[tile_at(j), lanes_of(c)], steps[c])
            return carry

        lax.fori_loop(b_ref[0, i], b_ref[1, i], step, 0)
        for c in range(pairs):
            dq_ref[tile_at(i), lanes_of(c)] = (heads_out(acc_ref[c]) * HEAD_DIM**-0.5).astype(BF)
        return carry

    lax.fori_loop(0, tiles, one, 0)


def query_back(bounds, q, k, v, g, kc, qc, height):
    cols = k.shape[1]
    pairs = cols // 128
    scratch = [pltpu.VMEM((pairs, 2 * TILE, 256), BF)] * 2 + [pltpu.VMEM((pairs, 128, 2 * TILE), F32)]
    out_shape = jax.ShapeDtypeStruct((height, cols), BF)
    return local_call(query_back_kernel, "query_back", out_shape, scratch, bounds, q, k, v, g, kc, qc)


def key_back_kernel(b_ref, q_ref, k_ref, v_ref, g_ref, kc_ref, qc_ref, dk_ref, dv_ref, r_ref, t_ref, ak_ref, av_ref):
    height, cols = dk_ref.shape
    pairs, tiles = cols // 128, height // TILE
    lane = lax.broadcasted_iota(jnp.int32, (TILE, 128), 1)

    def one(i, carry):
        own = pl.ds(pl.multiple_of(REACH * height + i * TILE, TILE), TILE)
        code = kc_ref[own, :]
        none, ones = jnp.zeros_like(code), jnp.ones_like(code)
        for c in range(pairs):
            logs, centres = [], []
            for h in (2 * c, 2 * c + 1):
                logs.append(jnp.where(lane < CLIPS, code, jnp.where(within(lane, LOGS + 3 * h), ones, none)))
                centres.append(jnp.where(within(lane, CENTRES + 3 * h), ones, none))
            r_ref[c] = stacked_heads(k_ref[own, lanes_of(c)], logs)
            t_ref[c] = stacked_heads(v_ref[own, lanes_of(c)], centres)
        ak_ref[...] = jnp.zeros(ak_ref.shape, F32)
        av_ref[...] = jnp.zeros(av_ref.shape, F32)

        def step(j, carry):
            code = qc_ref[tile_at(j), :]
            weights, steps = [], []
            for c in range(pairs):
                probs = jnp.exp(dot_nt(beside(q_ref[tile_at(j), lanes_of(c)], code), r_ref[c]))
                d_probs = dot_nt(beside(g_ref[tile_at(j), lanes_of(c)], code), t_ref[c])
                weights.append(probs.astype(BF))
                steps.append((probs * d_probs).astype(BF))
            for c in range(pairs):
                av_ref[c] += dot_tn(g_ref[tile_at(j), lanes_of(c)], weights[c])
                ak_ref[c] += dot_tn(q_ref[tile_at(j), lanes_of(c)], steps[c])
            return carry

        lax.fori_loop(b_ref[0, i], b_ref[1, i], step, 0)
        for c in range(pairs):
            dk_ref[tile_at(i), lanes_of(c)] = heads_out(ak_ref[c]).astype(BF)
            dv_ref[tile_at(i), lanes_of(c)] = heads_out(av_ref[c]).astype(BF)
        return carry

    lax.fori_loop(0, tiles, one, 0)


def key_back(bounds, q, k, v, g, kc, qc, height):
    cols = k.shape[1]
    pairs = cols // 128
    scratch = [pltpu.VMEM((pairs, 2 * TILE, 256), BF)] * 2 + [pltpu.VMEM((pairs, 128, 2 * TILE), F32)] * 2
    out_shape = (jax.ShapeDtypeStruct((height, cols), BF),) * 2
    return local_call(key_back_kernel, "key_back", out_shape, scratch, bounds, q, k, v, g, kc, qc)


class Ring:
    def __init__(self):
        d = lax.axis_index("dp")
        n = lax.axis_size("dp") // 2
        chip = d // 2
        core = d - 2 * chip
        odd = chip - 2 * (chip // 2)
        spot = (1 - odd) * (chip // 2) + odd * (n - 1 - chip // 2)
        self.here = (1 - core) * spot + core * (n - 1 - spot)
        self.n, self.core, self.hops = n, core, n // 2
        self.sibling = {"dp": d + 1 - 2 * core}
        self.after = {"dp": self.device_at(self.wrap(self.here + 1))}
        self.before = {"dp": self.device_at(self.wrap(self.here - 1))}

    def wrap(self, index):
        return lax.rem(index + 2 * self.n, self.n)

    def device_at(self, rank):
        n, core = self.n, self.core
        walk = (1 - core) * rank + core * (n - 1 - rank)
        late = walk // (n // 2)
        return 2 * ((1 - late) * (2 * walk) + late * (2 * (n - walk) - 1)) + core

    def spans(self, shape, i, owner, j):
        rows, cols = shape[0] // 2, shape[1]
        wide = STRIPS * STRIP
        high, count = rows * cols // (self.n * wide), cols // wide
        line = j // count
        row = pl.multiple_of(owner * rows + line * high, high)
        col = pl.multiple_of((j - line * count) * wide + i * STRIP, STRIP)
        return pl.ds(row, high), pl.ds(col, STRIP)


def units(arrays):
    return [(a, i, pl.ds(i * STRIP, STRIP), a * STRIPS + i) for a in range(arrays) for i in range(STRIPS)]


class Reduce:
    def __init__(self, ring, given, sibs, bufs, sems):
        self.ring, self.given, self.sibs, self.bufs, self.sems = ring, given, sibs, bufs, sems
        self.units = units(len(given))

    def s_copy(self, a):
        rows = self.given[a].shape[0] // 2
        span = pl.ds(pl.multiple_of((1 - self.ring.core) * rows, rows), rows)
        return remote(
            self.given[a].at[span], self.sibs[a], self.sems[0].at[a], self.sems[1].at[a], self.ring.sibling
        )

    def ways(self):
        ring = self.ring
        return (
            (0, ring.hops, lambda s: ring.wrap(ring.here + ring.hops - s), ring.after),
            (ring.hops + 1, ring.hops - 1, lambda s: ring.wrap(ring.here - ring.hops + 1 + s), ring.before),
        )

    def r_copy(self, u, way, s):
        a, _, strip, e = u
        base, _, _, target = way
        k = (s if base == 0 else self.ring.hops + s)
        src, dst = self.bufs[a].at[base + s, :, strip], self.bufs[a].at[base + s + 1, :, strip]
        return remote(src, dst, self.sems[2].at[e, k], self.sems[3].at[e, k], target)

    def terms(self, u, j):
        a, i, _, _ = u
        shape, core = self.given[a].shape, self.ring.core
        mine = self.given[a][self.ring.spans(shape, i, core, j)].astype(F32)
        return mine + self.sibs[a][self.ring.spans(shape, i, 0, j)].astype(F32)

    def swap(self, a):
        self.s_copy(a).start()

    def first(self, a):
        self.s_copy(a).wait_recv()
        for u in self.units:
            if u[0] == a:
                for way in self.ways():
                    self.bufs[a][way[0], :, u[2]] = self.terms(u, way[2](0)).astype(BF)
                    self.r_copy(u, way, 0).start()

    def step(self, s, both=True):
        for u in self.units:
            a, _, strip, _ = u
            for way in self.ways()[: 2 if both else 1]:
                slot = way[0] + s
                local = self.terms(u, way[2](s))
                self.r_copy(u, way, s - 1).wait_recv()
                self.bufs[a][slot, :, strip] = (self.bufs[a][slot, :, strip].astype(F32) + local).astype(BF)
                self.r_copy(u, way, s).start()

    def turn(self):
        hops = self.ring.hops
        for u in self.units:
            a, _, strip, _ = u
            local = self.terms(u, self.ring.here)
            ahead, back = self.ways()
            self.r_copy(u, back, hops - 2).wait_recv()
            local = local + self.bufs[a][2 * hops, :, strip].astype(F32)
            self.r_copy(u, ahead, hops - 1).wait_recv()
            self.bufs[a][hops, :, strip] = (self.bufs[a][hops, :, strip].astype(F32) + local).astype(BF)

    def settle(self):
        for a in range(len(self.given)):
            self.s_copy(a).wait_send()
        for way in self.ways():

            def step(s, carry):
                for u in self.units:
                    self.r_copy(u, way, s).wait_send()
                return carry

            lax.fori_loop(0, way[1], step, 0)


class Gather:
    def __init__(self, ring, outs, sems):
        self.ring, self.outs, self.sems = ring, outs, sems
        self.units = units(len(outs))

    def spot(self, u, j):
        out, ring = self.outs[u[0]], self.ring
        return out.at[ring.spans(out.shape, u[1], ring.core, ring.wrap(ring.here + j))]

    def g_copy(self, u, way, s):
        ring = self.ring
        spot = self.spot(u, -s if way == 0 else s)
        k = s if way == 0 else ring.hops + s
        target = ring.after if way == 0 else ring.before
        return remote(spot, spot, self.sems[0].at[u[3], k], self.sems[1].at[u[3], k], target)

    def c_copy(self, u, way, s):
        spot = self.spot(u, -s if way == 0 else s)
        k = s if way == 0 else self.ring.hops + s
        return remote(spot, spot, self.sems[2].at[u[3], k], self.sems[3].at[u[3], k], self.ring.sibling)

    def begin(self, sources):
        for u in self.units:
            a, _, strip, _ = u
            self.spot(u, 0)[...] = sources[a][:, strip]
            self.g_copy(u, 0, 0).start()
            self.g_copy(u, 1, 0).start()
            self.c_copy(u, 0, 0).start()

    def step(self, s):
        for u in self.units:
            for way in (0, 1):
                self.g_copy(u, way, s - 1).wait_recv()
                self.g_copy(u, way, s).start()
                self.c_copy(u, way, s).start()

    def last(self):
        hops = self.ring.hops
        for u in self.units:
            self.g_copy(u, 0, hops - 2).wait_recv()
            self.g_copy(u, 0, hops - 1).start()
            self.c_copy(u, 0, hops - 1).start()
            self.g_copy(u, 1, hops - 2).wait_recv()
            self.c_copy(u, 1, hops - 1).start()
        for u in self.units:
            self.g_copy(u, 0, hops - 1).wait_recv()
            self.c_copy(u, 0, hops).start()

    def settle(self):
        hops = self.ring.hops
        for way in (0, 1):

            def sent(s, carry):
                for u in self.units:
                    self.g_copy(u, way, s).wait_send()
                return carry

            def copied(s, carry):
                for u in self.units:
                    self.c_copy(u, way, s).wait()
                return carry

            lax.fori_loop(0, hops - way, sent, 0)
            lax.fori_loop(way, hops + 1 - way, copied, 0)


def between(step, done, hops):
    def body(s, carry):
        step(s)
        return carry

    if done < hops - 1:
        lax.fori_loop(done, hops - 1, body, 0)


def chunk_rows(shape, n):
    return shape[0] * shape[1] // (2 * n * STRIPS * STRIP)


def reduce_scratch(shapes, n):
    count = len(shapes)
    sibs = [pltpu.VMEM((rows // 2, cols), BF) for rows, cols in shapes]
    bufs = [pltpu.VMEM((n + 1, chunk_rows(shape, n), STRIPS * STRIP), BF) for shape in shapes]
    return sibs + bufs, [DMA((count,))] * 2 + [DMA((count * STRIPS, n - 1))] * 2


def gather_sems(count, n):
    return [DMA((count * STRIPS, n - 1))] * 2 + [DMA((count * STRIPS, n))] * 2


def norm_back_rows(grad, values, gain):
    middle = jnp.mean(values, axis=-1, keepdims=True)
    centred = values - middle
    inverse = lax.rsqrt(jnp.mean(centred * centred, axis=-1, keepdims=True) + 1e-05)
    n = centred * inverse
    t = grad * gain
    back = (t - jnp.mean(t, axis=-1, keepdims=True) - n * jnp.mean(t * n, axis=-1, keepdims=True)) * inverse
    return back, grad * n


def column_sums(values):
    return jnp.sum(values, axis=0, keepdims=True)


def mid_kernel(
    x_ref, cot_ref, mix_ref, lse_ref, kc_ref, wof_ref, row_ref, w1_ref, w2_ref,
    xw_ref, qc_ref, rg_ref, low_ref, vec_ref, own1_ref, own2_ref, res_ref, outp_ref,
    om_ref, dact_ref, mi_ref, act_ref, pg_ref, part_ref, oth_ref, f1_ref, f2_ref, st_ref, sw_ref,
    sib1, sib2, buf1, buf2,
    sm, rm, sy, ry, sx, rx, ss, rs, sf, rf, *ring_sems,
):
    d, core, has_left, has_right = place()
    t = lax.axis_index("tensor")
    height, cols = mix_ref.shape
    width, hidden = w1_ref.shape
    rows = height // PARTS
    sibling = {"dp": d + 1 - 2 * core}
    across = {"tensor": 1 - t}
    exists = (has_left, has_right)
    slots = (0, 2 * REACH)
    ring = Ring()
    reduce = Reduce(ring, (f1_ref, f2_ref), (sib1, sib2), (buf1, buf2), ring_sems)
    hops = ring.hops
    greet([
        (None, sibling), (None, across), (has_left, {"dp": d - 2}), (has_right, {"dp": d + 2}),
        (None, ring.after), (None, ring.before),
    ])

    def span(p):
        return pl.ds(pl.multiple_of(p * rows, rows), rows)

    def m_copy(p):
        return remote(mix_ref.at[span(p)], om_ref.at[span(p)], sm.at[p], rm.at[p], across)

    def y_copy(p):
        return remote(part_ref.at[span(p)], oth_ref.at[span(p)], sy.at[p], ry.at[p], across)

    def refs(p):
        if p == PARTS:
            return st_ref, lambda slot: sw_ref.at[slot]
        return xw_ref.at[REACH, span(p)], lambda slot: xw_ref.at[slot, span(p)]

    def x_copy(side, p):
        src, dst = refs(p)
        return remote(
            src, dst(slots[side]), sx.at[side, p], rx.at[side, p],
            {"dp": d + 2 if side == 0 else d - 2},
        )

    def s_copy(p):
        src, dst = refs(p)
        return remote(src, dst(1 + 2 * core), ss.at[p], rs.at[p], sibling)

    def f_copy(p):
        _, dst = refs(p)
        return remote(dst(4 - 4 * core), dst(3 - 2 * core), sf.at[p], rf.at[p], sibling)

    def send(p):
        for side in (0, 1):

            @pl.when(exists[1 - side])
            def _():
                x_copy(side, p).start()

        s_copy(p).start()

    def pass_on(p):
        for side in (0, 1):

            @pl.when(exists[side])
            def _():
                x_copy(side, p).wait_recv()

            @pl.when(jnp.logical_and(exists[side], core == 1 - side))
            def _():
                f_copy(p).start()

    m_copy(0).start()
    vec = row_ref[...].astype(F32)
    out_bias, gain, shift = vec[3:4], vec[4:5], vec[5:6]
    heads = pl.ds(pl.multiple_of(t * cols, cols), cols)
    others = pl.ds(pl.multiple_of((1 - t) * cols, cols), cols)
    picks = lax.broadcasted_iota(jnp.int32, (8, cols), 1) // HEAD_DIM
    picks = (picks == lax.broadcasted_iota(jnp.int32, (8, cols), 0)).astype(F32)
    st_ref[0:8, :] = lse_ref[...]
    vec_ref[...] = jnp.zeros(vec_ref.shape, F32)

    def early(p, carry):
        cot = cot_ref[span(p), :]
        dact_ref[span(p), :] = dot_nt(cot, w2_ref[...])
        vec_ref[3:4, :] += column_sums(cot.astype(F32))
        res_ref[span(p), :] = x_ref[span(p), :].astype(F32) + dot_nn(mix_ref[span(p), :], wof_ref[heads, :]) + out_bias

        @pl.when(p == 0)
        def _():
            m_copy(1).start()

        return carry

    lax.fori_loop(0, PARTS, early, 0)

    def forward(p, carry):
        m_copy(p).wait_recv()

        @pl.when(p == 0)
        def _():
            m_copy(2).start()

        residual = res_ref[span(p), :] + dot_nn(om_ref[span(p), :], wof_ref[others, :])
        res_ref[span(p), :] = residual
        mlp_input = (norm_rows(residual) * gain + shift).astype(BF)
        mi_ref[span(p), :] = mlp_input
        for i in range(hidden // width):
            part = slice(i * width, (i + 1) * width)
            preact = dot_nn(mlp_input, w1_ref[:, part]) + vec[6 + i : 7 + i]
            cdf = 0.5 * (1.0 + lax.erf(preact * (2.0**-0.5)))
            pdf = jnp.exp(-0.5 * preact * preact) * 0.3989422804014327
            act_ref[span(p), part] = (preact * cdf).astype(BF)
            pre_grad = (dact_ref[span(p), part] * (cdf + preact * pdf)).astype(BF)
            pg_ref[span(p), part] = pre_grad
            vec_ref[4 + i : 5 + i, :] += column_sums(pre_grad.astype(F32))
        part_ref[span(p), :] = dot_nt(pg_ref[span(p), :], w1_ref[...]).astype(BF)
        y_copy(p).start()
        return carry

    lax.fori_loop(0, PARTS, forward, 0)

    def weights(which):
        half = pl.ds(pl.multiple_of(which * (width // 2), width // 2), width // 2)
        f1_ref[half, :] = dot_tn(mi_ref[:, half], pg_ref[...]).astype(BF)
        half = pl.ds(pl.multiple_of(which * (hidden // 2), hidden // 2), hidden // 2)
        f2_ref[half, :] = dot_tn(act_ref[:, half], cot_ref[...]).astype(BF)

    def back(p):
        y_copy(p).wait_recv()
        grad = part_ref[span(p), :].astype(F32) + oth_ref[span(p), :].astype(F32)
        turned, scaled = norm_back_rows(grad, res_ref[span(p), :], gain)
        total = cot_ref[span(p), :].astype(F32) + turned
        low = total.astype(BF)
        rg_ref[span(p), :] = total
        low_ref[span(p), :] = low
        vec_ref[0:1, :] += column_sums(scaled)
        vec_ref[1:2, :] += column_sums(grad)
        vec_ref[2:3, :] += column_sums(low.astype(F32))
        mixed_grad = dot_nt(low, wof_ref[heads, :]).astype(BF)
        xw_ref[REACH, span(p), :] = mixed_grad
        product = mixed_grad.astype(F32) * mix_ref[span(p), :].astype(F32)
        st_ref[8:16, p * rows : (p + 1) * rows] = lax.dot_general(
            picks, product, (((1,), (1,)), ((), ())),
            precision=lax.Precision.HIGHEST, preferred_element_type=F32,
        )

    def code(slot):
        def step(i, carry):
            spot = pl.ds(pl.multiple_of(slot * height + i * TILE, TILE), TILE)
            stats = sw_ref[slot, :, pl.ds(pl.multiple_of(i * TILE, TILE), TILE)]
            qc_ref[spot, :] = code_tile(stats, kc_ref[spot, :])
            return carry

        lax.fori_loop(0, height // TILE, step, 0)

    def ring_step(s):
        if s < hops - 1:
            reduce.step(s)

    back(0)
    send(0)
    weights(1 - core)
    reduce.swap(0)
    reduce.swap(1)
    back(1)
    send(1)
    weights(core)
    reduce.first(0)
    reduce.first(1)
    back(2)
    send(2)
    send(PARTS)
    sw_ref[REACH] = st_ref[...]
    ring_step(1)
    pass_on(0)
    outp_ref[...] = dot_nn(act_ref[...], w2_ref[...]).astype(BF)
    ring_step(2)
    pass_on(1)
    between(reduce.step, 3, hops)
    reduce.step(hops - 1, False)
    pass_on(2)
    pass_on(PARTS)
    code(REACH)
    reduce.turn()
    own1_ref[...] = buf1[hops]
    own2_ref[...] = buf2[hops]
    for p in range(PARTS + 1):
        s_copy(p).wait()
        for side in (0, 1):

            @pl.when(exists[1 - side])
            def _():
                x_copy(side, p).wait_send()

            @pl.when(jnp.logical_and(exists[side], core == 1 - side))
            def _():
                f_copy(p).wait_send()

            @pl.when(jnp.logical_and(exists[side], core == side))
            def _():
                f_copy(p).wait_recv()

    code(3 - 2 * core)
    for side in (0, 1):

        @pl.when(exists[side])
        def _():
            code(slots[side])

        @pl.when(jnp.logical_and(exists[side], core == side))
        def _():
            code(1 + 2 * core)

    for p in range(PARTS):
        m_copy(p).wait_send()
        y_copy(p).wait_send()
    reduce.settle()


def mid(x, cot, mix, lse, kc, wof, vec, w1, w2):
    blocks = 2 * REACH + 1
    height, width = x.shape
    hidden = w1.shape[1]
    n = lax.axis_size("dp") // 2
    pair, line, some = DMA((2, PARTS + 1)), DMA((PARTS + 1,)), DMA((PARTS,))
    room, sems = reduce_scratch((w1.shape, w2.shape), n)
    shape = jax.ShapeDtypeStruct
    chunks = [shape((chunk_rows(w.shape, n), STRIPS * STRIP), BF) for w in (w1, w2)]
    return pl.pallas_call(
        mid_kernel,
        out_shape=(
            shape((blocks,) + mix.shape, BF), shape(kc.shape, BF), shape(x.shape, F32), shape(x.shape, BF),
            shape((16, width), F32), *chunks, shape(x.shape, F32), shape(x.shape, BF),
        ),
        in_specs=[whole()] * 9,
        out_specs=[whole()] * 9,
        scratch_shapes=[
            pltpu.VMEM(mix.shape, BF), pltpu.VMEM((height, hidden), F32), pltpu.VMEM(x.shape, BF),
            pltpu.VMEM((height, hidden), BF), pltpu.VMEM((height, hidden), BF), pltpu.VMEM(x.shape, BF),
            pltpu.VMEM(x.shape, BF), pltpu.VMEM(w1.shape, BF), pltpu.VMEM(w2.shape, BF),
            pltpu.VMEM((16, height), F32), pltpu.VMEM((blocks, 16, height), F32),
        ]
        + room
        + [some, some, some, some, pair, pair, line, line, line, line]
        + sems,
        compiler_params=pltpu.CompilerParams(
            collective_id=1, has_side_effects=True, vmem_limit_bytes=MID_BYTES
        ),
        name="mid",
    )(x, cot, mix, lse, kc, wof, vec, w1, w2)


def finish_kernel(
    rounds, dq_ref, dk_ref, dv_ref, wq_ref, wk_ref, wv_ref, a_ref, low_ref, o_ref, x_ref, rg_ref, row_ref, vec_ref,
    own1_ref, own2_ref, res_hbm, outp_hbm, outo_hbm,
    ig_ref, g_ref, vs_ref, g1_ref, g2_ref, lo_ref,
    part_ref, oth_ref, own_ref, send_ref, got_ref, res_ref, outp_ref, outo_ref, sib, buf,
    load, sy, ry, sd, rd, *ring_sems,
):
    d, core, _, _ = place()
    t = lax.axis_index("tensor")
    height, cols = dq_ref.shape
    width = x_ref.shape[1]
    piece = height // PIECES
    across = {"tensor": 1 - t}
    loads = [
        pltpu.make_async_copy(src, dst, load.at[i])
        for i, (src, dst) in enumerate(((res_hbm, res_ref), (outp_hbm, outp_ref), (outo_hbm, outo_ref)))
    ]
    for copy in loads:
        copy.start()
    ring = Ring()
    reduce = Reduce(ring, (own_ref,), (sib,), (buf,), ring_sems[:4])
    gather = Gather(ring, (g_ref,), ring_sems[4:8])
    wide = Gather(ring, (g1_ref, g2_ref), ring_sems[8:])
    hops = ring.hops
    partners = []
    for r in range(rounds):
        bit = (d // 2**r) - 2 * (d // 2 ** (r + 1))
        partners.append({"dp": d + 2**r * (1 - 2 * bit)})
    greet([(None, across), (None, ring.after), (None, ring.before)] + [(None, p) for p in partners])

    def y_copy(p):
        span = pl.ds(p * piece, piece)
        return remote(part_ref.at[span], oth_ref.at[span], sy.at[p], ry.at[p], across)

    def d_copy(r):
        return remote(send_ref.at[r], got_ref.at[r], sd.at[r], rd.at[r], partners[r])

    def share(p):
        span = pl.ds(p * piece, piece)
        part = dot_nt(dq_ref[span, :], wq_ref[...]) + dot_nt(dk_ref[span, :], wk_ref[...])
        part_ref[span, :] = (part + dot_nt(dv_ref[span, :], wv_ref[...])).astype(BF)

    def weights(which):
        span = pl.ds(pl.multiple_of(which * (width // 2), width // 2), width // 2)
        attn = a_ref[:, span]
        for i, ref in enumerate((dq_ref, dk_ref, dv_ref)):
            own_ref[span, i * cols : (i + 1) * cols] = dot_tn(attn, ref[...]).astype(BF)
        own_ref[span, 3 * cols : 4 * cols] = dot_tn(low_ref[:, span], o_ref[...]).astype(BF)

    def wide_step(s):
        if s < hops - 1:
            wide.step(s)

    wide.begin((own1_ref, own2_ref))
    weights(1 - core)
    reduce.swap(0)
    for p in range(AHEAD):
        share(p)
        y_copy(p).start()
    weights(core)
    wide_step(1)
    for p in range(AHEAD, PIECES):
        share(p)
    vec = row_ref[...].astype(F32)
    gain, fc2_bias = vec[0:1], vec[8:9]
    gains, shifts = [], []

    def back(p):
        span = pl.ds(p * piece, piece)
        y_copy(p).wait_recv()
        if p + AHEAD < PIECES:
            y_copy(p + AHEAD).start()
        grad = part_ref[span, :].astype(F32) + oth_ref[span, :].astype(F32)
        turned, scaled = norm_back_rows(grad, x_ref[span, :].astype(F32), gain)
        ig_ref[span, :] = rg_ref[span, :] + turned
        gains.append(column_sums(scaled))
        shifts.append(column_sums(grad))

    def reduce_step(s):
        if s < hops - 1:
            reduce.step(s)

    def gather_step(s):
        if s < hops - 1:
            gather.step(s)

    def layer_out(p):
        span = pl.ds(p * piece, piece)
        total = outp_ref[span, :].astype(F32) + outo_ref[span, :].astype(F32)
        lo_ref[span, :] = (res_ref[span, :] + total + fc2_bias).astype(BF)

    def double(s):
        if s < rounds:
            d_copy(s).wait_recv()
            total = send_ref[s] + got_ref[s]
            if s + 1 < rounds:
                send_ref[s + 1] = total
                d_copy(s + 1).start()
            else:
                vs_ref[...] = total

    reduce.first(0)
    back(0)
    wide_step(2)
    reduce_step(1)
    back(1)
    reduce_step(2)
    back(2)
    between(reduce.step, 3, hops)
    between(wide.step, 3, hops)
    reduce.step(hops - 1, False)
    back(3)
    wide.last()
    reduce.turn()
    gather.begin((buf.at[hops],))
    back(4)
    gather_step(1)
    back(5)
    send_ref[0] = vec_ref[...]
    send_ref[0, 6:7, 0:cols] = column_sums(dq_ref[...].astype(F32))
    send_ref[0, 6:7, cols : 2 * cols] = column_sums(dv_ref[...].astype(F32))
    send_ref[0, 7:8, :] = sum(gains[1:], gains[0])
    send_ref[0, 8:9, :] = sum(shifts[1:], shifts[0])
    d_copy(0).start()
    gather_step(2)
    for copy in loads:
        copy.wait()
    layer_out(0)
    double(0)
    layer_out(1)
    between(gather.step, 3, hops)
    double(1)
    layer_out(2)
    gather.last()
    double(2)
    layer_out(3)
    layer_out(4)
    layer_out(5)
    for s in range(3, rounds):
        double(s)
    for p in range(PIECES):
        y_copy(p).wait_send()
    for r in range(rounds):
        d_copy(r).wait_send()
    reduce.settle()
    wide.settle()
    gather.settle()


def finish(dq, dk, dv, wq, wk, wv, attn, low, o, x, rg, gain, vectors, own1, own2, res, outp, outo, shapes):
    height, cols = dq.shape
    width = x.shape[1]
    size = lax.axis_size("dp")
    rounds = size.bit_length() - 1
    n = size // 2
    weights = (width, 4 * cols)
    room, sems = reduce_scratch((weights,), n)
    shape = jax.ShapeDtypeStruct
    return pl.pallas_call(
        functools.partial(finish_kernel, rounds),
        out_shape=(
            shape((height, width), F32), shape(weights, BF), shape(vectors.shape, F32),
            *[shape(dims, BF) for dims in shapes], shape((height, width), BF),
        ),
        in_specs=[whole()] * 15 + [far()] * 3,
        out_specs=[whole()] * 6,
        scratch_shapes=[
            pltpu.VMEM((height, width), BF), pltpu.VMEM((height, width), BF), pltpu.VMEM(weights, BF),
            pltpu.VMEM((rounds,) + vectors.shape, F32), pltpu.VMEM((rounds,) + vectors.shape, F32),
            pltpu.VMEM((height, width), F32), pltpu.VMEM((height, width), BF), pltpu.VMEM((height, width), BF),
        ]
        + room
        + [DMA((3,)), DMA((PIECES,)), DMA((PIECES,)), DMA((rounds,)), DMA((rounds,))]
        + sems
        + gather_sems(1, n)
        + gather_sems(2, n),
        compiler_params=pltpu.CompilerParams(
            collective_id=2, has_side_effects=True, vmem_limit_bytes=FINISH_BYTES
        ),
        name="finish",
    )(dq, dk, dv, wq, wk, wv, attn, low, o, x, rg, gain, vectors, own1, own2, res, outp, outo)


def widen_kernel(a_ref, f1_ref, f2_ref, i_ref, l_ref, q_ref, k_ref, v_ref, o_ref, g1_ref, g2_ref, ig_ref, lo_ref):
    cols = q_ref.shape[1]
    for i, ref in enumerate((q_ref, k_ref, v_ref)):
        ref[...] = a_ref[:, i * cols : (i + 1) * cols].astype(F32)
    o_ref[...] = jnp.transpose(a_ref[:, 3 * cols :].astype(F32))
    g1_ref[...] = f1_ref[...].astype(F32)
    g2_ref[...] = f2_ref[...].astype(F32)
    ig_ref[...] = i_ref[...]
    lo_ref[...] = l_ref[...]


def widen(attn, f1, f2, ig, lo):
    width = attn.shape[0]
    cols, steps = attn.shape[1] // 4, width // 128
    shape = jax.ShapeDtypeStruct

    def block(array):
        return pl.BlockSpec((array.shape[0] // steps, array.shape[1]), lambda i: (i, 0))

    thin = shape((width, cols), F32)
    outs = (
        thin, thin, thin, shape((cols, width), F32), shape(f1.shape, F32), shape(f2.shape, F32),
        shape(ig.shape, ig.dtype), shape(lo.shape, lo.dtype),
    )
    return pl.pallas_call(
        widen_kernel,
        grid=(steps,),
        out_shape=outs,
        in_specs=[block(attn), block(f1), block(f2), block(ig), block(lo)],
        out_specs=[block(thin)] * 3
        + [pl.BlockSpec((cols, 128), lambda i: (0, i)), block(f1), block(f2), block(ig), block(lo)],
        compiler_params=pltpu.CompilerParams(vmem_limit_bytes=WIDEN_BYTES),
        name="widen",
    )(attn, f1, f2, ig, lo)


def swapped(value):
    return lax.ppermute(value, "tensor", [(0, 1), (1, 0)])


def on_device(
    inputs, clip_ids, attn_gain, attn_shift, w_query, query_bias, w_key, w_value, value_bias,
    w_out, out_bias, mlp_gain, mlp_shift, w_fc1, fc1_bias, w_fc2, fc2_bias, cotangent,
):
    height = inputs.shape[0]
    d = lax.axis_index("dp")
    reach = REACH * height
    cols = w_query.shape[1]

    padded = jnp.pad(clip_ids, (reach, 0), constant_values=-1)
    padded = jnp.pad(padded, (0, reach), constant_values=1 << 20)
    window = lax.dynamic_slice_in_dim(padded, d * height, height + 2 * reach)
    own = window[reach : reach + height]
    firsts, lasts = own[::TILE], own[TILE - 1 :: TILE]
    begin = jnp.sum((window[None, :] < firsts[:, None]).astype(jnp.int32), axis=1)
    end = jnp.sum((window[None, :] <= lasts[:, None]).astype(jnp.int32), axis=1)
    bounds = jnp.stack([begin // TILE, (end + TILE - 1) // TILE])
    labels = window.astype(F32).reshape(-1, 128)
    split = jnp.pad(query_bias, (0, cols)) + jnp.pad(value_bias, (cols, 0))
    width = inputs.shape[1]
    rows = [attn_gain, attn_shift, split, out_bias, mlp_gain, mlp_shift, fc1_bias[:width], fc1_bias[width:], fc2_bias]
    line = lax.broadcasted_iota(jnp.int32, (16, width), 0)
    vec = jnp.zeros((16, width), BF)
    for i, values in enumerate(rows):
        vec = jnp.where(line == i, values[None, :], vec)

    q, k, v, attn_input, w_out_full, norms, key_code = halo_qkv(
        inputs, w_out, w_query, w_key, w_value, vec, labels
    )
    mixed, logs = attend(bounds, q, k, v, key_code, norms, height)
    grad_win, query_code, residual_grad, low, vectors, own1, own2, residual, out_part = mid(
        inputs, cotangent, mixed, logs, key_code, w_out_full, vec, w_fc1, w_fc2
    )
    grad_win = grad_win.reshape(-1, grad_win.shape[2])
    out_part, query_code = lax.optimization_barrier((out_part, query_code))
    out_other = swapped(out_part)
    query_low = query_back(bounds, q, k, v, grad_win, key_code, query_code, height)
    key_low, value_low = key_back(bounds, q, k, v, grad_win, key_code, query_code, height)
    out_other, key_low = lax.optimization_barrier((out_other, key_low))
    inputs_grad, attn_sum, sums, fc1_sum, fc2_sum, layer_out = finish(
        query_low, key_low, value_low, w_query, w_key, w_value, attn_input, low, mixed, inputs,
        residual_grad, vec, vectors, own1, own2, residual, out_part, out_other, (w_fc1.shape, w_fc2.shape),
    )
    q_grad, k_grad, v_grad, o_grad, fc1_grad, fc2_grad, inputs_grad, layer_out = widen(
        attn_sum, fc1_sum, fc2_sum, inputs_grad, layer_out
    )
    sums, q_grad = lax.optimization_barrier((sums, q_grad))
    return (
        layer_out, inputs_grad, sums[7], sums[8],
        q_grad, sums[6, :cols], k_grad, v_grad, sums[6, cols:],
        o_grad, sums[2], sums[0], sums[1],
        fc1_grad, sums[4:6].reshape(-1), fc2_grad, sums[3],
    )


def solution(mesh):
    rows, cols, split, every = P("dp", None), P(None, "tensor"), P("tensor"), P()
    tall = P("tensor", None)
    in_specs = (
        rows, every, every, every, cols, split, cols, cols, split, tall, every, every, every,
        cols, split, tall, every, rows,
    )
    out_specs = (
        rows, rows, every, every, cols, split, cols, cols, split, tall, every, every, every,
        cols, split, tall, every,
    )
    return jax.shard_map(on_device, mesh=mesh, in_specs=in_specs, out_specs=out_specs, check_vma=False)
```

```python
import functools

import jax
import jax.numpy as jnp
from jax import lax
from jax.experimental import pallas as pl
from jax.experimental.pallas import tpu as pltpu
from jax.sharding import PartitionSpec as P

HEAD_DIM = 64
REACH = 2
TILE = 256
PIECES = 6
AHEAD = 2
NEG = -3e38
CLIPS = 49
LOGS = 49
CENTRES = 52
FAR = -(2.0**100)
SAFE = 40.0
BF = jnp.bfloat16
F32 = jnp.float32
MESH = pl.DeviceIdType.MESH
VMEM = pltpu.VMEM
VMEM_BYTES = 10_000_000
MID_BYTES = 28_000_000
FINISH_BYTES = 16_000_000
PARTS = 3
WIDEN_BYTES = 16_000_000
STRIP = 128
STRIPS = 3
DMA = pltpu.SemaphoreType.DMA


def dot_nn(left, right):
    return jnp.dot(left, right, preferred_element_type=F32)


def dot_tn(left, right):
    return lax.dot_general(left, right, (((0,), (0,)), ((), ())), preferred_element_type=F32)


def dot_nt(left, right):
    return lax.dot_general(left, right, (((1,), (1,)), ((), ())), preferred_element_type=F32)


def whole():
    return pl.BlockSpec(memory_space=VMEM)


def far():
    return pl.BlockSpec(memory_space=pltpu.HBM)


def in_hbm(value):
    return pltpu.with_memory_space_constraint(value, pltpu.HBM)


def remote(src, dst, send_sem, recv_sem, device):
    return pltpu.make_async_remote_copy(
        src_ref=src,
        dst_ref=dst,
        send_sem=send_sem,
        recv_sem=recv_sem,
        device_id=device,
        device_id_type=MESH,
    )


def place():
    d = lax.axis_index("dp")
    chip = d // 2
    core = d - 2 * chip
    has_left = chip > 0
    has_right = chip < lax.axis_size("dp") // 2 - 1
    return d, core, has_left, has_right


def greet(targets):
    barrier = pltpu.get_barrier_semaphore()
    count = 0
    for present, device in targets:
        if present is None:
            pl.semaphore_signal(barrier, inc=1, device_id=device, device_id_type=MESH)
            count = count + 1
        else:

            @pl.when(present)
            def _():
                pl.semaphore_signal(barrier, inc=1, device_id=device, device_id_type=MESH)

            count = count + present.astype(jnp.int32)
    pl.semaphore_wait(barrier, count)


def norm_rows(values):
    middle = jnp.mean(values, axis=-1, keepdims=True)
    centred = values - middle
    spread = jnp.mean(centred * centred, axis=-1, keepdims=True)
    return centred * lax.rsqrt(spread + 1e-05)


def halo_kernel(
    x_ref, wo_ref, wq_ref, wk_ref, wv_ref, vec_ref, lab_ref,
    q_ref, k_ref, v_ref, a_ref, wof_ref, n_ref, kc_ref,
    win, wq, wk, wv, load, sx, rx, sy, ry, ss, rs, sf, rf, sw, rw, sv, rv,
):
    d, core, has_left, has_right = place()
    t = lax.axis_index("tensor")
    height = x_ref.shape[0]
    cols = wq_ref.shape[1]
    half = height // 2
    piece = half // PIECES
    sibling = {"dp": d + 1 - 2 * core}
    across = {"tensor": 1 - t}
    exists = (has_left, has_right)
    slots = (0, 2 * REACH)
    part = wo_ref.shape[0] // 2
    wo_rows = pl.ds(pl.multiple_of(core * part, part), part)
    mine = pl.ds(pl.multiple_of(t * 2 * part, part), 2 * part)
    loads = [
        pltpu.make_async_copy(src, dst, load.at[i])
        for i, (src, dst) in enumerate(
            ((x_ref, win.at[REACH]), (wq_ref, wq), (wk_ref, wk), (wv_ref, wv), (wo_ref, wof_ref.at[mine]))
        )
    ]
    for copy in loads:
        copy.start()
    greet([(None, sibling), (None, across), (has_left, {"dp": d - 2}), (has_right, {"dp": d + 2})])

    def rows(which, p):
        return pl.ds(pl.multiple_of(which * half + p * piece, piece), piece)

    def x_copy(side, p):
        return remote(
            x_ref.at[rows(t, p)], win.at[slots[side], rows(t, p)], sx.at[side, p], rx.at[side, p],
            {"dp": d + 2 if side == 0 else d - 2},
        )

    def y_copy(side, p):
        spot = win.at[slots[side], rows(t, p)]
        return remote(spot, spot, sy.at[side, p], ry.at[side, p], across)

    def f_copy(which, p):
        span = rows(t if which == 0 else 1 - t, p)
        return remote(
            win.at[4 - 4 * core, span], win.at[3 - 2 * core, span], sf.at[which, p], rf.at[which, p],
            sibling,
        )

    own_copy = remote(x_ref, win.at[1 + 2 * core], ss, rs, sibling)

    def full_rows(which):
        return pl.ds(pl.multiple_of((2 * which + core) * part, part), part)

    w_copy = remote(wo_ref.at[wo_rows], wof_ref.at[full_rows(t)], sw, rw, across)
    wf_copy = remote(wof_ref.at[full_rows(1 - t)], wof_ref.at[full_rows(1 - t)], sv, rv, sibling)

    def send(p):
        for side in (0, 1):

            @pl.when(exists[1 - side])
            def _():
                x_copy(side, p).start()

    for p in range(AHEAD):
        send(p)
    w_copy.start()
    own_copy.start()
    vec = vec_ref[...].astype(F32)
    gain, shift = vec[0:1], vec[1:2]
    query_bias, value_bias = vec[2:3, :cols], vec[2:3, cols:]
    n_ref[...] = jnp.zeros(n_ref.shape, F32)

    def code(r, carry):
        labels = jnp.transpose(jnp.broadcast_to(lab_ref[pl.ds(r, 1), :], (128, 128)))
        lane = lax.broadcasted_iota(jnp.int32, (128, 128), 1)
        lane = lane - HEAD_DIM * (lane // HEAD_DIM)
        far = jnp.where(labels == lane.astype(F32), 0.0, FAR)
        kc_ref[pl.ds(pl.multiple_of(r * 128, 128), 128), :] = jnp.where(lane < CLIPS, far, 1.0).astype(BF)
        return carry

    lax.fori_loop(0, lab_ref.shape[0], code, 0)

    def raise_norm(spot, values):
        for c in range(cols // 128):
            span = values[:, c * 128 : c * 128 + 128]
            norm = jnp.max(jnp.sum(span * span, axis=1, keepdims=True), axis=0, keepdims=True)
            n_ref[spot, :] = jnp.maximum(n_ref[spot, :], norm)

    def project(slot, start):
        spot = pl.ds(pl.multiple_of(start, half // 2), half // 2)
        attn = (norm_rows(win[slot, spot, :].astype(F32)) * gain + shift).astype(BF)
        out = pl.ds(pl.multiple_of(slot * height + start, half // 2), half // 2)

        @pl.when(slot == REACH)
        def _():
            a_ref[spot, :] = attn

        query = (dot_nn(attn, wq[...]) + query_bias) * HEAD_DIM**-0.5
        key = dot_nn(attn, wk[...])
        q_ref[out, :] = query.astype(BF)
        k_ref[out, :] = key.astype(BF)
        raise_norm(slice(0, 8), query)
        raise_norm(slice(8, 16), key)
        v_ref[out, :] = (dot_nn(attn, wv[...]) + value_bias).astype(BF)

    def pass_on(p):
        for side in (0, 1):

            @pl.when(exists[side])
            def _():
                x_copy(side, p).wait_recv()
                y_copy(side, p).start()

            @pl.when(jnp.logical_and(exists[side], core == 1 - side))
            def _():
                f_copy(0, p).start()

        if p + AHEAD < PIECES:
            send(p + AHEAD)

    for copy in loads:
        copy.wait()

    low, high = range(PIECES // 2), range(PIECES // 2, PIECES)

    def forwarded(which, pieces):
        for side in (0, 1):

            @pl.when(jnp.logical_and(exists[side], core == side))
            def _():
                for p in pieces:
                    f_copy(which, p).wait_recv()

    def crossed(pieces):
        for p in pieces:
            for side in (0, 1):

                @pl.when(exists[side])
                def _():
                    y_copy(side, p).wait_recv()

                @pl.when(jnp.logical_and(exists[side], core == 1 - side))
                def _():
                    f_copy(1, p).start()

    def own_arrived():
        own_copy.wait_recv()
        w_copy.wait_recv()
        wf_copy.start()

    waits = {
        3: [lambda: pass_on(0)],
        4: [own_arrived],
        6: [lambda: pass_on(1)],
        8: [lambda: pass_on(2)] + [lambda p=p: pass_on(p) for p in range(3, PIECES // 2)],
        10: [lambda: forwarded(0, low)],
        11: [lambda: pass_on(high[0]), lambda: crossed(low)],
        13: [lambda: pass_on(high[1]), lambda: forwarded(1, low)],
        14: [lambda p=p: pass_on(p) for p in high[2:]],
        16: [lambda: forwarded(0, high)],
        17: [lambda: crossed(high)],
        19: [lambda: forwarded(1, high)],
    }
    left, right = has_left.astype(jnp.int32), has_right.astype(jnp.int32)
    near = (1 - core) * left + core * right

    def quarter(i, carry):
        for at, acts in waits.items():

            @pl.when(i == at)
            def _():
                for act in acts:
                    act()

        turn = (i - 8) // 3
        place_in = i - 8 - 3 * turn
        late = (i >= 8).astype(jnp.int32)
        second = (i >= 4).astype(jnp.int32)
        first, middle = (place_in == 0).astype(jnp.int32), (place_in == 1).astype(jnp.int32)
        third = 1 - first - middle
        early_slot = (1 - second) * REACH + second * (3 - 2 * core)
        late_slot = middle * 2 * REACH + third * (1 + 2 * core)
        slot = (1 - late) * early_slot + late * late_slot
        there = first * left + middle * right + third * near
        odd = turn - 2 * (turn // 2)
        late_part = 2 * ((1 - odd) * t + odd * (1 - t)) + turn // 2
        part_of = (1 - late) * (i - 4 * second) + late * late_part

        @pl.when((1 - late) + late * there == 1)
        def _():
            project(slot, part_of * (half // 2))

        return carry

    lax.fori_loop(0, 20, quarter, 0)
    wf_copy.wait_recv()
    for copy in (own_copy, w_copy, wf_copy):
        copy.wait_send()
    for p in range(PIECES):
        for side in (0, 1):

            @pl.when(exists[1 - side])
            def _():
                x_copy(side, p).wait_send()

            @pl.when(exists[side])
            def _():
                y_copy(side, p).wait_send()

            @pl.when(jnp.logical_and(exists[side], core == 1 - side))
            def _():
                f_copy(0, p).wait_send()
                f_copy(1, p).wait_send()


def halo_qkv(x, wo, wq, wk, wv, vec, labels):
    height, width = x.shape
    cols = wq.shape[1]
    blocks = 2 * REACH + 1
    shape = jax.ShapeDtypeStruct
    wide = shape((blocks * height, cols), BF)
    pair = DMA((2, PIECES))
    return pl.pallas_call(
        halo_kernel,
        out_shape=(
            wide, wide, wide, shape((height, width), BF), shape((2 * wo.shape[0], wo.shape[1]), BF),
            shape((16, 128), F32), shape((blocks * height, 128), BF),
        ),
        in_specs=[far()] * 5 + [whole()] * 2,
        out_specs=[whole()] * 7,
        scratch_shapes=[pltpu.VMEM((blocks, height, width), BF)]
        + [pltpu.VMEM(wq.shape, BF)] * 3
        + [DMA((5,)), pair, pair, pair, pair, DMA, DMA, pair, pair, DMA, DMA, DMA, DMA],
        compiler_params=pltpu.CompilerParams(
            collective_id=0, has_side_effects=True, vmem_limit_bytes=VMEM_BYTES
        ),
        name="halo_qkv",
    )(*[in_hbm(value) for value in (x, wo, wq, wk, wv)], vec, labels)


def split3(values):
    first = values.astype(BF).astype(F32)
    second = (values - first).astype(BF).astype(F32)
    return first, second, values - first - second


def free_lane(shape):
    lane = lax.broadcasted_iota(jnp.int32, shape, 1)
    return lane - HEAD_DIM * (lane // HEAD_DIM)


def clip_code(keys_code):
    same = jnp.logical_and(free_lane(keys_code.shape) < CLIPS, keys_code.astype(F32) == 0.0)
    return jnp.where(same, 1.0, 0.0)


def code_tile(rows, keys_code, cols):
    terms = jnp.concatenate(split3(-rows), axis=0).astype(BF)
    line = lax.broadcasted_iota(jnp.int32, (48, cols), 0)
    lane = lax.broadcasted_iota(jnp.int32, (48, cols), 1)
    term = line // 16
    row = line - 16 * term
    centre = row // 8
    head = row - 8 * centre
    pair = head // 2
    spot = 128 * pair + HEAD_DIM * (1 - (head - 2 * pair)) + LOGS + (CENTRES - LOGS) * centre + term
    picks = jnp.where(lane == spot, 1.0, 0.0).astype(BF)
    same = clip_code(keys_code)
    return (dot_tn(terms, picks) + jnp.concatenate([same] * (cols // 128), axis=1)).astype(BF)


def tile_at(j):
    return pl.ds(pl.multiple_of(j * TILE, TILE), TILE)


def lanes_of(c):
    return pl.ds(c * 128, 128)


def with_code(values, code):
    lower = lax.broadcasted_iota(jnp.int32, values.shape, 1) < HEAD_DIM
    return jnp.where(lower, values, code), jnp.where(lower, code, values)


def against(moving, still):
    return jnp.concatenate([dot_nt(moving[h], still[h * TILE : (h + 1) * TILE]) for h in (0, 1)], axis=1)


def add_heads(acc_ref, c, values, weights):
    turned = jnp.transpose(values)
    acc_ref[c, :HEAD_DIM] += dot_nn(turned[:HEAD_DIM], weights[:, :TILE])
    acc_ref[c, HEAD_DIM:] += dot_nn(turned[HEAD_DIM:], weights[:, TILE:])


def keep(code, low, high):
    lane = free_lane(code.shape)
    return jnp.where(jnp.logical_and(lane >= low, lane < high), code, jnp.zeros_like(code))


def attend_kernel(height, first, b_ref, q_ref, k_ref, v_ref, kc_ref, n_ref, o_ref, lse_ref, r_ref, m_ref, l_ref, acc_ref):
    cols = o_ref.shape[1]
    pairs, tiles = cols // 128, o_ref.shape[0] // TILE
    steep = jnp.logical_not(jnp.max(n_ref[0:8, :]) * jnp.max(n_ref[8:16, :]) <= SAFE * SAFE)
    def groups(values):
        return values.reshape(TILE // 8, 8, values.shape[1])

    def one(i, carry):
        lo, hi = b_ref[0, first + i], b_ref[1, first + i]
        own = pl.ds(pl.multiple_of(REACH * height + (first + i) * TILE, TILE), TILE)
        code = clip_code(kc_ref[own, :]).astype(BF)
        for c in range(pairs):
            r_ref[c] = jnp.concatenate(with_code(q_ref[own, lanes_of(c)], code), axis=0)
        acc_ref[...] = jnp.zeros(acc_ref.shape, F32)
        l_ref[...] = jnp.zeros(l_ref.shape, F32)
        m_ref[...] = jnp.zeros(m_ref.shape, F32)

        def score(j, c):
            return against(with_code(k_ref[tile_at(j), lanes_of(c)], kc_ref[tile_at(j), :]), r_ref[c])

        def step(shift, j, carry):
            raised = []
            for c in range(pairs):
                s = score(j, c)
                e = jnp.exp(s - m_ref[c, 0:1, :] if shift else s)
                l_ref[c] += jnp.sum(groups(e), axis=0)
                raised.append(e.astype(BF))
            for c in range(pairs):
                add_heads(acc_ref, c, v_ref[tile_at(j), lanes_of(c)], raised[c])
            return carry

        @pl.when(jnp.logical_not(steep))
        def _():
            lax.fori_loop(lo, hi, functools.partial(step, False), 0)

        @pl.when(steep)
        def _():
            m_ref[...] = jnp.full(m_ref.shape, NEG, F32)

            def peak(j, carry):
                for c in range(pairs):
                    m_ref[c] = jnp.maximum(m_ref[c], jnp.max(groups(score(j, c)), axis=0))
                return carry

            lax.fori_loop(lo, hi, peak, 0)
            for c in range(pairs):
                m_ref[c] = jnp.broadcast_to(jnp.max(m_ref[c], axis=0, keepdims=True), m_ref.shape[1:])
            lax.fori_loop(lo, hi, functools.partial(step, True), 0)

        for c in range(pairs):
            total = jnp.sum(l_ref[c], axis=0, keepdims=True)
            share = jnp.concatenate(
                [acc_ref[c, :HEAD_DIM] / total[:, :TILE], acc_ref[c, HEAD_DIM:] / total[:, TILE:]], axis=0
            )
            o_ref[tile_at(i), lanes_of(c)] = jnp.transpose(share).astype(BF)
            logs = m_ref[c, 0:1, :] + jnp.log(total)
            lse_ref[2 * c : 2 * c + 1, tile_at(i)] = logs[:, :TILE]
            lse_ref[2 * c + 1 : 2 * c + 2, tile_at(i)] = logs[:, TILE:]
        return carry

    lse_ref[...] = jnp.zeros(lse_ref.shape, F32)
    lax.fori_loop(0, tiles, one, 0)


def local_call(kernel, name, out_shape, scratch, bounds, *values):
    grid = pltpu.PrefetchScalarGridSpec(
        num_scalar_prefetch=1,
        grid=(1,),
        in_specs=[whole()] * len(values),
        out_specs=jax.tree.map(lambda _: whole(), out_shape),
        scratch_shapes=scratch,
    )
    return pl.pallas_call(
        kernel,
        grid_spec=grid,
        out_shape=out_shape,
        compiler_params=pltpu.CompilerParams(vmem_limit_bytes=VMEM_BYTES),
        name=name,
    )(bounds, *values)


def attend(bounds, q, k, v, kc, norms, height, first, count):
    cols = k.shape[1]
    pairs = cols // 128
    rows = count * TILE
    out_shape = (jax.ShapeDtypeStruct((rows, cols), BF), jax.ShapeDtypeStruct((8, rows), F32))
    scratch = [
        pltpu.VMEM((pairs, 2 * TILE, 128), BF),
        pltpu.VMEM((pairs, 8, 2 * TILE), F32),
        pltpu.VMEM((pairs, 8, 2 * TILE), F32),
        pltpu.VMEM((pairs, 128, TILE), F32),
    ]
    kernel = functools.partial(attend_kernel, height, first)
    return local_call(kernel, "attend", out_shape, scratch, bounds, q, k, v, kc, norms)


def query_back_kernel(b_ref, q_ref, k_ref, v_ref, g_ref, kc_ref, qc_ref, dq_ref, r_ref, t_ref, acc_ref):
    height, cols = dq_ref.shape
    pairs, tiles = cols // 128, height // TILE
    def one(i, carry):
        own = pl.ds(pl.multiple_of(REACH * height + i * TILE, TILE), TILE)
        for c in range(pairs):
            code = qc_ref[own, lanes_of(c)]
            logs, centres = keep(code, 0, CENTRES), keep(code, CENTRES, CENTRES + 3)
            r_ref[c] = jnp.concatenate(with_code(q_ref[own, lanes_of(c)], logs), axis=0)
            t_ref[c] = jnp.concatenate(with_code(g_ref[own, lanes_of(c)], centres), axis=0)
        acc_ref[...] = jnp.zeros(acc_ref.shape, F32)

        def step(j, carry):
            code = kc_ref[tile_at(j), :]
            steps = []
            for c in range(pairs):
                probs = jnp.exp(against(with_code(k_ref[tile_at(j), lanes_of(c)], code), r_ref[c]))
                d_probs = against(with_code(v_ref[tile_at(j), lanes_of(c)], code), t_ref[c])
                steps.append((probs * d_probs).astype(BF))
            for c in range(pairs):
                add_heads(acc_ref, c, k_ref[tile_at(j), lanes_of(c)], steps[c])
            return carry

        lax.fori_loop(b_ref[0, i], b_ref[1, i], step, 0)
        for c in range(pairs):
            dq_ref[tile_at(i), lanes_of(c)] = (jnp.transpose(acc_ref[c]) * HEAD_DIM**-0.5).astype(BF)
        return carry

    lax.fori_loop(0, tiles, one, 0)


def query_back(bounds, q, k, v, g, kc, qc, height):
    cols = k.shape[1]
    pairs = cols // 128
    scratch = [pltpu.VMEM((pairs, 2 * TILE, 128), BF)] * 2 + [pltpu.VMEM((pairs, 128, TILE), F32)]
    out_shape = jax.ShapeDtypeStruct((height, cols), BF)
    return local_call(query_back_kernel, "query_back", out_shape, scratch, bounds, q, k, v, g, kc, qc)


def key_back_kernel(b_ref, q_ref, k_ref, v_ref, g_ref, kc_ref, qc_ref, dk_ref, dv_ref, r_ref, t_ref, ak_ref, av_ref):
    height, cols = dk_ref.shape
    pairs, tiles = cols // 128, height // TILE
    def one(i, carry):
        own = pl.ds(pl.multiple_of(REACH * height + i * TILE, TILE), TILE)
        code = kc_ref[own, :]
        logs, centres = keep(code, 0, CENTRES), keep(code, CENTRES, CENTRES + 3)
        for c in range(pairs):
            r_ref[c] = jnp.concatenate(with_code(k_ref[own, lanes_of(c)], logs), axis=0)
            t_ref[c] = jnp.concatenate(with_code(v_ref[own, lanes_of(c)], centres), axis=0)
        ak_ref[...] = jnp.zeros(ak_ref.shape, F32)
        av_ref[...] = jnp.zeros(av_ref.shape, F32)

        def step(j, carry):
            weights, steps = [], []
            for c in range(pairs):
                code = qc_ref[tile_at(j), lanes_of(c)]
                probs = jnp.exp(against(with_code(q_ref[tile_at(j), lanes_of(c)], code), r_ref[c]))
                d_probs = against(with_code(g_ref[tile_at(j), lanes_of(c)], code), t_ref[c])
                weights.append(probs.astype(BF))
                steps.append((probs * d_probs).astype(BF))
            for c in range(pairs):
                add_heads(av_ref, c, g_ref[tile_at(j), lanes_of(c)], weights[c])
                add_heads(ak_ref, c, q_ref[tile_at(j), lanes_of(c)], steps[c])
            return carry

        lax.fori_loop(b_ref[0, i], b_ref[1, i], step, 0)
        for c in range(pairs):
            dk_ref[tile_at(i), lanes_of(c)] = jnp.transpose(ak_ref[c]).astype(BF)
            dv_ref[tile_at(i), lanes_of(c)] = jnp.transpose(av_ref[c]).astype(BF)
        return carry

    lax.fori_loop(0, tiles, one, 0)


def key_back(bounds, q, k, v, g, kc, qc, height):
    cols = k.shape[1]
    pairs = cols // 128
    scratch = [pltpu.VMEM((pairs, 2 * TILE, 128), BF)] * 2 + [pltpu.VMEM((pairs, 128, TILE), F32)] * 2
    out_shape = (jax.ShapeDtypeStruct((height, cols), BF),) * 2
    return local_call(key_back_kernel, "key_back", out_shape, scratch, bounds, q, k, v, g, kc, qc)


class Ring:
    def __init__(self):
        d = lax.axis_index("dp")
        n = lax.axis_size("dp") // 2
        chip = d // 2
        core = d - 2 * chip
        odd = chip - 2 * (chip // 2)
        spot = (1 - odd) * (chip // 2) + odd * (n - 1 - chip // 2)
        self.here = (1 - core) * spot + core * (n - 1 - spot)
        self.n, self.core, self.hops = n, core, n // 2
        self.sibling = {"dp": d + 1 - 2 * core}
        self.after = {"dp": self.device_at(self.wrap(self.here + 1))}
        self.before = {"dp": self.device_at(self.wrap(self.here - 1))}

    def wrap(self, index):
        return lax.rem(index + 2 * self.n, self.n)

    def device_at(self, rank):
        n, core = self.n, self.core
        walk = (1 - core) * rank + core * (n - 1 - rank)
        late = walk // (n // 2)
        return 2 * ((1 - late) * (2 * walk) + late * (2 * (n - walk) - 1)) + core

    def spans(self, shape, i, owner, j):
        rows, cols = shape[0] // 2, shape[1]
        wide = STRIPS * STRIP
        high, count = rows * cols // (self.n * wide), cols // wide
        line = j // count
        row = pl.multiple_of(owner * rows + line * high, high)
        col = pl.multiple_of((j - line * count) * wide + i * STRIP, STRIP)
        return pl.ds(row, high), pl.ds(col, STRIP)


def units(arrays):
    return [(a, i, pl.ds(i * STRIP, STRIP), a * STRIPS + i) for a in range(arrays) for i in range(STRIPS)]


class Reduce:
    def __init__(self, ring, given, sibs, bufs, sems):
        self.ring, self.given, self.sibs, self.bufs, self.sems = ring, given, sibs, bufs, sems
        self.units = units(len(given))

    def s_copy(self, a):
        rows = self.given[a].shape[0] // 2
        span = pl.ds(pl.multiple_of((1 - self.ring.core) * rows, rows), rows)
        return remote(
            self.given[a].at[span], self.sibs[a], self.sems[0].at[a], self.sems[1].at[a], self.ring.sibling
        )

    def ways(self):
        ring = self.ring
        return (
            (0, ring.hops, lambda s: ring.wrap(ring.here + ring.hops - s), ring.after),
            (ring.hops + 1, ring.hops - 1, lambda s: ring.wrap(ring.here - ring.hops + 1 + s), ring.before),
        )

    def r_copy(self, u, way, s):
        a, _, strip, e = u
        base, _, _, target = way
        k = (s if base == 0 else self.ring.hops + s)
        src, dst = self.bufs[a].at[base + s, :, strip], self.bufs[a].at[base + s + 1, :, strip]
        return remote(src, dst, self.sems[2].at[e, k], self.sems[3].at[e, k], target)

    def terms(self, u, j):
        a, i, _, _ = u
        shape, core = self.given[a].shape, self.ring.core
        mine = self.given[a][self.ring.spans(shape, i, core, j)].astype(F32)
        return mine + self.sibs[a][self.ring.spans(shape, i, 0, j)].astype(F32)

    def swap(self, a):
        self.s_copy(a).start()

    def first(self, a):
        self.s_copy(a).wait_recv()
        for u in self.units:
            if u[0] == a:
                for way in self.ways():
                    self.bufs[a][way[0], :, u[2]] = self.terms(u, way[2](0)).astype(BF)
                    self.r_copy(u, way, 0).start()

    def step(self, s, both=True):
        for u in self.units:
            a, _, strip, _ = u
            for way in self.ways()[: 2 if both else 1]:
                slot = way[0] + s
                local = self.terms(u, way[2](s))
                self.r_copy(u, way, s - 1).wait_recv()
                self.bufs[a][slot, :, strip] = (self.bufs[a][slot, :, strip].astype(F32) + local).astype(BF)
                self.r_copy(u, way, s).start()

    def turn(self):
        hops = self.ring.hops
        for u in self.units:
            a, _, strip, _ = u
            local = self.terms(u, self.ring.here)
            ahead, back = self.ways()
            self.r_copy(u, back, hops - 2).wait_recv()
            local = local + self.bufs[a][2 * hops, :, strip].astype(F32)
            self.r_copy(u, ahead, hops - 1).wait_recv()
            self.bufs[a][hops, :, strip] = (self.bufs[a][hops, :, strip].astype(F32) + local).astype(BF)

    def settle(self):
        for a in range(len(self.given)):
            self.s_copy(a).wait_send()
        for way in self.ways():

            def step(s, carry):
                for u in self.units:
                    self.r_copy(u, way, s).wait_send()
                return carry

            lax.fori_loop(0, way[1], step, 0)


class Gather:
    def __init__(self, ring, outs, sems):
        self.ring, self.outs, self.sems = ring, outs, sems
        self.units = units(len(outs))

    def spot(self, u, j):
        out, ring = self.outs[u[0]], self.ring
        return out.at[ring.spans(out.shape, u[1], ring.core, ring.wrap(ring.here + j))]

    def g_copy(self, u, way, s):
        ring = self.ring
        spot = self.spot(u, -s if way == 0 else s)
        k = s if way == 0 else ring.hops + s
        target = ring.after if way == 0 else ring.before
        return remote(spot, spot, self.sems[0].at[u[3], k], self.sems[1].at[u[3], k], target)

    def c_copy(self, u, way, s):
        spot = self.spot(u, -s if way == 0 else s)
        k = s if way == 0 else self.ring.hops + s
        return remote(spot, spot, self.sems[2].at[u[3], k], self.sems[3].at[u[3], k], self.ring.sibling)

    def begin(self, sources):
        for u in self.units:
            a, _, strip, _ = u
            self.spot(u, 0)[...] = sources[a][:, strip]
            self.g_copy(u, 0, 0).start()
            self.g_copy(u, 1, 0).start()
            self.c_copy(u, 0, 0).start()

    def step(self, s):
        for u in self.units:
            for way in (0, 1):
                self.g_copy(u, way, s - 1).wait_recv()
                self.g_copy(u, way, s).start()
                self.c_copy(u, way, s).start()

    def last(self):
        hops = self.ring.hops
        for u in self.units:
            self.g_copy(u, 0, hops - 2).wait_recv()
            self.g_copy(u, 0, hops - 1).start()
            self.c_copy(u, 0, hops - 1).start()
            self.g_copy(u, 1, hops - 2).wait_recv()
            self.c_copy(u, 1, hops - 1).start()
        for u in self.units:
            self.g_copy(u, 0, hops - 1).wait_recv()
            self.c_copy(u, 0, hops).start()

    def settle(self):
        hops = self.ring.hops
        for way in (0, 1):

            def sent(s, carry):
                for u in self.units:
                    self.g_copy(u, way, s).wait_send()
                return carry

            def copied(s, carry):
                for u in self.units:
                    self.c_copy(u, way, s).wait()
                return carry

            lax.fori_loop(0, hops - way, sent, 0)
            lax.fori_loop(way, hops + 1 - way, copied, 0)


def between(step, done, hops):
    def body(s, carry):
        step(s)
        return carry

    if done < hops - 1:
        lax.fori_loop(done, hops - 1, body, 0)


def chunk_rows(shape, n):
    return shape[0] * shape[1] // (2 * n * STRIPS * STRIP)


def reduce_scratch(shapes, n):
    count = len(shapes)
    sibs = [pltpu.VMEM((rows // 2, cols), BF) for rows, cols in shapes]
    bufs = [pltpu.VMEM((n + 1, chunk_rows(shape, n), STRIPS * STRIP), BF) for shape in shapes]
    return sibs + bufs, [DMA((count,))] * 2 + [DMA((count * STRIPS, n - 1))] * 2


def gather_sems(count, n):
    return [DMA((count * STRIPS, n - 1))] * 2 + [DMA((count * STRIPS, n))] * 2


def norm_back_rows(grad, values, gain):
    middle = jnp.mean(values, axis=-1, keepdims=True)
    centred = values - middle
    inverse = lax.rsqrt(jnp.mean(centred * centred, axis=-1, keepdims=True) + 1e-05)
    n = centred * inverse
    t = grad * gain
    back = (t - jnp.mean(t, axis=-1, keepdims=True) - n * jnp.mean(t * n, axis=-1, keepdims=True)) * inverse
    return back, grad * n


def column_sums(values):
    return jnp.sum(values, axis=0, keepdims=True)


def mid_kernel(
    x_ref, cot_ref, mixa_ref, mixb_ref, oma_ref, lsea_ref, lseb_ref, kc_ref, wof_ref, row_ref, w1_ref, w2_ref,
    xw_ref, qc_ref, rg_ref, low_ref, vec_ref, own1_ref, own2_ref, res_ref, outp_ref, mix_ref,
    om_ref, dact_ref, mi_ref, act_ref, pg_ref, part_ref, oth_ref, f1_ref, f2_ref, st_ref, sw_ref,
    sib1, sib2, buf1, buf2,
    sm, rm, sy, ry, sx, rx, ss, rs, sf, rf, *ring_sems,
):
    d, core, has_left, has_right = place()
    t = lax.axis_index("tensor")
    height, cols = mix_ref.shape
    width, hidden = w1_ref.shape
    rows = height // PARTS
    sibling = {"dp": d + 1 - 2 * core}
    across = {"tensor": 1 - t}
    exists = (has_left, has_right)
    slots = (0, 2 * REACH)
    ring = Ring()
    reduce = Reduce(ring, (f1_ref, f2_ref), (sib1, sib2), (buf1, buf2), ring_sems)
    hops = ring.hops
    greet([
        (None, sibling), (None, across), (has_left, {"dp": d - 2}), (has_right, {"dp": d + 2}),
        (None, ring.after), (None, ring.before),
    ])

    def span(p):
        return pl.ds(pl.multiple_of(p * rows, rows), rows)

    head = mixa_ref.shape[0]
    m_copy = remote(mixb_ref, om_ref.at[pl.ds(head, height - head)], sm, rm, across)

    def y_copy(p):
        return remote(part_ref.at[span(p)], oth_ref.at[span(p)], sy.at[p], ry.at[p], across)

    def refs(p):
        if p == PARTS:
            return st_ref, lambda slot: sw_ref.at[slot]
        return xw_ref.at[REACH, span(p)], lambda slot: xw_ref.at[slot, span(p)]

    def x_copy(side, p):
        src, dst = refs(p)
        return remote(
            src, dst(slots[side]), sx.at[side, p], rx.at[side, p],
            {"dp": d + 2 if side == 0 else d - 2},
        )

    def s_copy(p):
        src, dst = refs(p)
        return remote(src, dst(1 + 2 * core), ss.at[p], rs.at[p], sibling)

    def f_copy(p):
        _, dst = refs(p)
        return remote(dst(4 - 4 * core), dst(3 - 2 * core), sf.at[p], rf.at[p], sibling)

    def send(p):
        for side in (0, 1):

            @pl.when(exists[1 - side])
            def _():
                x_copy(side, p).start()

        s_copy(p).start()

    def pass_on(p):
        for side in (0, 1):

            @pl.when(exists[side])
            def _():
                x_copy(side, p).wait_recv()

            @pl.when(jnp.logical_and(exists[side], core == 1 - side))
            def _():
                f_copy(p).start()

    m_copy.start()
    mix_ref[:head, :] = mixa_ref[...]
    mix_ref[head:, :] = mixb_ref[...]
    om_ref[:head, :] = oma_ref[...]
    vec = row_ref[...].astype(F32)
    out_bias, gain, shift = vec[3:4], vec[4:5], vec[5:6]
    heads = pl.ds(pl.multiple_of(t * cols, cols), cols)
    others = pl.ds(pl.multiple_of((1 - t) * cols, cols), cols)
    picks = lax.broadcasted_iota(jnp.int32, (8, cols), 1) // HEAD_DIM
    picks = (picks == lax.broadcasted_iota(jnp.int32, (8, cols), 0)).astype(F32)
    st_ref[0:8, :head] = lsea_ref[...]
    st_ref[0:8, head:] = lseb_ref[...]
    vec_ref[...] = jnp.zeros(vec_ref.shape, F32)

    def early(p, carry):
        cot = cot_ref[span(p), :]
        dact_ref[span(p), :] = dot_nt(cot, w2_ref[...])
        vec_ref[3:4, :] += column_sums(cot.astype(F32))
        res_ref[span(p), :] = x_ref[span(p), :].astype(F32) + dot_nn(mix_ref[span(p), :], wof_ref[heads, :]) + out_bias
        return carry

    lax.fori_loop(0, PARTS, early, 0)

    def forward(p, carry):
        @pl.when((p + 1) * rows > head)
        def _():
            m_copy.wait_recv()

        residual = res_ref[span(p), :] + dot_nn(om_ref[span(p), :], wof_ref[others, :])
        res_ref[span(p), :] = residual
        mlp_input = (norm_rows(residual) * gain + shift).astype(BF)
        mi_ref[span(p), :] = mlp_input
        for i in range(hidden // width):
            part = slice(i * width, (i + 1) * width)
            preact = dot_nn(mlp_input, w1_ref[:, part]) + vec[6 + i : 7 + i]
            cdf = 0.5 * (1.0 + lax.erf(preact * (2.0**-0.5)))
            pdf = jnp.exp(-0.5 * preact * preact) * 0.3989422804014327
            act_ref[span(p), part] = (preact * cdf).astype(BF)
            pre_grad = (dact_ref[span(p), part] * (cdf + preact * pdf)).astype(BF)
            pg_ref[span(p), part] = pre_grad
            vec_ref[4 + i : 5 + i, :] += column_sums(pre_grad.astype(F32))
        part_ref[span(p), :] = dot_nt(pg_ref[span(p), :], w1_ref[...]).astype(BF)
        y_copy(p).start()
        return carry

    lax.fori_loop(0, PARTS, forward, 0)

    def weights(which):
        half = pl.ds(pl.multiple_of(which * (width // 2), width // 2), width // 2)
        f1_ref[half, :] = dot_tn(mi_ref[:, half], pg_ref[...]).astype(BF)
        half = pl.ds(pl.multiple_of(which * (hidden // 2), hidden // 2), hidden // 2)
        f2_ref[half, :] = dot_tn(act_ref[:, half], cot_ref[...]).astype(BF)

    def back(p):
        y_copy(p).wait_recv()
        grad = part_ref[span(p), :].astype(F32) + oth_ref[span(p), :].astype(F32)
        turned, scaled = norm_back_rows(grad, res_ref[span(p), :], gain)
        total = cot_ref[span(p), :].astype(F32) + turned
        low = total.astype(BF)
        rg_ref[span(p), :] = total
        low_ref[span(p), :] = low
        vec_ref[0:1, :] += column_sums(scaled)
        vec_ref[1:2, :] += column_sums(grad)
        vec_ref[2:3, :] += column_sums(low.astype(F32))
        mixed_grad = dot_nt(low, wof_ref[heads, :]).astype(BF)
        xw_ref[REACH, span(p), :] = mixed_grad
        product = mixed_grad.astype(F32) * mix_ref[span(p), :].astype(F32)
        st_ref[8:16, p * rows : (p + 1) * rows] = lax.dot_general(
            picks, product, (((1,), (1,)), ((), ())),
            precision=lax.Precision.HIGHEST, preferred_element_type=F32,
        )

    def code(slot):
        def step(i, carry):
            spot = pl.ds(pl.multiple_of(slot * height + i * TILE, TILE), TILE)
            stats = sw_ref[slot, :, pl.ds(pl.multiple_of(i * TILE, TILE), TILE)]
            qc_ref[spot, :] = code_tile(stats, kc_ref[spot, :], cols)
            return carry

        lax.fori_loop(0, height // TILE, step, 0)

    def ring_step(s):
        if s < hops - 1:
            reduce.step(s)

    back(0)
    send(0)
    weights(1 - core)
    reduce.swap(0)
    reduce.swap(1)
    back(1)
    send(1)
    weights(core)
    reduce.first(0)
    reduce.first(1)
    outp_ref[...] = dot_nn(act_ref[...], w2_ref[...]).astype(BF)
    ring_step(1)
    back(2)
    send(2)
    send(PARTS)
    sw_ref[REACH] = st_ref[...]
    pass_on(0)
    ring_step(2)
    pass_on(1)
    between(reduce.step, 3, hops)
    reduce.step(hops - 1, False)
    pass_on(2)
    pass_on(PARTS)
    code(REACH)
    reduce.turn()
    own1_ref[...] = buf1[hops]
    own2_ref[...] = buf2[hops]
    for p in range(PARTS + 1):
        s_copy(p).wait()
        for side in (0, 1):

            @pl.when(exists[1 - side])
            def _():
                x_copy(side, p).wait_send()

            @pl.when(jnp.logical_and(exists[side], core == 1 - side))
            def _():
                f_copy(p).wait_send()

            @pl.when(jnp.logical_and(exists[side], core == side))
            def _():
                f_copy(p).wait_recv()

    code(3 - 2 * core)
    for side in (0, 1):

        @pl.when(exists[side])
        def _():
            code(slots[side])

        @pl.when(jnp.logical_and(exists[side], core == side))
        def _():
            code(1 + 2 * core)

    for p in range(PARTS):
        y_copy(p).wait_send()
    m_copy.wait_send()
    reduce.settle()


def mid(x, cot, mixa, mixb, oma, lsea, lseb, kc, wof, vec, w1, w2):
    blocks = 2 * REACH + 1
    height, width = x.shape
    hidden = w1.shape[1]
    mix = jax.ShapeDtypeStruct((height, mixa.shape[1]), BF)
    n = lax.axis_size("dp") // 2
    pair, line, some = DMA((2, PARTS + 1)), DMA((PARTS + 1,)), DMA((PARTS,))
    room, sems = reduce_scratch((w1.shape, w2.shape), n)
    shape = jax.ShapeDtypeStruct
    chunks = [shape((chunk_rows(w.shape, n), STRIPS * STRIP), BF) for w in (w1, w2)]
    return pl.pallas_call(
        mid_kernel,
        out_shape=(
            shape((blocks,) + mix.shape, BF), shape((kc.shape[0], mix.shape[1]), BF), shape(x.shape, F32), shape(x.shape, BF),
            shape((16, width), F32), *chunks, shape(x.shape, F32), shape(x.shape, BF), mix,
        ),
        in_specs=[whole()] * 12,
        out_specs=[whole()] * 10,
        scratch_shapes=[
            pltpu.VMEM(mix.shape, BF), pltpu.VMEM((height, hidden), F32), pltpu.VMEM(x.shape, BF),
            pltpu.VMEM((height, hidden), BF), pltpu.VMEM((height, hidden), BF), pltpu.VMEM(x.shape, BF),
            pltpu.VMEM(x.shape, BF), pltpu.VMEM(w1.shape, BF), pltpu.VMEM(w2.shape, BF),
            pltpu.VMEM((16, height), F32), pltpu.VMEM((blocks, 16, height), F32),
        ]
        + room
        + [DMA, DMA, some, some, pair, pair, line, line, line, line]
        + sems,
        compiler_params=pltpu.CompilerParams(
            collective_id=1, has_side_effects=True, vmem_limit_bytes=MID_BYTES
        ),
        name="mid",
    )(x, cot, mixa, mixb, oma, lsea, lseb, kc, wof, vec, w1, w2)


def finish_kernel(
    rounds, dq_ref, dk_ref, dv_ref, wq_ref, wk_ref, wv_ref, a_ref, low_ref, o_ref, x_ref, rg_ref, row_ref, vec_ref,
    own1_ref, own2_ref, res_hbm, outp_hbm, outo_hbm,
    ig_ref, g_ref, vs_ref, g1_ref, g2_ref, lo_ref,
    part_ref, oth_ref, own_ref, send_ref, got_ref, res_ref, outp_ref, outo_ref, sib, buf,
    load, sy, ry, sd, rd, *ring_sems,
):
    d, core, _, _ = place()
    t = lax.axis_index("tensor")
    height, cols = dq_ref.shape
    width = x_ref.shape[1]
    piece = height // PIECES
    across = {"tensor": 1 - t}
    loads = [
        pltpu.make_async_copy(src, dst, load.at[i])
        for i, (src, dst) in enumerate(((res_hbm, res_ref), (outp_hbm, outp_ref), (outo_hbm, outo_ref)))
    ]
    for copy in loads:
        copy.start()
    ring = Ring()
    reduce = Reduce(ring, (own_ref,), (sib,), (buf,), ring_sems[:4])
    gather = Gather(ring, (g_ref,), ring_sems[4:8])
    wide = Gather(ring, (g1_ref, g2_ref), ring_sems[8:])
    hops = ring.hops
    partners = []
    for r in range(rounds):
        bit = (d // 2**r) - 2 * (d // 2 ** (r + 1))
        partners.append({"dp": d + 2**r * (1 - 2 * bit)})
    greet([(None, across), (None, ring.after), (None, ring.before)] + [(None, p) for p in partners])

    def y_copy(p):
        span = pl.ds(p * piece, piece)
        return remote(part_ref.at[span], oth_ref.at[span], sy.at[p], ry.at[p], across)

    def d_copy(r):
        return remote(send_ref.at[r], got_ref.at[r], sd.at[r], rd.at[r], partners[r])

    def share(p):
        span = pl.ds(p * piece, piece)
        part = dot_nt(dq_ref[span, :], wq_ref[...]) + dot_nt(dk_ref[span, :], wk_ref[...])
        part_ref[span, :] = (part + dot_nt(dv_ref[span, :], wv_ref[...])).astype(BF)

    def weights(which):
        span = pl.ds(pl.multiple_of(which * (width // 2), width // 2), width // 2)
        attn = a_ref[:, span]
        for i, ref in enumerate((dq_ref, dk_ref, dv_ref)):
            own_ref[span, i * cols : (i + 1) * cols] = dot_tn(attn, ref[...]).astype(BF)
        own_ref[span, 3 * cols : 4 * cols] = dot_tn(low_ref[:, span], o_ref[...]).astype(BF)

    def wide_step(s):
        if s < hops - 1:
            wide.step(s)

    wide.begin((own1_ref, own2_ref))
    weights(1 - core)
    reduce.swap(0)
    for p in range(AHEAD):
        share(p)
        y_copy(p).start()
    weights(core)
    wide_step(1)
    for p in range(AHEAD, PIECES):
        share(p)
    vec = row_ref[...].astype(F32)
    gain, fc2_bias = vec[0:1], vec[8:9]
    gains, shifts = [], []

    def back(p):
        span = pl.ds(p * piece, piece)
        y_copy(p).wait_recv()
        if p + AHEAD < PIECES:
            y_copy(p + AHEAD).start()
        grad = part_ref[span, :].astype(F32) + oth_ref[span, :].astype(F32)
        turned, scaled = norm_back_rows(grad, x_ref[span, :].astype(F32), gain)
        ig_ref[span, :] = rg_ref[span, :] + turned
        gains.append(column_sums(scaled))
        shifts.append(column_sums(grad))

    def reduce_step(s):
        if s < hops - 1:
            reduce.step(s)

    def gather_step(s):
        if s < hops - 1:
            gather.step(s)

    def layer_out(p):
        span = pl.ds(p * piece, piece)
        total = outp_ref[span, :].astype(F32) + outo_ref[span, :].astype(F32)
        lo_ref[span, :] = (res_ref[span, :] + total + fc2_bias).astype(BF)

    def double(s):
        if s < rounds:
            d_copy(s).wait_recv()
            total = send_ref[s] + got_ref[s]
            if s + 1 < rounds:
                send_ref[s + 1] = total
                d_copy(s + 1).start()
            else:
                vs_ref[...] = total

    reduce.first(0)
    back(0)
    wide_step(2)
    reduce_step(1)
    back(1)
    reduce_step(2)
    back(2)
    between(reduce.step, 3, hops)
    between(wide.step, 3, hops)
    reduce.step(hops - 1, False)
    back(3)
    wide.last()
    reduce.turn()
    gather.begin((buf.at[hops],))
    back(4)
    gather_step(1)
    back(5)
    send_ref[0] = vec_ref[...]
    send_ref[0, 6:7, 0:cols] = column_sums(dq_ref[...].astype(F32))
    send_ref[0, 6:7, cols : 2 * cols] = column_sums(dv_ref[...].astype(F32))
    send_ref[0, 7:8, :] = sum(gains[1:], gains[0])
    send_ref[0, 8:9, :] = sum(shifts[1:], shifts[0])
    d_copy(0).start()
    gather_step(2)
    for copy in loads:
        copy.wait()
    layer_out(0)
    double(0)
    layer_out(1)
    between(gather.step, 3, hops)
    double(1)
    layer_out(2)
    gather.last()
    double(2)
    layer_out(3)
    layer_out(4)
    layer_out(5)
    for s in range(3, rounds):
        double(s)
    for p in range(PIECES):
        y_copy(p).wait_send()
    for r in range(rounds):
        d_copy(r).wait_send()
    reduce.settle()
    wide.settle()
    gather.settle()


def finish(dq, dk, dv, wq, wk, wv, attn, low, o, x, rg, gain, vectors, own1, own2, res, outp, outo, shapes):
    height, cols = dq.shape
    width = x.shape[1]
    size = lax.axis_size("dp")
    rounds = size.bit_length() - 1
    n = size // 2
    weights = (width, 4 * cols)
    room, sems = reduce_scratch((weights,), n)
    shape = jax.ShapeDtypeStruct
    return pl.pallas_call(
        functools.partial(finish_kernel, rounds),
        out_shape=(
            shape((height, width), F32), shape(weights, BF), shape(vectors.shape, F32),
            *[shape(dims, BF) for dims in shapes], shape((height, width), BF),
        ),
        in_specs=[whole()] * 15 + [far()] * 3,
        out_specs=[whole()] * 6,
        scratch_shapes=[
            pltpu.VMEM((height, width), BF), pltpu.VMEM((height, width), BF), pltpu.VMEM(weights, BF),
            pltpu.VMEM((rounds,) + vectors.shape, F32), pltpu.VMEM((rounds,) + vectors.shape, F32),
            pltpu.VMEM((height, width), F32), pltpu.VMEM((height, width), BF), pltpu.VMEM((height, width), BF),
        ]
        + room
        + [DMA((3,)), DMA((PIECES,)), DMA((PIECES,)), DMA((rounds,)), DMA((rounds,))]
        + sems
        + gather_sems(1, n)
        + gather_sems(2, n),
        compiler_params=pltpu.CompilerParams(
            collective_id=2, has_side_effects=True, vmem_limit_bytes=FINISH_BYTES
        ),
        name="finish",
    )(dq, dk, dv, wq, wk, wv, attn, low, o, x, rg, gain, vectors, own1, own2, res, outp, outo)


def widen_kernel(a_ref, f1_ref, f2_ref, i_ref, l_ref, q_ref, k_ref, v_ref, o_ref, g1_ref, g2_ref, ig_ref, lo_ref):
    cols = q_ref.shape[1]
    for i, ref in enumerate((q_ref, k_ref, v_ref)):
        ref[...] = a_ref[:, i * cols : (i + 1) * cols].astype(F32)
    o_ref[...] = jnp.transpose(a_ref[:, 3 * cols :].astype(F32))
    g1_ref[...] = f1_ref[...].astype(F32)
    g2_ref[...] = f2_ref[...].astype(F32)
    ig_ref[...] = i_ref[...]
    lo_ref[...] = l_ref[...]


def widen(attn, f1, f2, ig, lo):
    width = attn.shape[0]
    cols, steps = attn.shape[1] // 4, width // 128
    shape = jax.ShapeDtypeStruct

    def block(array):
        return pl.BlockSpec((array.shape[0] // steps, array.shape[1]), lambda i: (i, 0))

    thin = shape((width, cols), F32)
    outs = (
        thin, thin, thin, shape((cols, width), F32), shape(f1.shape, F32), shape(f2.shape, F32),
        shape(ig.shape, ig.dtype), shape(lo.shape, lo.dtype),
    )
    return pl.pallas_call(
        widen_kernel,
        grid=(steps,),
        out_shape=outs,
        in_specs=[block(attn), block(f1), block(f2), block(ig), block(lo)],
        out_specs=[block(thin)] * 3
        + [pl.BlockSpec((cols, 128), lambda i: (0, i)), block(f1), block(f2), block(ig), block(lo)],
        compiler_params=pltpu.CompilerParams(vmem_limit_bytes=WIDEN_BYTES),
        name="widen",
    )(attn, f1, f2, ig, lo)


def swapped(value):
    return lax.ppermute(value, "tensor", [(0, 1), (1, 0)])


def on_device(
    inputs, clip_ids, attn_gain, attn_shift, w_query, query_bias, w_key, w_value, value_bias,
    w_out, out_bias, mlp_gain, mlp_shift, w_fc1, fc1_bias, w_fc2, fc2_bias, cotangent,
):
    height = inputs.shape[0]
    d = lax.axis_index("dp")
    reach = REACH * height
    cols = w_query.shape[1]

    padded = jnp.pad(clip_ids, (reach, 0), constant_values=-1)
    padded = jnp.pad(padded, (0, reach), constant_values=1 << 20)
    window = lax.dynamic_slice_in_dim(padded, d * height, height + 2 * reach)
    own = window[reach : reach + height]
    firsts, lasts = own[::TILE], own[TILE - 1 :: TILE]
    begin = jnp.sum((window[None, :] < firsts[:, None]).astype(jnp.int32), axis=1)
    end = jnp.sum((window[None, :] <= lasts[:, None]).astype(jnp.int32), axis=1)
    bounds = jnp.stack([begin // TILE, (end + TILE - 1) // TILE])
    labels = window.astype(F32).reshape(-1, 128)
    split = jnp.pad(query_bias, (0, cols)) + jnp.pad(value_bias, (cols, 0))
    width = inputs.shape[1]
    rows = [attn_gain, attn_shift, split, out_bias, mlp_gain, mlp_shift, fc1_bias[:width], fc1_bias[width:], fc2_bias]
    line = lax.broadcasted_iota(jnp.int32, (16, width), 0)
    vec = jnp.zeros((16, width), BF)
    for i, values in enumerate(rows):
        vec = jnp.where(line == i, values[None, :], vec)

    q, k, v, attn_input, w_out_full, norms, key_code = halo_qkv(
        inputs, w_out, w_query, w_key, w_value, vec, labels
    )
    most = height // TILE - 1
    mixed_a, logs_a = attend(bounds, q, k, v, key_code, norms, height, 0, most)
    other_a = swapped(mixed_a)
    mixed_a, bounds = lax.optimization_barrier((mixed_a, bounds))
    mixed_b, logs_b = attend(bounds, q, k, v, key_code, norms, height, most, 1)
    grad_win, query_code, residual_grad, low, vectors, own1, own2, residual, out_part, mixed = mid(
        inputs, cotangent, mixed_a, mixed_b, other_a, logs_a, logs_b, key_code, w_out_full, vec, w_fc1, w_fc2
    )
    grad_win = grad_win.reshape(-1, grad_win.shape[2])
    out_part, query_code = lax.optimization_barrier((out_part, query_code))
    out_other = swapped(out_part)
    query_low = query_back(bounds, q, k, v, grad_win, key_code, query_code, height)
    key_low, value_low = key_back(bounds, q, k, v, grad_win, key_code, query_code, height)
    out_other, key_low = lax.optimization_barrier((out_other, key_low))
    inputs_grad, attn_sum, sums, fc1_sum, fc2_sum, layer_out = finish(
        query_low, key_low, value_low, w_query, w_key, w_value, attn_input, low, mixed, inputs,
        residual_grad, vec, vectors, own1, own2, residual, out_part, out_other, (w_fc1.shape, w_fc2.shape),
    )
    q_grad, k_grad, v_grad, o_grad, fc1_grad, fc2_grad, inputs_grad, layer_out = widen(
        attn_sum, fc1_sum, fc2_sum, inputs_grad, layer_out
    )
    sums, q_grad = lax.optimization_barrier((sums, q_grad))
    return (
        layer_out, inputs_grad, sums[7], sums[8],
        q_grad, sums[6, :cols], k_grad, v_grad, sums[6, cols:],
        o_grad, sums[2], sums[0], sums[1],
        fc1_grad, sums[4:6].reshape(-1), fc2_grad, sums[3],
    )


def solution(mesh):
    rows, cols, split, every = P("dp", None), P(None, "tensor"), P("tensor"), P()
    tall = P("tensor", None)
    in_specs = (
        rows, every, every, every, cols, split, cols, cols, split, tall, every, every, every,
        cols, split, tall, every, rows,
    )
    out_specs = (
        rows, rows, every, every, cols, split, cols, cols, split, tall, every, every, every,
        cols, split, tall, every,
    )
    return jax.shard_map(on_device, mesh=mesh, in_specs=in_specs, out_specs=out_specs, check_vma=False)
```

```python
import functools

import jax
import jax.numpy as jnp
from jax import lax
from jax.experimental import pallas as pl
from jax.experimental.pallas import tpu as pltpu
from jax.sharding import PartitionSpec as P

HEAD_DIM = 64
REACH = 2
TILE = 256
PIECES = 6
AHEAD = 2
NEG = -3e38
CLIPS = 49
LOGS = 49
CENTRES = 52
FAR = -(2.0**100)
SAFE = 40.0
BF = jnp.bfloat16
F32 = jnp.float32
MESH = pl.DeviceIdType.MESH
VMEM = pltpu.VMEM
VMEM_BYTES = 10_000_000
MID_BYTES = 28_000_000
FINISH_BYTES = 16_000_000
PARTS = 3
WIDEN_BYTES = 16_000_000
STRIP = 128
STRIPS = 3
DMA = pltpu.SemaphoreType.DMA


def dot_nn(left, right):
    return jnp.dot(left, right, preferred_element_type=F32)


def dot_tn(left, right):
    return lax.dot_general(left, right, (((0,), (0,)), ((), ())), preferred_element_type=F32)


def dot_nt(left, right):
    return lax.dot_general(left, right, (((1,), (1,)), ((), ())), preferred_element_type=F32)


def whole():
    return pl.BlockSpec(memory_space=VMEM)


def far():
    return pl.BlockSpec(memory_space=pltpu.HBM)


def in_hbm(value):
    return pltpu.with_memory_space_constraint(value, pltpu.HBM)


def remote(src, dst, send_sem, recv_sem, device):
    return pltpu.make_async_remote_copy(
        src_ref=src,
        dst_ref=dst,
        send_sem=send_sem,
        recv_sem=recv_sem,
        device_id=device,
        device_id_type=MESH,
    )


def place():
    d = lax.axis_index("dp")
    chip = d // 2
    core = d - 2 * chip
    has_left = chip > 0
    has_right = chip < lax.axis_size("dp") // 2 - 1
    return d, core, has_left, has_right


def greet(targets):
    barrier = pltpu.get_barrier_semaphore()
    count = 0
    for present, device in targets:
        if present is None:
            pl.semaphore_signal(barrier, inc=1, device_id=device, device_id_type=MESH)
            count = count + 1
        else:

            @pl.when(present)
            def _():
                pl.semaphore_signal(barrier, inc=1, device_id=device, device_id_type=MESH)

            count = count + present.astype(jnp.int32)
    pl.semaphore_wait(barrier, count)


def norm_rows(values):
    middle = jnp.mean(values, axis=-1, keepdims=True)
    centred = values - middle
    spread = jnp.mean(centred * centred, axis=-1, keepdims=True)
    return centred * lax.rsqrt(spread + 1e-05)


def halo_kernel(
    x_ref, wo_ref, wq_ref, wk_ref, wv_ref, vec_ref, lab_ref,
    q_ref, k_ref, v_ref, a_ref, wof_ref, n_ref, kc_ref,
    win, wq, wk, wv, load, sx, rx, sy, ry, ss, rs, sf, rf, sw, rw, sv, rv,
):
    d, core, has_left, has_right = place()
    t = lax.axis_index("tensor")
    height = x_ref.shape[0]
    cols = wq_ref.shape[1]
    half = height // 2
    piece = half // PIECES
    sibling = {"dp": d + 1 - 2 * core}
    across = {"tensor": 1 - t}
    exists = (has_left, has_right)
    slots = (0, 2 * REACH)
    part = wo_ref.shape[0] // 2
    wo_rows = pl.ds(pl.multiple_of(core * part, part), part)
    mine = pl.ds(pl.multiple_of(t * 2 * part, part), 2 * part)
    loads = [
        pltpu.make_async_copy(src, dst, load.at[i])
        for i, (src, dst) in enumerate(
            ((x_ref, win.at[REACH]), (wq_ref, wq), (wk_ref, wk), (wv_ref, wv), (wo_ref, wof_ref.at[mine]))
        )
    ]
    for copy in loads:
        copy.start()
    greet([(None, sibling), (None, across), (has_left, {"dp": d - 2}), (has_right, {"dp": d + 2})])

    def rows(which, p):
        return pl.ds(pl.multiple_of(which * half + p * piece, piece), piece)

    def x_copy(side, p):
        return remote(
            x_ref.at[rows(t, p)], win.at[slots[side], rows(t, p)], sx.at[side, p], rx.at[side, p],
            {"dp": d + 2 if side == 0 else d - 2},
        )

    def y_copy(side, p):
        spot = win.at[slots[side], rows(t, p)]
        return remote(spot, spot, sy.at[side, p], ry.at[side, p], across)

    def f_copy(which, p):
        span = rows(t if which == 0 else 1 - t, p)
        return remote(
            win.at[4 - 4 * core, span], win.at[3 - 2 * core, span], sf.at[which, p], rf.at[which, p],
            sibling,
        )

    own_copy = remote(x_ref, win.at[1 + 2 * core], ss, rs, sibling)

    def full_rows(which):
        return pl.ds(pl.multiple_of((2 * which + core) * part, part), part)

    w_copy = remote(wo_ref.at[wo_rows], wof_ref.at[full_rows(t)], sw, rw, across)
    wf_copy = remote(wof_ref.at[full_rows(1 - t)], wof_ref.at[full_rows(1 - t)], sv, rv, sibling)

    def send(p):
        for side in (0, 1):

            @pl.when(exists[1 - side])
            def _():
                x_copy(side, p).start()

    for p in range(AHEAD):
        send(p)
    w_copy.start()
    own_copy.start()
    vec = vec_ref[...].astype(F32)
    gain, shift = vec[0:1], vec[1:2]
    query_bias, value_bias = vec[2:3, :cols], vec[2:3, cols:]
    n_ref[...] = jnp.zeros(n_ref.shape, F32)

    def code(r, carry):
        labels = jnp.transpose(jnp.broadcast_to(lab_ref[pl.ds(r, 1), :], (128, 128)))
        lane = lax.broadcasted_iota(jnp.int32, (128, 128), 1)
        lane = lane - HEAD_DIM * (lane // HEAD_DIM)
        far = jnp.where(labels == lane.astype(F32), 0.0, FAR)
        kc_ref[pl.ds(pl.multiple_of(r * 128, 128), 128), :] = jnp.where(lane < CLIPS, far, 1.0).astype(BF)
        return carry

    lax.fori_loop(0, lab_ref.shape[0], code, 0)

    def raise_norm(spot, values):
        for c in range(cols // 128):
            span = values[:, c * 128 : c * 128 + 128]
            norm = jnp.max(jnp.sum(span * span, axis=1, keepdims=True), axis=0, keepdims=True)
            n_ref[spot, :] = jnp.maximum(n_ref[spot, :], norm)

    def project(slot, start):
        spot = pl.ds(pl.multiple_of(start, half // 2), half // 2)
        attn = (norm_rows(win[slot, spot, :].astype(F32)) * gain + shift).astype(BF)
        out = pl.ds(pl.multiple_of(slot * height + start, half // 2), half // 2)

        @pl.when(slot == REACH)
        def _():
            a_ref[spot, :] = attn

        query = (dot_nn(attn, wq[...]) + query_bias) * HEAD_DIM**-0.5
        key = dot_nn(attn, wk[...])
        q_ref[out, :] = query.astype(BF)
        k_ref[out, :] = key.astype(BF)
        raise_norm(slice(0, 8), query)
        raise_norm(slice(8, 16), key)
        v_ref[out, :] = (dot_nn(attn, wv[...]) + value_bias).astype(BF)

    def pass_on(p):
        for side in (0, 1):

            @pl.when(exists[side])
            def _():
                x_copy(side, p).wait_recv()
                y_copy(side, p).start()

            @pl.when(jnp.logical_and(exists[side], core == 1 - side))
            def _():
                f_copy(0, p).start()

        if p + AHEAD < PIECES:
            send(p + AHEAD)

    for copy in loads:
        copy.wait()

    low, high = range(PIECES // 2), range(PIECES // 2, PIECES)

    def forwarded(which, pieces):
        for side in (0, 1):

            @pl.when(jnp.logical_and(exists[side], core == side))
            def _():
                for p in pieces:
                    f_copy(which, p).wait_recv()

    def crossed(pieces):
        for p in pieces:
            for side in (0, 1):

                @pl.when(exists[side])
                def _():
                    y_copy(side, p).wait_recv()

                @pl.when(jnp.logical_and(exists[side], core == 1 - side))
                def _():
                    f_copy(1, p).start()

    def own_arrived():
        own_copy.wait_recv()
        w_copy.wait_recv()
        wf_copy.start()

    waits = {
        3: [lambda: pass_on(0)],
        4: [own_arrived],
        6: [lambda: pass_on(1)],
        8: [lambda: pass_on(2)] + [lambda p=p: pass_on(p) for p in range(3, PIECES // 2)],
        10: [lambda: forwarded(0, low)],
        11: [lambda: pass_on(high[0]), lambda: crossed(low)],
        13: [lambda: pass_on(high[1]), lambda: forwarded(1, low)],
        14: [lambda p=p: pass_on(p) for p in high[2:]],
        16: [lambda: forwarded(0, high)],
        17: [lambda: crossed(high)],
        19: [lambda: forwarded(1, high)],
    }
    left, right = has_left.astype(jnp.int32), has_right.astype(jnp.int32)
    near = (1 - core) * left + core * right

    def quarter(i, carry):
        for at, acts in waits.items():

            @pl.when(i == at)
            def _():
                for act in acts:
                    act()

        turn = (i - 8) // 3
        place_in = i - 8 - 3 * turn
        late = (i >= 8).astype(jnp.int32)
        second = (i >= 4).astype(jnp.int32)
        first, middle = (place_in == 0).astype(jnp.int32), (place_in == 1).astype(jnp.int32)
        third = 1 - first - middle
        early_slot = (1 - second) * REACH + second * (3 - 2 * core)
        late_slot = middle * 2 * REACH + third * (1 + 2 * core)
        slot = (1 - late) * early_slot + late * late_slot
        there = first * left + middle * right + third * near
        odd = turn - 2 * (turn // 2)
        late_part = 2 * ((1 - odd) * t + odd * (1 - t)) + turn // 2
        part_of = (1 - late) * (i - 4 * second) + late * late_part

        @pl.when((1 - late) + late * there == 1)
        def _():
            project(slot, part_of * (half // 2))

        return carry

    lax.fori_loop(0, 20, quarter, 0)
    wf_copy.wait_recv()
    for copy in (own_copy, w_copy, wf_copy):
        copy.wait_send()
    for p in range(PIECES):
        for side in (0, 1):

            @pl.when(exists[1 - side])
            def _():
                x_copy(side, p).wait_send()

            @pl.when(exists[side])
            def _():
                y_copy(side, p).wait_send()

            @pl.when(jnp.logical_and(exists[side], core == 1 - side))
            def _():
                f_copy(0, p).wait_send()
                f_copy(1, p).wait_send()


def halo_qkv(x, wo, wq, wk, wv, vec, labels):
    height, width = x.shape
    cols = wq.shape[1]
    blocks = 2 * REACH + 1
    shape = jax.ShapeDtypeStruct
    wide = shape((blocks * height, cols), BF)
    pair = DMA((2, PIECES))
    return pl.pallas_call(
        halo_kernel,
        out_shape=(
            wide, wide, wide, shape((height, width), BF), shape((2 * wo.shape[0], wo.shape[1]), BF),
            shape((16, 128), F32), shape((blocks * height, 128), BF),
        ),
        in_specs=[far()] * 5 + [whole()] * 2,
        out_specs=[whole()] * 7,
        scratch_shapes=[pltpu.VMEM((blocks, height, width), BF)]
        + [pltpu.VMEM(wq.shape, BF)] * 3
        + [DMA((5,)), pair, pair, pair, pair, DMA, DMA, pair, pair, DMA, DMA, DMA, DMA],
        compiler_params=pltpu.CompilerParams(
            collective_id=0, has_side_effects=True, vmem_limit_bytes=VMEM_BYTES
        ),
        name="halo_qkv",
    )(*[in_hbm(value) for value in (x, wo, wq, wk, wv)], vec, labels)


def split3(values):
    first = values.astype(BF).astype(F32)
    second = (values - first).astype(BF).astype(F32)
    return first, second, values - first - second


def free_lane(shape):
    lane = lax.broadcasted_iota(jnp.int32, shape, 1)
    return lane - HEAD_DIM * (lane // HEAD_DIM)


def clip_code(keys_code):
    same = jnp.logical_and(free_lane(keys_code.shape) < CLIPS, keys_code.astype(F32) == 0.0)
    return jnp.where(same, 1.0, 0.0)


def code_tile(rows, keys_code, cols):
    terms = jnp.concatenate(split3(-rows), axis=0).astype(BF)
    line = lax.broadcasted_iota(jnp.int32, (48, cols), 0)
    lane = lax.broadcasted_iota(jnp.int32, (48, cols), 1)
    term = line // 16
    row = line - 16 * term
    centre = row // 8
    head = row - 8 * centre
    pair = head // 2
    spot = 128 * pair + HEAD_DIM * (1 - (head - 2 * pair)) + LOGS + (CENTRES - LOGS) * centre + term
    picks = jnp.where(lane == spot, 1.0, 0.0).astype(BF)
    same = clip_code(keys_code)
    return (dot_tn(terms, picks) + jnp.concatenate([same] * (cols // 128), axis=1)).astype(BF)


def tile_at(j):
    return pl.ds(pl.multiple_of(j * TILE, TILE), TILE)


def lanes_of(c):
    return pl.ds(c * 128, 128)


def with_code(values, code):
    lower = lax.broadcasted_iota(jnp.int32, values.shape, 1) < HEAD_DIM
    return jnp.where(lower, values, code), jnp.where(lower, code, values)


def against(moving, still):
    return jnp.concatenate([dot_nt(moving[h], still[h * TILE : (h + 1) * TILE]) for h in (0, 1)], axis=1)


def add_heads(acc_ref, c, values, weights):
    turned = jnp.transpose(values)
    acc_ref[c, :HEAD_DIM] += dot_nn(turned[:HEAD_DIM], weights[:, :TILE])
    acc_ref[c, HEAD_DIM:] += dot_nn(turned[HEAD_DIM:], weights[:, TILE:])


def keep(code, low, high):
    lane = free_lane(code.shape)
    return jnp.where(jnp.logical_and(lane >= low, lane < high), code, jnp.zeros_like(code))


def attend_kernel(height, first, b_ref, q_ref, k_ref, v_ref, kc_ref, n_ref, o_ref, lse_ref, r_ref, m_ref, l_ref, acc_ref):
    cols = o_ref.shape[1]
    pairs, tiles = cols // 128, o_ref.shape[0] // TILE
    steep = jnp.logical_not(jnp.max(n_ref[0:8, :]) * jnp.max(n_ref[8:16, :]) <= SAFE * SAFE)
    def groups(values):
        return values.reshape(TILE // 8, 8, values.shape[1])

    def one(i, carry):
        lo, hi = b_ref[0, first + i], b_ref[1, first + i]
        own = pl.ds(pl.multiple_of(REACH * height + (first + i) * TILE, TILE), TILE)
        code = clip_code(kc_ref[own, :]).astype(BF)
        for c in range(pairs):
            r_ref[c] = jnp.concatenate(with_code(q_ref[own, lanes_of(c)], code), axis=0)
        acc_ref[...] = jnp.zeros(acc_ref.shape, F32)
        l_ref[...] = jnp.zeros(l_ref.shape, F32)
        m_ref[...] = jnp.zeros(m_ref.shape, F32)

        def score(j, c):
            return against(with_code(k_ref[tile_at(j), lanes_of(c)], kc_ref[tile_at(j), :]), r_ref[c])

        def step(shift, j, carry):
            raised = []
            for c in range(pairs):
                s = score(j, c)
                e = jnp.exp(s - m_ref[c, 0:1, :] if shift else s)
                l_ref[c] += jnp.sum(groups(e), axis=0)
                raised.append(e.astype(BF))
            for c in range(pairs):
                add_heads(acc_ref, c, v_ref[tile_at(j), lanes_of(c)], raised[c])
            return carry

        @pl.when(jnp.logical_not(steep))
        def _():
            lax.fori_loop(lo, hi, functools.partial(step, False), 0)

        @pl.when(steep)
        def _():
            m_ref[...] = jnp.full(m_ref.shape, NEG, F32)

            def peak(j, carry):
                for c in range(pairs):
                    m_ref[c] = jnp.maximum(m_ref[c], jnp.max(groups(score(j, c)), axis=0))
                return carry

            lax.fori_loop(lo, hi, peak, 0)
            for c in range(pairs):
                m_ref[c] = jnp.broadcast_to(jnp.max(m_ref[c], axis=0, keepdims=True), m_ref.shape[1:])
            lax.fori_loop(lo, hi, functools.partial(step, True), 0)

        for c in range(pairs):
            total = jnp.sum(l_ref[c], axis=0, keepdims=True)
            share = jnp.concatenate(
                [acc_ref[c, :HEAD_DIM] / total[:, :TILE], acc_ref[c, HEAD_DIM:] / total[:, TILE:]], axis=0
            )
            o_ref[tile_at(i), lanes_of(c)] = jnp.transpose(share).astype(BF)
            logs = m_ref[c, 0:1, :] + jnp.log(total)
            lse_ref[2 * c : 2 * c + 1, tile_at(i)] = logs[:, :TILE]
            lse_ref[2 * c + 1 : 2 * c + 2, tile_at(i)] = logs[:, TILE:]
        return carry

    lse_ref[...] = jnp.zeros(lse_ref.shape, F32)
    lax.fori_loop(0, tiles, one, 0)


def local_call(kernel, name, out_shape, scratch, bounds, *values):
    grid = pltpu.PrefetchScalarGridSpec(
        num_scalar_prefetch=1,
        grid=(1,),
        in_specs=[whole()] * len(values),
        out_specs=jax.tree.map(lambda _: whole(), out_shape),
        scratch_shapes=scratch,
    )
    return pl.pallas_call(
        kernel,
        grid_spec=grid,
        out_shape=out_shape,
        compiler_params=pltpu.CompilerParams(vmem_limit_bytes=VMEM_BYTES),
        name=name,
    )(bounds, *values)


def attend(bounds, q, k, v, kc, norms, height, first, count):
    cols = k.shape[1]
    pairs = cols // 128
    rows = count * TILE
    out_shape = (jax.ShapeDtypeStruct((rows, cols), BF), jax.ShapeDtypeStruct((8, rows), F32))
    scratch = [
        pltpu.VMEM((pairs, 2 * TILE, 128), BF),
        pltpu.VMEM((pairs, 8, 2 * TILE), F32),
        pltpu.VMEM((pairs, 8, 2 * TILE), F32),
        pltpu.VMEM((pairs, 128, TILE), F32),
    ]
    kernel = functools.partial(attend_kernel, height, first)
    return local_call(kernel, "attend", out_shape, scratch, bounds, q, k, v, kc, norms)


def query_back_kernel(b_ref, q_ref, k_ref, v_ref, g_ref, kc_ref, qc_ref, dq_ref, r_ref, t_ref, acc_ref):
    height, cols = dq_ref.shape
    pairs, tiles = cols // 128, height // TILE
    def one(i, carry):
        own = pl.ds(pl.multiple_of(REACH * height + i * TILE, TILE), TILE)
        for c in range(pairs):
            code = qc_ref[own, lanes_of(c)]
            logs, centres = keep(code, 0, CENTRES), keep(code, CENTRES, CENTRES + 3)
            r_ref[c] = jnp.concatenate(with_code(q_ref[own, lanes_of(c)], logs), axis=0)
            t_ref[c] = jnp.concatenate(with_code(g_ref[own, lanes_of(c)], centres), axis=0)
        acc_ref[...] = jnp.zeros(acc_ref.shape, F32)

        def step(j, carry):
            code = kc_ref[tile_at(j), :]
            steps = []
            for c in range(pairs):
                probs = jnp.exp(against(with_code(k_ref[tile_at(j), lanes_of(c)], code), r_ref[c]))
                d_probs = against(with_code(v_ref[tile_at(j), lanes_of(c)], code), t_ref[c])
                steps.append((probs * d_probs).astype(BF))
            for c in range(pairs):
                add_heads(acc_ref, c, k_ref[tile_at(j), lanes_of(c)], steps[c])
            return carry

        lax.fori_loop(b_ref[0, i], b_ref[1, i], step, 0)
        for c in range(pairs):
            dq_ref[tile_at(i), lanes_of(c)] = (jnp.transpose(acc_ref[c]) * HEAD_DIM**-0.5).astype(BF)
        return carry

    lax.fori_loop(0, tiles, one, 0)


def query_back(bounds, q, k, v, g, kc, qc, height):
    cols = k.shape[1]
    pairs = cols // 128
    scratch = [pltpu.VMEM((pairs, 2 * TILE, 128), BF)] * 2 + [pltpu.VMEM((pairs, 128, TILE), F32)]
    out_shape = jax.ShapeDtypeStruct((height, cols), BF)
    return local_call(query_back_kernel, "query_back", out_shape, scratch, bounds, q, k, v, g, kc, qc)


def key_back_kernel(b_ref, q_ref, k_ref, v_ref, g_ref, kc_ref, qc_ref, dk_ref, dv_ref, r_ref, t_ref, ak_ref, av_ref):
    height, cols = dk_ref.shape
    pairs, tiles = cols // 128, height // TILE
    def one(i, carry):
        own = pl.ds(pl.multiple_of(REACH * height + i * TILE, TILE), TILE)
        code = kc_ref[own, :]
        logs, centres = keep(code, 0, CENTRES), keep(code, CENTRES, CENTRES + 3)
        for c in range(pairs):
            r_ref[c] = jnp.concatenate(with_code(k_ref[own, lanes_of(c)], logs), axis=0)
            t_ref[c] = jnp.concatenate(with_code(v_ref[own, lanes_of(c)], centres), axis=0)
        ak_ref[...] = jnp.zeros(ak_ref.shape, F32)
        av_ref[...] = jnp.zeros(av_ref.shape, F32)

        def step(j, carry):
            weights, steps = [], []
            for c in range(pairs):
                code = qc_ref[tile_at(j), lanes_of(c)]
                probs = jnp.exp(against(with_code(q_ref[tile_at(j), lanes_of(c)], code), r_ref[c]))
                d_probs = against(with_code(g_ref[tile_at(j), lanes_of(c)], code), t_ref[c])
                weights.append(probs.astype(BF))
                steps.append((probs * d_probs).astype(BF))
            for c in range(pairs):
                add_heads(av_ref, c, g_ref[tile_at(j), lanes_of(c)], weights[c])
                add_heads(ak_ref, c, q_ref[tile_at(j), lanes_of(c)], steps[c])
            return carry

        lax.fori_loop(b_ref[0, i], b_ref[1, i], step, 0)
        for c in range(pairs):
            dk_ref[tile_at(i), lanes_of(c)] = jnp.transpose(ak_ref[c]).astype(BF)
            dv_ref[tile_at(i), lanes_of(c)] = jnp.transpose(av_ref[c]).astype(BF)
        return carry

    lax.fori_loop(0, tiles, one, 0)


def key_back(bounds, q, k, v, g, kc, qc, height):
    cols = k.shape[1]
    pairs = cols // 128
    scratch = [pltpu.VMEM((pairs, 2 * TILE, 128), BF)] * 2 + [pltpu.VMEM((pairs, 128, TILE), F32)] * 2
    out_shape = (jax.ShapeDtypeStruct((height, cols), BF),) * 2
    return local_call(key_back_kernel, "key_back", out_shape, scratch, bounds, q, k, v, g, kc, qc)


class Ring:
    def __init__(self):
        d = lax.axis_index("dp")
        n = lax.axis_size("dp") // 2
        chip = d // 2
        core = d - 2 * chip
        odd = chip - 2 * (chip // 2)
        spot = (1 - odd) * (chip // 2) + odd * (n - 1 - chip // 2)
        self.here = (1 - core) * spot + core * (n - 1 - spot)
        self.n, self.core, self.hops = n, core, n // 2
        self.sibling = {"dp": d + 1 - 2 * core}
        self.after = {"dp": self.device_at(self.wrap(self.here + 1))}
        self.before = {"dp": self.device_at(self.wrap(self.here - 1))}

    def wrap(self, index):
        return lax.rem(index + 2 * self.n, self.n)

    def device_at(self, rank):
        n, core = self.n, self.core
        walk = (1 - core) * rank + core * (n - 1 - rank)
        late = walk // (n // 2)
        return 2 * ((1 - late) * (2 * walk) + late * (2 * (n - walk) - 1)) + core

    def spans(self, shape, i, owner, j):
        rows, cols = shape[0] // 2, shape[1]
        wide = STRIPS * STRIP
        high, count = rows * cols // (self.n * wide), cols // wide
        line = j // count
        row = pl.multiple_of(owner * rows + line * high, high)
        col = pl.multiple_of((j - line * count) * wide + i * STRIP, STRIP)
        return pl.ds(row, high), pl.ds(col, STRIP)


def units(arrays):
    return [(a, i, pl.ds(i * STRIP, STRIP), a * STRIPS + i) for a in range(arrays) for i in range(STRIPS)]


class Reduce:
    def __init__(self, ring, given, sibs, bufs, sems):
        self.ring, self.given, self.sibs, self.bufs, self.sems = ring, given, sibs, bufs, sems
        self.units = units(len(given))

    def s_copy(self, a):
        rows = self.given[a].shape[0] // 2
        span = pl.ds(pl.multiple_of((1 - self.ring.core) * rows, rows), rows)
        return remote(
            self.given[a].at[span], self.sibs[a], self.sems[0].at[a], self.sems[1].at[a], self.ring.sibling
        )

    def ways(self):
        ring = self.ring
        return (
            (0, ring.hops, lambda s: ring.wrap(ring.here + ring.hops - s), ring.after),
            (ring.hops + 1, ring.hops - 1, lambda s: ring.wrap(ring.here - ring.hops + 1 + s), ring.before),
        )

    def r_copy(self, u, way, s):
        a, _, strip, e = u
        base, _, _, target = way
        k = (s if base == 0 else self.ring.hops + s)
        src, dst = self.bufs[a].at[base + s, :, strip], self.bufs[a].at[base + s + 1, :, strip]
        return remote(src, dst, self.sems[2].at[e, k], self.sems[3].at[e, k], target)

    def terms(self, u, j):
        a, i, _, _ = u
        shape, core = self.given[a].shape, self.ring.core
        mine = self.given[a][self.ring.spans(shape, i, core, j)].astype(F32)
        return mine + self.sibs[a][self.ring.spans(shape, i, 0, j)].astype(F32)

    def swap(self, a):
        self.s_copy(a).start()

    def first(self, a):
        self.s_copy(a).wait_recv()
        for u in self.units:
            if u[0] == a:
                for way in self.ways():
                    self.bufs[a][way[0], :, u[2]] = self.terms(u, way[2](0)).astype(BF)
                    self.r_copy(u, way, 0).start()

    def step(self, s, both=True):
        for u in self.units:
            a, _, strip, _ = u
            for way in self.ways()[: 2 if both else 1]:
                slot = way[0] + s
                local = self.terms(u, way[2](s))
                self.r_copy(u, way, s - 1).wait_recv()
                self.bufs[a][slot, :, strip] = (self.bufs[a][slot, :, strip].astype(F32) + local).astype(BF)
                self.r_copy(u, way, s).start()

    def turn(self):
        hops = self.ring.hops
        for u in self.units:
            a, _, strip, _ = u
            local = self.terms(u, self.ring.here)
            ahead, back = self.ways()
            self.r_copy(u, back, hops - 2).wait_recv()
            local = local + self.bufs[a][2 * hops, :, strip].astype(F32)
            self.r_copy(u, ahead, hops - 1).wait_recv()
            self.bufs[a][hops, :, strip] = (self.bufs[a][hops, :, strip].astype(F32) + local).astype(BF)

    def settle(self):
        for a in range(len(self.given)):
            self.s_copy(a).wait_send()
        for way in self.ways():

            def step(s, carry):
                for u in self.units:
                    self.r_copy(u, way, s).wait_send()
                return carry

            lax.fori_loop(0, way[1], step, 0)


class Gather:
    def __init__(self, ring, outs, sems):
        self.ring, self.outs, self.sems = ring, outs, sems
        self.units = units(len(outs))

    def spot(self, u, j):
        out, ring = self.outs[u[0]], self.ring
        return out.at[ring.spans(out.shape, u[1], ring.core, ring.wrap(ring.here + j))]

    def g_copy(self, u, way, s):
        ring = self.ring
        spot = self.spot(u, -s if way == 0 else s)
        k = s if way == 0 else ring.hops + s
        target = ring.after if way == 0 else ring.before
        return remote(spot, spot, self.sems[0].at[u[3], k], self.sems[1].at[u[3], k], target)

    def c_copy(self, u, way, s):
        spot = self.spot(u, -s if way == 0 else s)
        k = s if way == 0 else self.ring.hops + s
        return remote(spot, spot, self.sems[2].at[u[3], k], self.sems[3].at[u[3], k], self.ring.sibling)

    def begin(self, sources):
        for u in self.units:
            a, _, strip, _ = u
            self.spot(u, 0)[...] = sources[a][:, strip]
            self.g_copy(u, 0, 0).start()
            self.g_copy(u, 1, 0).start()
            self.c_copy(u, 0, 0).start()

    def step(self, s):
        for u in self.units:
            for way in (0, 1):
                self.g_copy(u, way, s - 1).wait_recv()
                self.g_copy(u, way, s).start()
                self.c_copy(u, way, s).start()

    def last(self):
        hops = self.ring.hops
        for u in self.units:
            self.g_copy(u, 0, hops - 2).wait_recv()
            self.g_copy(u, 0, hops - 1).start()
            self.c_copy(u, 0, hops - 1).start()
            self.g_copy(u, 1, hops - 2).wait_recv()
            self.c_copy(u, 1, hops - 1).start()
        for u in self.units:
            self.g_copy(u, 0, hops - 1).wait_recv()
            self.c_copy(u, 0, hops).start()

    def settle(self):
        hops = self.ring.hops
        for way in (0, 1):

            def sent(s, carry):
                for u in self.units:
                    self.g_copy(u, way, s).wait_send()
                return carry

            def copied(s, carry):
                for u in self.units:
                    self.c_copy(u, way, s).wait()
                return carry

            lax.fori_loop(0, hops - way, sent, 0)
            lax.fori_loop(way, hops + 1 - way, copied, 0)


def between(step, done, hops):
    def body(s, carry):
        step(s)
        return carry

    if done < hops - 1:
        lax.fori_loop(done, hops - 1, body, 0)


def chunk_rows(shape, n):
    return shape[0] * shape[1] // (2 * n * STRIPS * STRIP)


def reduce_scratch(shapes, n):
    count = len(shapes)
    sibs = [pltpu.VMEM((rows // 2, cols), BF) for rows, cols in shapes]
    bufs = [pltpu.VMEM((n + 1, chunk_rows(shape, n), STRIPS * STRIP), BF) for shape in shapes]
    return sibs + bufs, [DMA((count,))] * 2 + [DMA((count * STRIPS, n - 1))] * 2


def gather_sems(count, n):
    return [DMA((count * STRIPS, n - 1))] * 2 + [DMA((count * STRIPS, n))] * 2


def norm_back_rows(grad, values, gain):
    middle = jnp.mean(values, axis=-1, keepdims=True)
    centred = values - middle
    inverse = lax.rsqrt(jnp.mean(centred * centred, axis=-1, keepdims=True) + 1e-05)
    n = centred * inverse
    t = grad * gain
    back = (t - jnp.mean(t, axis=-1, keepdims=True) - n * jnp.mean(t * n, axis=-1, keepdims=True)) * inverse
    return back, grad * n


def column_sums(values):
    return jnp.sum(values, axis=0, keepdims=True)


def mid_kernel(
    x_ref, cot_ref, mixa_ref, mixb_ref, oma_ref, lsea_ref, lseb_ref, kc_ref, wof_ref, row_ref, w1_ref, w2_ref,
    xw_ref, qc_ref, rg_ref, low_ref, vec_ref, own1_ref, own2_ref, res_ref, outp_ref, mix_ref,
    om_ref, dact_ref, mi_ref, act_ref, pg_ref, part_ref, oth_ref, f1_ref, f2_ref, st_ref, sw_ref,
    sib1, sib2, buf1, buf2,
    sm, rm, sy, ry, sx, rx, ss, rs, sf, rf, *ring_sems,
):
    d, core, has_left, has_right = place()
    t = lax.axis_index("tensor")
    height, cols = mix_ref.shape
    width, hidden = w1_ref.shape
    rows = height // PARTS
    sibling = {"dp": d + 1 - 2 * core}
    across = {"tensor": 1 - t}
    exists = (has_left, has_right)
    slots = (0, 2 * REACH)
    ring = Ring()
    reduce = Reduce(ring, (f1_ref, f2_ref), (sib1, sib2), (buf1, buf2), ring_sems)
    hops = ring.hops
    greet([
        (None, sibling), (None, across), (has_left, {"dp": d - 2}), (has_right, {"dp": d + 2}),
        (None, ring.after), (None, ring.before),
    ])

    def span(p):
        return pl.ds(pl.multiple_of(p * rows, rows), rows)

    head = mixa_ref.shape[0]
    m_copy = remote(mixb_ref, om_ref.at[pl.ds(head, height - head)], sm, rm, across)

    def y_copy(p):
        return remote(part_ref.at[span(p)], oth_ref.at[span(p)], sy.at[p], ry.at[p], across)

    def refs(p):
        if p == PARTS:
            return st_ref, lambda slot: sw_ref.at[slot]
        return xw_ref.at[REACH, span(p)], lambda slot: xw_ref.at[slot, span(p)]

    def x_copy(side, p):
        src, dst = refs(p)
        return remote(
            src, dst(slots[side]), sx.at[side, p], rx.at[side, p],
            {"dp": d + 2 if side == 0 else d - 2},
        )

    def s_copy(p):
        src, dst = refs(p)
        return remote(src, dst(1 + 2 * core), ss.at[p], rs.at[p], sibling)

    def f_copy(p):
        _, dst = refs(p)
        return remote(dst(4 - 4 * core), dst(3 - 2 * core), sf.at[p], rf.at[p], sibling)

    def send(p):
        for side in (0, 1):

            @pl.when(exists[1 - side])
            def _():
                x_copy(side, p).start()

        s_copy(p).start()

    def pass_on(p):
        for side in (0, 1):

            @pl.when(exists[side])
            def _():
                x_copy(side, p).wait_recv()

            @pl.when(jnp.logical_and(exists[side], core == 1 - side))
            def _():
                f_copy(p).start()

    m_copy.start()
    mix_ref[:head, :] = mixa_ref[...]
    mix_ref[head:, :] = mixb_ref[...]
    om_ref[:head, :] = oma_ref[...]
    vec = row_ref[...].astype(F32)
    out_bias, gain, shift = vec[3:4], vec[4:5], vec[5:6]
    heads = pl.ds(pl.multiple_of(t * cols, cols), cols)
    others = pl.ds(pl.multiple_of((1 - t) * cols, cols), cols)
    picks = lax.broadcasted_iota(jnp.int32, (8, cols), 1) // HEAD_DIM
    picks = (picks == lax.broadcasted_iota(jnp.int32, (8, cols), 0)).astype(F32)
    st_ref[0:8, :head] = lsea_ref[...]
    st_ref[0:8, head:] = lseb_ref[...]
    vec_ref[...] = jnp.zeros(vec_ref.shape, F32)

    def early(p, carry):
        cot = cot_ref[span(p), :]
        dact_ref[span(p), :] = dot_nt(cot, w2_ref[...])
        vec_ref[3:4, :] += column_sums(cot.astype(F32))
        res_ref[span(p), :] = x_ref[span(p), :].astype(F32) + dot_nn(mix_ref[span(p), :], wof_ref[heads, :]) + out_bias
        return carry

    lax.fori_loop(0, PARTS, early, 0)

    def forward(p, carry):
        @pl.when((p + 1) * rows > head)
        def _():
            m_copy.wait_recv()

        residual = res_ref[span(p), :] + dot_nn(om_ref[span(p), :], wof_ref[others, :])
        res_ref[span(p), :] = residual
        mlp_input = (norm_rows(residual) * gain + shift).astype(BF)
        mi_ref[span(p), :] = mlp_input
        for i in range(hidden // width):
            part = slice(i * width, (i + 1) * width)
            preact = dot_nn(mlp_input, w1_ref[:, part]) + vec[6 + i : 7 + i]
            cdf = 0.5 * (1.0 + lax.erf(preact * (2.0**-0.5)))
            pdf = jnp.exp(-0.5 * preact * preact) * 0.3989422804014327
            act_ref[span(p), part] = (preact * cdf).astype(BF)
            pre_grad = (dact_ref[span(p), part] * (cdf + preact * pdf)).astype(BF)
            pg_ref[span(p), part] = pre_grad
            vec_ref[4 + i : 5 + i, :] += column_sums(pre_grad.astype(F32))
        part_ref[span(p), :] = dot_nt(pg_ref[span(p), :], w1_ref[...]).astype(BF)
        y_copy(p).start()
        return carry

    lax.fori_loop(0, PARTS, forward, 0)

    def weights(which):
        half = pl.ds(pl.multiple_of(which * (width // 2), width // 2), width // 2)
        f1_ref[half, :] = dot_tn(mi_ref[:, half], pg_ref[...]).astype(BF)
        half = pl.ds(pl.multiple_of(which * (hidden // 2), hidden // 2), hidden // 2)
        f2_ref[half, :] = dot_tn(act_ref[:, half], cot_ref[...]).astype(BF)

    def back(p):
        y_copy(p).wait_recv()
        grad = part_ref[span(p), :].astype(F32) + oth_ref[span(p), :].astype(F32)
        turned, scaled = norm_back_rows(grad, res_ref[span(p), :], gain)
        total = cot_ref[span(p), :].astype(F32) + turned
        low = total.astype(BF)
        rg_ref[span(p), :] = total
        low_ref[span(p), :] = low
        vec_ref[0:1, :] += column_sums(scaled)
        vec_ref[1:2, :] += column_sums(grad)
        vec_ref[2:3, :] += column_sums(low.astype(F32))
        mixed_grad = dot_nt(low, wof_ref[heads, :]).astype(BF)
        xw_ref[REACH, span(p), :] = mixed_grad
        product = mixed_grad.astype(F32) * mix_ref[span(p), :].astype(F32)
        st_ref[8:16, p * rows : (p + 1) * rows] = lax.dot_general(
            picks, product, (((1,), (1,)), ((), ())),
            precision=lax.Precision.HIGHEST, preferred_element_type=F32,
        )

    def code(slot):
        def step(i, carry):
            spot = pl.ds(pl.multiple_of(slot * height + i * TILE, TILE), TILE)
            stats = sw_ref[slot, :, pl.ds(pl.multiple_of(i * TILE, TILE), TILE)]
            qc_ref[spot, :] = code_tile(stats, kc_ref[spot, :], cols)
            return carry

        lax.fori_loop(0, height // TILE, step, 0)

    def ring_step(s):
        if s < hops - 1:
            reduce.step(s)

    back(0)
    send(0)
    weights(1 - core)
    reduce.swap(0)
    reduce.swap(1)
    back(1)
    send(1)
    weights(core)
    reduce.first(0)
    reduce.first(1)
    outp_ref[...] = dot_nn(act_ref[...], w2_ref[...]).astype(BF)
    ring_step(1)
    back(2)
    send(2)
    send(PARTS)
    sw_ref[REACH] = st_ref[...]
    code(REACH)
    pass_on(0)
    ring_step(2)
    pass_on(1)
    between(reduce.step, 3, hops)
    reduce.step(hops - 1, False)
    pass_on(2)
    pass_on(PARTS)
    s_copy(PARTS).wait_recv()
    code(3 - 2 * core)
    for side in (0, 1):

        @pl.when(exists[side])
        def _():
            code(slots[side])

    reduce.turn()
    own1_ref[...] = buf1[hops]
    own2_ref[...] = buf2[hops]
    for p in range(PARTS + 1):
        if p < PARTS:
            s_copy(p).wait()
        else:
            s_copy(p).wait_send()
        for side in (0, 1):

            @pl.when(exists[1 - side])
            def _():
                x_copy(side, p).wait_send()

            @pl.when(jnp.logical_and(exists[side], core == 1 - side))
            def _():
                f_copy(p).wait_send()

            @pl.when(jnp.logical_and(exists[side], core == side))
            def _():
                f_copy(p).wait_recv()

    for side in (0, 1):

        @pl.when(jnp.logical_and(exists[side], core == side))
        def _():
            code(1 + 2 * core)

    for p in range(PARTS):
        y_copy(p).wait_send()
    m_copy.wait_send()
    reduce.settle()


def mid(x, cot, mixa, mixb, oma, lsea, lseb, kc, wof, vec, w1, w2):
    blocks = 2 * REACH + 1
    height, width = x.shape
    hidden = w1.shape[1]
    mix = jax.ShapeDtypeStruct((height, mixa.shape[1]), BF)
    n = lax.axis_size("dp") // 2
    pair, line, some = DMA((2, PARTS + 1)), DMA((PARTS + 1,)), DMA((PARTS,))
    room, sems = reduce_scratch((w1.shape, w2.shape), n)
    shape = jax.ShapeDtypeStruct
    chunks = [shape((chunk_rows(w.shape, n), STRIPS * STRIP), BF) for w in (w1, w2)]
    return pl.pallas_call(
        mid_kernel,
        out_shape=(
            shape((blocks,) + mix.shape, BF), shape((kc.shape[0], mix.shape[1]), BF), shape(x.shape, F32), shape(x.shape, BF),
            shape((16, width), F32), *chunks, shape(x.shape, F32), shape(x.shape, BF), mix,
        ),
        in_specs=[whole()] * 12,
        out_specs=[whole()] * 10,
        scratch_shapes=[
            pltpu.VMEM(mix.shape, BF), pltpu.VMEM((height, hidden), F32), pltpu.VMEM(x.shape, BF),
            pltpu.VMEM((height, hidden), BF), pltpu.VMEM((height, hidden), BF), pltpu.VMEM(x.shape, BF),
            pltpu.VMEM(x.shape, BF), pltpu.VMEM(w1.shape, BF), pltpu.VMEM(w2.shape, BF),
            pltpu.VMEM((16, height), F32), pltpu.VMEM((blocks, 16, height), F32),
        ]
        + room
        + [DMA, DMA, some, some, pair, pair, line, line, line, line]
        + sems,
        compiler_params=pltpu.CompilerParams(
            collective_id=1, has_side_effects=True, vmem_limit_bytes=MID_BYTES
        ),
        name="mid",
    )(x, cot, mixa, mixb, oma, lsea, lseb, kc, wof, vec, w1, w2)


def finish_kernel(
    rounds, dq_ref, dk_ref, dv_ref, wq_ref, wk_ref, wv_ref, a_ref, low_ref, o_ref, x_ref, rg_ref, row_ref, vec_ref,
    own1_ref, own2_ref, res_hbm, outp_hbm, outo_hbm,
    ig_ref, g_ref, vs_ref, g1_ref, g2_ref, lo_ref,
    part_ref, oth_ref, own_ref, send_ref, got_ref, res_ref, outp_ref, outo_ref, sib, buf,
    load, sy, ry, sd, rd, *ring_sems,
):
    d, core, _, _ = place()
    t = lax.axis_index("tensor")
    height, cols = dq_ref.shape
    width = x_ref.shape[1]
    piece = height // PIECES
    across = {"tensor": 1 - t}
    loads = [
        pltpu.make_async_copy(src, dst, load.at[i])
        for i, (src, dst) in enumerate(((res_hbm, res_ref), (outp_hbm, outp_ref), (outo_hbm, outo_ref)))
    ]
    for copy in loads:
        copy.start()
    ring = Ring()
    reduce = Reduce(ring, (own_ref,), (sib,), (buf,), ring_sems[:4])
    gather = Gather(ring, (g_ref,), ring_sems[4:8])
    wide = Gather(ring, (g1_ref, g2_ref), ring_sems[8:])
    hops = ring.hops
    partners = []
    for r in range(rounds):
        bit = (d // 2**r) - 2 * (d // 2 ** (r + 1))
        partners.append({"dp": d + 2**r * (1 - 2 * bit)})
    greet([(None, across), (None, ring.after), (None, ring.before)] + [(None, p) for p in partners])

    def y_copy(p):
        span = pl.ds(p * piece, piece)
        return remote(part_ref.at[span], oth_ref.at[span], sy.at[p], ry.at[p], across)

    def d_copy(r):
        return remote(send_ref.at[r], got_ref.at[r], sd.at[r], rd.at[r], partners[r])

    def share(p):
        span = pl.ds(p * piece, piece)
        part = dot_nt(dq_ref[span, :], wq_ref[...]) + dot_nt(dk_ref[span, :], wk_ref[...])
        part_ref[span, :] = (part + dot_nt(dv_ref[span, :], wv_ref[...])).astype(BF)

    def weights(which):
        span = pl.ds(pl.multiple_of(which * (width // 2), width // 2), width // 2)
        attn = a_ref[:, span]
        for i, ref in enumerate((dq_ref, dk_ref, dv_ref)):
            own_ref[span, i * cols : (i + 1) * cols] = dot_tn(attn, ref[...]).astype(BF)
        own_ref[span, 3 * cols : 4 * cols] = dot_tn(low_ref[:, span], o_ref[...]).astype(BF)

    def wide_step(s):
        if s < hops - 1:
            wide.step(s)

    wide.begin((own1_ref, own2_ref))
    weights(1 - core)
    reduce.swap(0)
    for p in range(AHEAD):
        share(p)
        y_copy(p).start()
    weights(core)
    wide_step(1)
    for p in range(AHEAD, PIECES):
        share(p)
    vec = row_ref[...].astype(F32)
    gain, fc2_bias = vec[0:1], vec[8:9]
    gains, shifts = [], []

    def back(p):
        span = pl.ds(p * piece, piece)
        y_copy(p).wait_recv()
        if p + AHEAD < PIECES:
            y_copy(p + AHEAD).start()
        grad = part_ref[span, :].astype(F32) + oth_ref[span, :].astype(F32)
        turned, scaled = norm_back_rows(grad, x_ref[span, :].astype(F32), gain)
        ig_ref[span, :] = rg_ref[span, :] + turned
        gains.append(column_sums(scaled))
        shifts.append(column_sums(grad))

    def reduce_step(s):
        if s < hops - 1:
            reduce.step(s)

    def gather_step(s):
        if s < hops - 1:
            gather.step(s)

    def layer_out(p):
        span = pl.ds(p * piece, piece)
        total = outp_ref[span, :].astype(F32) + outo_ref[span, :].astype(F32)
        lo_ref[span, :] = (res_ref[span, :] + total + fc2_bias).astype(BF)

    def double(s):
        if s < rounds:
            d_copy(s).wait_recv()
            total = send_ref[s] + got_ref[s]
            if s + 1 < rounds:
                send_ref[s + 1] = total
                d_copy(s + 1).start()
            else:
                vs_ref[...] = total

    reduce.first(0)
    back(0)
    wide_step(2)
    reduce_step(1)
    back(1)
    reduce_step(2)
    back(2)
    between(reduce.step, 3, hops)
    between(wide.step, 3, hops)
    reduce.step(hops - 1, False)
    back(3)
    wide.last()
    reduce.turn()
    gather.begin((buf.at[hops],))
    back(4)
    gather_step(1)
    back(5)
    send_ref[0] = vec_ref[...]
    send_ref[0, 6:7, 0:cols] = column_sums(dq_ref[...].astype(F32))
    send_ref[0, 6:7, cols : 2 * cols] = column_sums(dv_ref[...].astype(F32))
    send_ref[0, 7:8, :] = sum(gains[1:], gains[0])
    send_ref[0, 8:9, :] = sum(shifts[1:], shifts[0])
    d_copy(0).start()
    gather_step(2)
    for copy in loads:
        copy.wait()
    layer_out(0)
    double(0)
    layer_out(1)
    between(gather.step, 3, hops)
    double(1)
    layer_out(2)
    gather.last()
    double(2)
    layer_out(3)
    layer_out(4)
    layer_out(5)
    for s in range(3, rounds):
        double(s)
    for p in range(PIECES):
        y_copy(p).wait_send()
    for r in range(rounds):
        d_copy(r).wait_send()
    reduce.settle()
    wide.settle()
    gather.settle()


def finish(dq, dk, dv, wq, wk, wv, attn, low, o, x, rg, gain, vectors, own1, own2, res, outp, outo, shapes):
    height, cols = dq.shape
    width = x.shape[1]
    size = lax.axis_size("dp")
    rounds = size.bit_length() - 1
    n = size // 2
    weights = (width, 4 * cols)
    room, sems = reduce_scratch((weights,), n)
    shape = jax.ShapeDtypeStruct
    return pl.pallas_call(
        functools.partial(finish_kernel, rounds),
        out_shape=(
            shape((height, width), F32), shape(weights, BF), shape(vectors.shape, F32),
            *[shape(dims, BF) for dims in shapes], shape((height, width), BF),
        ),
        in_specs=[whole()] * 15 + [far()] * 3,
        out_specs=[whole()] * 6,
        scratch_shapes=[
            pltpu.VMEM((height, width), BF), pltpu.VMEM((height, width), BF), pltpu.VMEM(weights, BF),
            pltpu.VMEM((rounds,) + vectors.shape, F32), pltpu.VMEM((rounds,) + vectors.shape, F32),
            pltpu.VMEM((height, width), F32), pltpu.VMEM((height, width), BF), pltpu.VMEM((height, width), BF),
        ]
        + room
        + [DMA((3,)), DMA((PIECES,)), DMA((PIECES,)), DMA((rounds,)), DMA((rounds,))]
        + sems
        + gather_sems(1, n)
        + gather_sems(2, n),
        compiler_params=pltpu.CompilerParams(
            collective_id=2, has_side_effects=True, vmem_limit_bytes=FINISH_BYTES
        ),
        name="finish",
    )(dq, dk, dv, wq, wk, wv, attn, low, o, x, rg, gain, vectors, own1, own2, res, outp, outo)


def widen_kernel(a_ref, f1_ref, f2_ref, i_ref, l_ref, q_ref, k_ref, v_ref, o_ref, g1_ref, g2_ref, ig_ref, lo_ref):
    cols = q_ref.shape[1]
    for i, ref in enumerate((q_ref, k_ref, v_ref)):
        ref[...] = a_ref[:, i * cols : (i + 1) * cols].astype(F32)
    o_ref[...] = jnp.transpose(a_ref[:, 3 * cols :].astype(F32))
    g1_ref[...] = f1_ref[...].astype(F32)
    g2_ref[...] = f2_ref[...].astype(F32)
    ig_ref[...] = i_ref[...]
    lo_ref[...] = l_ref[...]


def widen(attn, f1, f2, ig, lo):
    width = attn.shape[0]
    cols, steps = attn.shape[1] // 4, width // 128
    shape = jax.ShapeDtypeStruct

    def block(array):
        return pl.BlockSpec((array.shape[0] // steps, array.shape[1]), lambda i: (i, 0))

    thin = shape((width, cols), F32)
    outs = (
        thin, thin, thin, shape((cols, width), F32), shape(f1.shape, F32), shape(f2.shape, F32),
        shape(ig.shape, ig.dtype), shape(lo.shape, lo.dtype),
    )
    return pl.pallas_call(
        widen_kernel,
        grid=(steps,),
        out_shape=outs,
        in_specs=[block(attn), block(f1), block(f2), block(ig), block(lo)],
        out_specs=[block(thin)] * 3
        + [pl.BlockSpec((cols, 128), lambda i: (0, i)), block(f1), block(f2), block(ig), block(lo)],
        compiler_params=pltpu.CompilerParams(vmem_limit_bytes=WIDEN_BYTES),
        name="widen",
    )(attn, f1, f2, ig, lo)


def swapped(value):
    return lax.ppermute(value, "tensor", [(0, 1), (1, 0)])


def on_device(
    inputs, clip_ids, attn_gain, attn_shift, w_query, query_bias, w_key, w_value, value_bias,
    w_out, out_bias, mlp_gain, mlp_shift, w_fc1, fc1_bias, w_fc2, fc2_bias, cotangent,
):
    height = inputs.shape[0]
    d = lax.axis_index("dp")
    reach = REACH * height
    cols = w_query.shape[1]

    padded = jnp.pad(clip_ids, (reach, 0), constant_values=-1)
    padded = jnp.pad(padded, (0, reach), constant_values=1 << 20)
    window = lax.dynamic_slice_in_dim(padded, d * height, height + 2 * reach)
    own = window[reach : reach + height]
    firsts, lasts = own[::TILE], own[TILE - 1 :: TILE]
    begin = jnp.sum((window[None, :] < firsts[:, None]).astype(jnp.int32), axis=1)
    end = jnp.sum((window[None, :] <= lasts[:, None]).astype(jnp.int32), axis=1)
    bounds = jnp.stack([begin // TILE, (end + TILE - 1) // TILE])
    labels = window.astype(F32).reshape(-1, 128)
    split = jnp.pad(query_bias, (0, cols)) + jnp.pad(value_bias, (cols, 0))
    width = inputs.shape[1]
    rows = [attn_gain, attn_shift, split, out_bias, mlp_gain, mlp_shift, fc1_bias[:width], fc1_bias[width:], fc2_bias]
    line = lax.broadcasted_iota(jnp.int32, (16, width), 0)
    vec = jnp.zeros((16, width), BF)
    for i, values in enumerate(rows):
        vec = jnp.where(line == i, values[None, :], vec)

    q, k, v, attn_input, w_out_full, norms, key_code = halo_qkv(
        inputs, w_out, w_query, w_key, w_value, vec, labels
    )
    most = height // TILE - 1
    mixed_a, logs_a = attend(bounds, q, k, v, key_code, norms, height, 0, most)
    other_a = swapped(mixed_a)
    mixed_a, bounds = lax.optimization_barrier((mixed_a, bounds))
    mixed_b, logs_b = attend(bounds, q, k, v, key_code, norms, height, most, 1)
    grad_win, query_code, residual_grad, low, vectors, own1, own2, residual, out_part, mixed = mid(
        inputs, cotangent, mixed_a, mixed_b, other_a, logs_a, logs_b, key_code, w_out_full, vec, w_fc1, w_fc2
    )
    grad_win = grad_win.reshape(-1, grad_win.shape[2])
    out_part, query_code = lax.optimization_barrier((out_part, query_code))
    out_other = swapped(out_part)
    query_low = query_back(bounds, q, k, v, grad_win, key_code, query_code, height)
    key_low, value_low = key_back(bounds, q, k, v, grad_win, key_code, query_code, height)
    out_other, key_low = lax.optimization_barrier((out_other, key_low))
    inputs_grad, attn_sum, sums, fc1_sum, fc2_sum, layer_out = finish(
        query_low, key_low, value_low, w_query, w_key, w_value, attn_input, low, mixed, inputs,
        residual_grad, vec, vectors, own1, own2, residual, out_part, out_other, (w_fc1.shape, w_fc2.shape),
    )
    q_grad, k_grad, v_grad, o_grad, fc1_grad, fc2_grad, inputs_grad, layer_out = widen(
        attn_sum, fc1_sum, fc2_sum, inputs_grad, layer_out
    )
    sums, q_grad = lax.optimization_barrier((sums, q_grad))
    return (
        layer_out, inputs_grad, sums[7], sums[8],
        q_grad, sums[6, :cols], k_grad, v_grad, sums[6, cols:],
        o_grad, sums[2], sums[0], sums[1],
        fc1_grad, sums[4:6].reshape(-1), fc2_grad, sums[3],
    )


def solution(mesh):
    rows, cols, split, every = P("dp", None), P(None, "tensor"), P("tensor"), P()
    tall = P("tensor", None)
    in_specs = (
        rows, every, every, every, cols, split, cols, cols, split, tall, every, every, every,
        cols, split, tall, every, rows,
    )
    out_specs = (
        rows, rows, every, every, cols, split, cols, cols, split, tall, every, every, every,
        cols, split, tall, every,
    )
    return jax.shard_map(on_device, mesh=mesh, in_specs=in_specs, out_specs=out_specs, check_vma=False)
```
